32 devices in a mesh: dp: 8 (over z, x), tensor: 4 (over y, core).
Axes of the slice: x: 2, y: 2, z: 4, core: 2. Of those that a mesh axis runs over, the one named last changes fastest.
Arguments:
- tokens: bfloat16 [4096, 1024], P('dp'), may hold values from -6 to 6
- cotangent: bfloat16 [4096, 1024], P('dp'), may hold values from -6 to 6
- w_qkv: float32 [2, 3, 1024, 1024], P(None, None, 'dp', 'tensor'), may hold values from -0.1875 to 0.1875
- w_out: float32 [2, 1024, 1024], P(None, 'dp', 'tensor'), may hold values from -2.5 to 2.5
- router: float32 [2, 1024, 8], P(None, 'dp'), may hold values from -0.125 to 0.125
- gains: float32 [2, 2, 1024], P(None, None, 'dp'), may hold values from 0.5 to 1.5
- rel_table: float32 [2, 32, 16], P(None, 'dp', 'tensor'), may hold values from -4 to 4
- w_gate: float32 [2, 8, 1024, 2816], P(None, 'dp', None, 'tensor'), may hold values from -0.1875 to 0.1875
- w_up: float32 [2, 8, 1024, 2816], P(None, 'dp', None, 'tensor'), may hold values from -0.1875 to 0.1875
- w_down: float32 [2, 8, 2816, 1024], P(None, 'dp', 'tensor'), may hold values from -0.109375 to 0.109375
- routes: int32 [2, 4096, 2], P(None, 'dp'), may hold values from 0 to 7, as said below
- slots: int32 [2, 4096, 2], P(None, 'dp'), may hold values from 0 to 191, as said below
- segments: int32 [4096], P('dp'), may hold values from 0 to 2, as said below
Outputs:
- output: bfloat16 [4096, 1024], P('dp')
- tokens_grad: float32 [4096, 1024], P('dp')
- w_qkv_grad: float32 [2, 3, 1024, 1024], P(None, None, 'dp', 'tensor')
- w_out_grad: float32 [2, 1024, 1024], P(None, 'dp', 'tensor')
- router_grad: float32 [2, 1024, 8], P(None, 'dp')
- gains_grad: float32 [2, 2, 1024], P(None, None, 'dp')
- rel_table_grad: float32 [2, 32, 16], P(None, 'dp', 'tensor')
- w_gate_grad: float32 [2, 8, 1024, 2816], P(None, 'dp', None, 'tensor')
- w_up_grad: float32 [2, 8, 1024, 2816], P(None, 'dp', None, 'tensor')
- w_down_grad: float32 [2, 8, 2816, 1024], P(None, 'dp', 'tensor')
The draws below stay inside these ranges and needn't reach their ends.
Inputs may be any that keep to these rules, and one draw needn't show every extreme that they name: `routes`: the two experts of a row differ. In each layer the rows of one sequence name each expert at most 192 times, and one expert, the same for every sequence and layer, exactly 192 times. `slots`: in each layer, the rows of one sequence that name one expert hold its slot numbers 0, 1, ... up to their count less one, each once. `segments`: each sequence is cut into aligned blocks of 256 tokens; a block is text (0 throughout) or a picture piece whose id is its block number within the sequence plus one.
All inputs are finite; a program needn't handle non-finite values.
Results may differ from the reference program's by a relative error of at most 0.035.
Values may be sent and summed in bfloat16 or wider, within the bound.
A program may use at most 256 MiB of HBM per device.

```python
import jax
import jax.numpy as jnp
from jax import lax

D = 1024
HEADS = 16
HDIM = 64
FF = 2816
SEQ = 512
LAYERS = 2
PIECE = 256
BUCKETS = 32
EXPERTS = 8
CAP = 192
BLOCK = 512
TOKENS = 4096
N_DP = 8


def route_tables(key):
    base_key = jax.random.fold_in(key, 101)
    favored = jax.random.randint(jax.random.fold_in(base_key, 1), (), 0, EXPERTS)
    weights = 2 * EXPERTS - jnp.arange(1, EXPERTS, dtype=jnp.int32)
    weight_sum = 3 * EXPERTS * (EXPERTS - 1) // 2
    remaining = 2 * SEQ - CAP
    pair_count = (EXPERTS - 1) // 2
    first_index = 2 * jnp.arange(pair_count, dtype=jnp.int32)

    def one_block(block_key):
        keys_all = jax.random.split(block_key, 3)
        load_rows = remaining * weights // weight_sum
        load_rows = load_rows + (jnp.arange(EXPERTS - 1, dtype=jnp.int32) < remaining - jnp.sum(load_rows)).astype(jnp.int32)
        move_limit = jnp.minimum(load_rows[first_index + 1] // 2, CAP - load_rows[first_index])
        moved_rows = jax.random.randint(keys_all[0], (pair_count,), 0, move_limit + 1).astype(jnp.int32)
        load_rows = load_rows.at[first_index].add(moved_rows).at[first_index + 1].add(-moved_rows)
        counts = jnp.concatenate([jnp.full((1,), CAP, jnp.int32), load_rows])
        shuffled = jax.random.permutation(keys_all[1], EXPERTS).astype(jnp.int32)
        ranking = jnp.where(shuffled == favored, -1, jnp.arange(EXPERTS, dtype=jnp.int32))
        expert_order = shuffled[jnp.argsort(ranking)]
        run_ends = jnp.cumsum(counts)
        assign = jnp.arange(2 * SEQ, dtype=jnp.int32)
        run_index = jnp.sum((assign[:, None] >= run_ends[None, :]).astype(jnp.int32), axis=1)
        expert_of = expert_order[run_index]
        slot_of = assign - (run_ends - counts)[run_index]
        token_order = jax.random.permutation(keys_all[2], SEQ).astype(jnp.int32)
        route_pairs = jnp.stack([expert_of[:SEQ], expert_of[SEQ:]], axis=-1)
        slot_pairs = jnp.stack([slot_of[:SEQ], slot_of[SEQ:]], axis=-1)
        route_block = jnp.zeros((SEQ, 2), jnp.int32).at[token_order].set(route_pairs)
        slot_block = jnp.zeros((SEQ, 2), jnp.int32).at[token_order].set(slot_pairs)
        return (route_block, slot_block)
    block_keys = jax.random.split(jax.random.fold_in(base_key, 2), LAYERS * (TOKENS // SEQ))
    route_all, slot_all = jax.vmap(one_block)(block_keys)
    return (route_all.reshape(LAYERS, TOKENS, 2).astype(jnp.int32), slot_all.reshape(LAYERS, TOKENS, 2).astype(jnp.int32))


def draw_routes(key, part):
    return route_tables(key)[0]


def draw_slots(key, part):
    return route_tables(key)[1]


def draw_segments(key, part):
    piece_count = SEQ // PIECE
    chosen = jax.random.randint(jax.random.fold_in(key, 202), (TOKENS // SEQ, piece_count), 0, 2).astype(jnp.int32)
    chosen = chosen.at[0, piece_count - 1].set(1)
    labels = chosen * (jnp.arange(piece_count, dtype=jnp.int32) + 1)[None, :]
    return jnp.repeat(labels, PIECE, axis=1).reshape(TOKENS).astype(jnp.int32)


def block_levels(key, shape, cuts, least, high):
    level = 1.0
    for dim, blocks in cuts:
        draws = jax.random.uniform(jax.random.fold_in(jax.random.fold_in(key, 6), dim), (blocks,), jnp.float32, least / len(cuts), high / len(cuts))
        level = level * jnp.repeat(jnp.exp(draws), shape[dim] // blocks).reshape((-1,) + (1,) * (len(shape) - 1 - dim))
    return level


def gaussian(stream_key, shape, spread, bound, cuts=(), kind=jnp.bfloat16):
    factor_of = block_levels(stream_key, shape, cuts, -0.22, 0.18) if cuts else 1.0
    drawn = jax.random.normal(stream_key, shape, jnp.float32) * spread * factor_of
    return jnp.minimum(jnp.maximum(drawn, -bound), bound).astype(kind)


def setup_inputs(seed: int = 0) -> dict:
    keys = jax.random.split(jax.random.key(seed), 14)
    return {
        "tokens": gaussian(keys[0], (TOKENS, D), 1.0, 6.0, ((0, 8),)),
        "cotangent": gaussian(keys[1], (TOKENS, D), 1.0, 6.0, ((0, 8),)),
        "w_qkv": gaussian(keys[2], (LAYERS, 3, D, D), D ** -0.5, 0.1875, ((2, 8), (3, 4)), jnp.float32),
        "w_out": gaussian(keys[3], (LAYERS, D, D), (D // 256 + 1) ** -0.5, 2.5, ((1, 8), (2, 4)), jnp.float32),
        "router": gaussian(keys[4], (LAYERS, D, EXPERTS), (2 * D) ** -0.5, 0.125, ((1, 8),), jnp.float32),
        "gains": jnp.clip(1.0 + 0.1 * jax.random.normal(keys[5], (LAYERS, 2, D), jnp.float32), 0.5, 1.5),
        "rel_table": gaussian(keys[6], (LAYERS, BUCKETS, HEADS), 1.0, 4.0, ((1, 8), (2, 4)), jnp.float32),
        "w_gate": gaussian(keys[7], (LAYERS, EXPERTS, D, FF), D ** -0.5, 0.1875, ((1, 8), (3, 4)), jnp.float32),
        "w_up": gaussian(keys[8], (LAYERS, EXPERTS, D, FF), D ** -0.5, 0.1875, ((1, 8), (3, 4)), jnp.float32),
        "w_down": gaussian(keys[9], (LAYERS, EXPERTS, FF, D), FF ** -0.5, 0.109375, ((1, 8), (2, 4)), jnp.float32),
        "routes": draw_routes(jax.random.fold_in(keys[13], 71), 0),
        "slots": draw_slots(jax.random.fold_in(keys[13], 71), 0),
        "segments": draw_segments(jax.random.fold_in(keys[13], 71), 0),
    }


@jax.custom_vjp
def low(v):
    return lax.optimization_barrier(v.astype(jnp.bfloat16)).astype(jnp.float32)

@jax.custom_vjp
def low_back(v):
    return v

def low_keep(v):
    return (low(v), None)

def low_pass(kept, grad):
    return (grad,)

def back_keep(v):
    return (v, None)

def back_low(kept, grad):
    return (low(grad),)
low.defvjp(low_keep, low_pass)
low_back.defvjp(back_keep, back_low)
eps_norm = 1e-06
rise_points = (12, 16, 23, 32, 46, 64, 91)
masked_score = -1e+30
highest = lax.Precision.HIGHEST

def bucket_index(offset):
    upward = (offset > 0).astype(jnp.int32) * (BUCKETS // 2)
    distance = jnp.abs(offset)
    far_part = 8 + sum(((distance >= rise_point).astype(jnp.int32) for rise_point in rise_points))
    return upward + jnp.where(distance < 8, distance, far_part)

def inverse_rms(row_values):
    return lax.rsqrt(lax.optimization_barrier(jnp.mean(row_values * row_values, axis=-1, keepdims=True)) + eps_norm)

def attend_sequence(query_rows, key_rows, value_rows, segment, relvec):
    score_scale = HDIM ** (-0.5)
    position = jnp.arange(SEQ, dtype=jnp.int32)

    def one_block(block_start):
        rows_q = lax.dynamic_slice_in_dim(query_rows, block_start, BLOCK, 0)
        row_pos = block_start + jnp.arange(BLOCK, dtype=jnp.int32)
        row_seg = lax.dynamic_slice_in_dim(segment, block_start, BLOCK, 0)
        allowed = (position[None, :] <= row_pos[:, None]) | (row_seg[:, None] == segment[None, :]) & (row_seg[:, None] > 0)
        bias_index = position[None, :] - row_pos[:, None] + (SEQ - 1)
        scores = jnp.einsum('qhd,khd->hqk', rows_q, key_rows, precision=highest) * score_scale
        scores = low_back(scores + jnp.take(relvec, bias_index, axis=1))
        scores = jnp.where(allowed[None], scores, masked_score)
        prob_rows = low_back(low(jax.nn.softmax(scores, axis=-1)))
        return jnp.einsum('hqk,khd->qhd', prob_rows, value_rows, precision=highest)
    starts = jnp.arange(SEQ // BLOCK, dtype=jnp.int32) * BLOCK
    return lax.map(jax.checkpoint(one_block), starts).reshape(SEQ, HEADS, HDIM)

def layer_forward(hidden, qkv_w, out_w, router_w, gain_w, table_w, gate_w, up_w, down_w, route_rows, slot_rows, segments):
    gain_low = low(gain_w)
    normed_one = low(hidden * inverse_rms(hidden) * gain_low[0])
    projected = low_back(low(jnp.einsum('td,cde->cte', normed_one, low(qkv_w), precision=highest)))
    projected = projected.reshape(3, N_DP, SEQ, HEADS, HDIM)
    offsets = jnp.arange(2 * SEQ - 1, dtype=jnp.int32) - (SEQ - 1)
    one_hot = (bucket_index(offsets)[:, None] == jnp.arange(BUCKETS, dtype=jnp.int32)[None, :]).astype(jnp.float32)
    relvec = jnp.dot(one_hot, low(table_w), precision=highest).T
    context = lax.map(lambda pieces: attend_sequence(pieces[0], pieces[1], pieces[2], pieces[3], relvec), (projected[0], projected[1], projected[2], segments.reshape(N_DP, SEQ)))
    context = low_back(low(context.reshape(TOKENS, D)))
    attn_out = low_back(jnp.einsum('te,de->td', context, low(out_w), precision=highest))
    middle = hidden + attn_out
    normed_two = low(middle * inverse_rms(middle) * gain_low[1])
    logits = low_back(jnp.dot(normed_two, low(router_w), precision=highest))
    route_hot = (route_rows[:, :, None] == jnp.arange(EXPERTS, dtype=jnp.int32)[None, None, :]).astype(jnp.float32)
    gate_share = jax.nn.softmax(jnp.einsum('tke,te->tk', route_hot, logits, precision=highest), axis=-1)
    source = jnp.arange(TOKENS, dtype=jnp.int32) // SEQ
    target = ((route_rows * N_DP + source[:, None]) * CAP + slot_rows).astype(jnp.int32)
    buffer_rows = jnp.zeros((EXPERTS * N_DP * CAP, D), jnp.float32).at[target.reshape(-1)].add(jnp.repeat(normed_two, 2, axis=0))
    buffer_rows = low_back(buffer_rows).reshape(EXPERTS, N_DP * CAP, D)

    def one_expert(pieces):
        expert_rows, gate_one, up_one, down_one = pieces
        gate_pre = low_back(jnp.dot(expert_rows, low(gate_one), precision=highest))
        up_pre = low_back(jnp.dot(expert_rows, low(up_one), precision=highest))
        inner_rows = low(jax.nn.gelu(gate_pre, approximate=True) * up_pre)
        return jnp.dot(inner_rows, low(down_one), precision=highest)
    produced = lax.map(jax.checkpoint(one_expert), (buffer_rows, gate_w, up_w, down_w))
    produced = low_back(low(produced)).reshape(EXPERTS * N_DP * CAP, D)
    picked = produced[target]
    return middle + jnp.einsum('tk,tkd->td', gate_share, picked, precision=highest)

def reference(tokens, cotangent, w_qkv, w_out, router, gains, rel_table, w_gate, w_up, w_down, routes, slots, segments):

    def forward(hidden, qkv_all, out_all, router_all, gain_all, table_all, gate_all, up_all, down_all):
        for layer_index in range(LAYERS):
            hidden = layer_forward(hidden, qkv_all[layer_index], out_all[layer_index], router_all[layer_index], gain_all[layer_index], table_all[layer_index], gate_all[layer_index], up_all[layer_index], down_all[layer_index], routes[layer_index], slots[layer_index], segments)
        return hidden
    output, pullback = jax.vjp(forward, tokens.astype(jnp.float32), w_qkv, w_out, router, gains, rel_table, w_gate, w_up, w_down)
    all_grads = pullback(cotangent.astype(jnp.float32))
    return (output.astype(jnp.bfloat16), all_grads[0], all_grads[1], all_grads[2], all_grads[3], all_grads[4], all_grads[5], all_grads[6], all_grads[7], all_grads[8])
```

```python
import functools

import jax
import jax.numpy as jnp
from jax import lax
from jax.experimental import pallas as pl
from jax.experimental.pallas import tpu as pltpu
from jax.sharding import PartitionSpec as P

D = 1024
HDIM = 64
SEQ = 512
LAYERS = 2
BUCKETS = 32
HALF = 256
SLICES = 4
CHUNKS = 8
LANES = 128
WINDOW = 768

eps_norm = 1e-06
rise_points = (12, 16, 23, 32, 46, 64, 91)
masked_score = -1e30
vmem_bytes = 60 * 1024 * 1024
f32 = jnp.float32
bf16 = jnp.bfloat16
MESH = pl.DeviceIdType.MESH
nn_dims = (((1,), (0,)), ((), ()))
nt_dims = (((1,), (1,)), ((), ()))
tn_dims = (((0,), (0,)), ((), ()))
vmem_spec = pl.BlockSpec(memory_space=pltpu.VMEM)
any_spec = pl.BlockSpec(memory_space=pl.ANY)


def nn(a, b):
    return lax.dot_general(a, b, nn_dims, preferred_element_type=f32)


def nt(a, b):
    return lax.dot_general(a, b, nt_dims, preferred_element_type=f32)


def tn(a, b):
    return lax.dot_general(a, b, tn_dims, preferred_element_type=f32)


def shaped(shape, kind):
    return jax.ShapeDtypeStruct(shape, kind)


def bucket_index(offset):
    upward = jnp.where(offset > 0, BUCKETS // 2, 0)
    distance = jnp.abs(offset)
    far_part = 8 + sum(((distance >= rise_point).astype(jnp.int32) for rise_point in rise_points))
    return upward + jnp.where(distance < 8, distance, far_part)


def toeplitz_bias(row):
    tile = jnp.broadcast_to(row, (HALF, WINDOW))
    rolled = pltpu.roll(tile, WINDOW - HALF + 1, 1, stride=1, stride_axis=0)
    return rolled[:, : 2 * HALF]


def diagonal_sums(grad):
    rows = jnp.concatenate([grad, jnp.zeros((HALF, WINDOW - 2 * HALF), f32)], axis=1)
    count = HALF
    while count > 8:
        count //= 2
        rows = rows[:count] + pltpu.roll(rows[count:], WINDOW - count, 1)
    total = jnp.zeros((8, WINDOW), f32)
    place = lax.broadcasted_iota(jnp.int32, (8, WINDOW), 0)
    for i in range(8):
        moved = pltpu.roll(rows, (HALF - 1 - i) % WINDOW, 1)
        total = total + jnp.where(place == i, moved, 0.0)
    return total


def half_lanes(shape, which):
    lane = lax.broadcasted_iota(jnp.int32, shape, 1)
    return (lane < HDIM) if which == 0 else (lane >= HDIM)


def bias_row(table, head):
    place = lax.broadcasted_iota(jnp.int32, (BUCKETS, WINDOW), 1) - (SEQ - 1)
    hot = (bucket_index(place) == lax.broadcasted_iota(jnp.int32, (BUCKETS, WINDOW), 0)).astype(bf16)
    return nn(table.astype(bf16), hot)[head : head + 1]


def allowed_tile(seg_col, seg_row):
    i = lax.broadcasted_iota(jnp.int32, (HALF, HALF), 0)
    j = lax.broadcasted_iota(jnp.int32, (HALF, HALF), 1)
    return (j <= i) | ((seg_col == seg_row) & (seg_col > 0))


def masked_scores(query, keys, bias, allowed, block):
    raw = nt(query, keys)
    if block == 0:
        return jnp.where(allowed, raw + bias[:, HALF:], masked_score)
    left = raw[:, :HALF] + bias[:, :HALF]
    right = jnp.where(allowed, raw[:, HALF:] + bias[:, HALF:], masked_score)
    return jnp.concatenate([left, right], axis=1)


def attend_forward(proj, ctx_ref, lse_ref, table, seg_col, seg_row):
    pairs = proj.shape[1] // (3 * LANES)
    width = pairs * LANES
    bias_all = bias_rows(table)
    lane = lax.broadcasted_iota(jnp.int32, (HALF, LANES), 1)
    for block in range(2):
        rows = slice(block * HALF, (block + 1) * HALF)
        count = (block + 1) * HALF
        allowed = allowed_tile(seg_col[rows], seg_row[:, rows])
        lse = jnp.zeros((HALF, LANES), f32)
        for pair in range(pairs):
            cols = slice(pair * LANES, (pair + 1) * LANES)
            q2 = proj[rows, cols]
            k2 = proj[:count, width + pair * LANES : width + (pair + 1) * LANES]
            v2 = proj[:count, 2 * width + pair * LANES : 2 * width + (pair + 1) * LANES]
            outs = []
            for which in range(2):
                head = 2 * pair + which
                qm = jnp.where(half_lanes(q2.shape, which), q2 * jnp.asarray(HDIM**-0.5, bf16), jnp.zeros_like(q2))
                scores = masked_scores(qm, k2, toeplitz_bias(bias_all[head : head + 1]), allowed, block)
                top = jnp.max(scores, axis=1, keepdims=True)
                powers = jnp.exp(scores - top)
                total = jnp.sum(powers, axis=1, keepdims=True)
                probs = (powers * (1.0 / total)).astype(bf16)
                outs.append(nn(probs, v2))
                lse = jnp.where(lane == head, top + jnp.log(total), lse)
            ctx_ref[rows, cols] = jnp.where(half_lanes(outs[0].shape, 0), outs[0], outs[1]).astype(bf16)
        lse_ref[rows, :] = lse


def bias_rows(table):
    place = lax.broadcasted_iota(jnp.int32, (BUCKETS, WINDOW), 1) - (SEQ - 1)
    hot = (bucket_index(place) == lax.broadcasted_iota(jnp.int32, (BUCKETS, WINDOW), 0)).astype(bf16)
    return nn(table, hot)


def attend_backward(proj, dctx, lse_ref, table, seg_col, seg_row, dk_acc, dv_acc, pg_ref, tg_ref):
    pairs = proj.shape[1] // (3 * LANES)
    width = pairs * LANES
    bias_all = bias_rows(table)
    scale = jnp.asarray(HDIM**-0.5, bf16)
    place = lax.broadcasted_iota(jnp.int32, (8, WINDOW), 0)
    diag_all = jnp.zeros((8, WINDOW), f32)
    for pair in range(pairs):
        cols = slice(pair * LANES, (pair + 1) * LANES)
        bias_grads = [None, None]
        for block in (1, 0):
            rows = slice(block * HALF, (block + 1) * HALF)
            count = (block + 1) * HALF
            allowed = allowed_tile(seg_col[rows], seg_row[:, rows])
            q2 = proj[rows, cols]
            k2 = proj[:count, width + pair * LANES : width + (pair + 1) * LANES]
            v2 = proj[:count, 2 * width + pair * LANES : 2 * width + (pair + 1) * LANES]
            g2 = dctx[rows, cols]
            outs = []
            dk = None
            dv = None
            for which in range(2):
                head = 2 * pair + which
                mine = half_lanes(q2.shape, which)
                qm = jnp.where(mine, q2 * scale, jnp.zeros_like(q2))
                gm = jnp.where(mine, g2, jnp.zeros_like(g2))
                scores = masked_scores(qm, k2, toeplitz_bias(bias_all[head : head + 1]), allowed, block)
                probs = jnp.exp(scores - lse_ref[rows, head : head + 1])
                prob_grad = nt(gm, v2).astype(bf16).astype(f32)
                inner = jnp.sum(probs * prob_grad, axis=1, keepdims=True)
                grad = probs * (prob_grad - inner)
                grad_low = grad.astype(bf16)
                dv_one = tn(probs.astype(bf16), gm)
                dk_one = tn(grad_low, qm)
                dv = dv_one if dv is None else dv + dv_one
                dk = dk_one if dk is None else dk + dk_one
                outs.append(nn(grad_low, k2))
                wide = grad_low.astype(f32)
                if block == 1:
                    bias_grads[which] = wide
                else:
                    bias_grads[which] = jnp.concatenate(
                        [bias_grads[which][:, :HALF], bias_grads[which][:, HALF:] + wide], axis=1
                    )
            dq = jnp.where(half_lanes(outs[0].shape, 0), outs[0], outs[1]) * HDIM**-0.5
            pg_ref[rows, cols] = dq.astype(bf16)
            if block == 1:
                dk_acc[...] = dk
                dv_acc[...] = dv
            else:
                dk_acc[:HALF] = dk_acc[:HALF] + dk
                dv_acc[:HALF] = dv_acc[:HALF] + dv
        pg_ref[:, width + pair * LANES : width + (pair + 1) * LANES] = dk_acc[...].astype(bf16)
        pg_ref[:, 2 * width + pair * LANES : 2 * width + (pair + 1) * LANES] = dv_acc[...].astype(bf16)
        for which in range(2):
            sums = jnp.sum(diagonal_sums(bias_grads[which]), axis=0, keepdims=True)
            diag_all = jnp.where(place == 2 * pair + which, sums, diag_all)
    spot = lax.broadcasted_iota(jnp.int32, (WINDOW, LANES), 0) - (SEQ - 1)
    hot = (bucket_index(spot) == lax.broadcasted_iota(jnp.int32, (WINDOW, LANES), 1)).astype(f32)
    tg_ref[...] = lax.dot_general(
        diag_all, hot, nn_dims, precision=lax.Precision.HIGHEST, preferred_element_type=f32
    )


def project(x, r_col, wqkv, proj_ref):
    for c in range(3):
        width = wqkv.shape[2]
        proj_ref[:, c * width : (c + 1) * width] = (nn(x, wqkv[c]) * r_col).astype(bf16)


def project_out(ctx_ref, wo, part_ref):
    for q in range(SLICES):
        part_ref[q] = nt(ctx_ref[...], wo[q * HALF : (q + 1) * HALF, :]).astype(bf16)


def first_attention_kernel(tok, gain, wqkv, wo, table, seg_col, seg_row, hg, r1, proj, lse, ctx, part):
    x = tok[...].astype(f32)
    r = lax.rsqrt(jnp.sum(x * x, axis=1, keepdims=True) * (1.0 / D) + eps_norm)
    hg[...] = (x * gain[...]).astype(bf16)
    r1[...] = jnp.broadcast_to(r, (SEQ, LANES))
    project(hg[...], r, wqkv, proj)
    attend_forward(proj, ctx, lse, table[...], seg_col[...], seg_row[...])
    project_out(ctx, wo, part)


def next_attention_kernel(hg, r1, wqkv, wo, table, seg_col, seg_row, proj, lse, ctx, part):
    project(hg[...], r1[:, :1], wqkv, proj)
    attend_forward(proj, ctx, lse, table[...], seg_col[...], seg_row[...])
    project_out(ctx, wo, part)


def attention_forward(first, x, extra, wqkv, wo, table, seg_col, seg_row):
    width = wqkv.shape[2]
    outs = [
        shaped((SEQ, 3 * width), bf16),
        shaped((SEQ, LANES), f32),
        shaped((SEQ, width), bf16),
        shaped((SLICES, SEQ, HALF), bf16),
    ]
    if first:
        outs = [shaped((SEQ, D), bf16), shaped((SEQ, LANES), f32)] + outs
    return pl.pallas_call(
        first_attention_kernel if first else next_attention_kernel,
        out_shape=outs,
        in_specs=[vmem_spec] * 7,
        out_specs=[vmem_spec] * len(outs),
        compiler_params=pltpu.CompilerParams(vmem_limit_bytes=vmem_bytes),
    )(x, extra, wqkv, wo, table, seg_col, seg_row)


def attention_backward_kernel(
    agf, wo, ctx, proj, lse, table, seg_col, seg_row, hg, r1, wqkv, wog, qkvg, ng, tg, pg, dk_acc, dv_acc
):
    dctx = nn(agf[...], wo[...]).astype(bf16)
    wog[...] = tn(agf[...], ctx[...]).astype(bf16)
    attend_backward(
        proj, dctx, lse, table[...], seg_col[...], seg_row[...], dk_acc, dv_acc, pg, tg
    )
    width = wqkv.shape[2]
    for q in range(SLICES):
        total = None
        for c in range(3):
            one = nt(pg[:, c * width : (c + 1) * width], wqkv[c, q * HALF : (q + 1) * HALF, :])
            total = one if total is None else total + one
        ng[q] = total.astype(bf16)
    normed = (hg[...].astype(f32) * r1[:, :1]).astype(bf16)
    for c in range(3):
        qkvg[c] = tn(normed, pg[:, c * width : (c + 1) * width]).astype(bf16)


def attention_backward(agf, wo, ctx, proj, lse, table, seg_col, seg_row, hg, r1, wqkv):
    width = wqkv.shape[2]
    return pl.pallas_call(
        attention_backward_kernel,
        out_shape=[
            shaped((D, width), bf16),
            shaped((3, D, width), bf16),
            shaped((SLICES, SEQ, HALF), bf16),
            shaped((8, LANES), f32),
        ],
        in_specs=[vmem_spec] * 11,
        out_specs=[vmem_spec] * 4,
        scratch_shapes=[
            pltpu.VMEM((SEQ, 3 * width), bf16),
            pltpu.VMEM((SEQ, LANES), f32),
            pltpu.VMEM((SEQ, LANES), f32),
        ],
        compiler_params=pltpu.CompilerParams(vmem_limit_bytes=vmem_bytes),
    )(agf, wo, ctx, proj, lse, table, seg_col, seg_row, hg, r1, wqkv)


def places():
    d = lax.axis_index("dp")
    t = lax.axis_index("tensor")
    sib = t + 1 - 2 * lax.rem(t, 2)
    far = lax.rem(t + 2, SLICES)
    opp = SLICES - 1 - t
    return d, t, sib, far, opp


def remote(src, dst, send, recv, device):
    return pltpu.make_async_remote_copy(
        src_ref=src, dst_ref=dst, send_sem=send, recv_sem=recv, device_id=device, device_id_type=MESH
    )


def greet(n, with_dp):
    d, t, sib, far, opp = places()
    barrier = pltpu.get_barrier_semaphore()
    for peer in (sib, far, opp):
        pl.semaphore_signal(barrier, inc=1, device_id=(d, peer), device_id_type=MESH)
    if with_dp:

        def hello(j, carry):
            pl.semaphore_signal(barrier, inc=1, device_id=(lax.rem(d + j, n), t), device_id_type=MESH)
            return carry

        lax.fori_loop(1, n, hello, 0)
    pl.semaphore_wait(barrier, 3 + (n - 1 if with_dp else 0))


class Tiny:
    scratch = lambda rows, cols: [
        pltpu.VMEM((SLICES, rows, cols), f32),
        pltpu.SemaphoreType.DMA((3,)),
        pltpu.SemaphoreType.DMA((3,)),
    ]

    def __init__(self, refs):
        self.buf, self.send, self.recv = refs

    def copies(self):
        d, t, sib, far, opp = places()
        return [
            remote(self.buf.at[t], self.buf.at[t], self.send.at[i], self.recv.at[i], (d, peer))
            for i, peer in enumerate((sib, far, opp))
        ]

    def start(self, tile):
        d, t, sib, far, opp = places()
        self.buf[t] = tile
        for copy in self.copies():
            copy.start()

    def finish(self):
        for copy in self.copies():
            copy.wait()

    def total(self):
        self.finish()
        return (self.buf[0] + self.buf[1]) + (self.buf[2] + self.buf[3])


class Gather:
    scratch = lambda rows: [
        pltpu.VMEM((SLICES, rows, HALF), bf16),
        pltpu.SemaphoreType.DMA((3,)),
        pltpu.SemaphoreType.DMA((3,)),
    ]

    def __init__(self, refs):
        self.buf, self.send, self.recv = refs

    def copies(self):
        d, t, sib, far, opp = places()
        return [
            lambda: remote(self.buf.at[t], self.buf.at[t], self.send.at[0], self.recv.at[0], (d, far)),
            lambda: remote(self.buf.at[t], self.buf.at[t], self.send.at[1], self.recv.at[1], (d, sib)),
            lambda: remote(self.buf.at[far], self.buf.at[far], self.send.at[2], self.recv.at[2], (d, sib)),
        ]

    def start(self, tile):
        d, t, sib, far, opp = places()
        self.buf[t] = tile
        far_copy, near_copy, pass_copy = self.copies()
        far_copy().start()
        near_copy().start()

    def forward(self):
        far_copy, near_copy, pass_copy = self.copies()
        far_copy().wait_recv()
        pass_copy().start()

    def finish(self):
        far_copy, near_copy, pass_copy = self.copies()
        near_copy().wait_recv()
        pass_copy().wait_recv()
        far_copy().wait_send()
        near_copy().wait_send()
        pass_copy().wait_send()

    def store(self, out_ref, sems):
        copies = [
            pltpu.make_async_copy(self.buf.at[q], out_ref.at[:, pl.ds(q * HALF, HALF)], sems.at[q])
            for q in range(SLICES)
        ]
        for copy in copies:
            copy.start()
        return copies


class Reduce:
    scratch = lambda rows: [
        pltpu.VMEM((2, rows, HALF), bf16),
        pltpu.VMEM((2, rows, HALF), bf16),
        pltpu.SemaphoreType.DMA((3,)),
        pltpu.SemaphoreType.DMA((3,)),
    ]

    def __init__(self, part, refs):
        self.part = part
        self.near, self.across, self.send, self.recv = refs

    def copies(self):
        d, t, sib, far, opp = places()
        return [
            lambda: remote(self.part.at[opp], self.near.at[1], self.send.at[0], self.recv.at[0], (d, sib)),
            lambda: remote(self.part.at[sib], self.near.at[0], self.send.at[1], self.recv.at[1], (d, sib)),
            lambda: remote(self.across.at[0], self.across.at[1], self.send.at[2], self.recv.at[2], (d, far)),
        ]

    def start(self):
        first, second, third = self.copies()
        first().start()
        second().start()

    def total(self):
        d, t, sib, far, opp = places()
        first, second, third = self.copies()
        first().wait_recv()
        self.across[0] = (self.part[far].astype(f32) + self.near[1].astype(f32)).astype(bf16)
        third().start()
        second().wait_recv()
        mine = self.part[t].astype(f32) + self.near[0].astype(f32)
        third().wait_recv()
        first().wait_send()
        second().wait_send()
        third().wait_send()
        return mine + self.across[1].astype(f32)


def to_row(col):
    return jnp.transpose(jnp.broadcast_to(col, (col.shape[0], LANES)))[:8]


def to_cols(rows8):
    return jnp.transpose(jnp.concatenate([rows8] * (LANES // 8), axis=0))


def hot_columns(targ, k, count):
    return (targ[:, k : k + 1] == lax.broadcasted_iota(jnp.int32, (SEQ, count), 1)).astype(f32).astype(bf16)


class Route:
    scratch = lambda n, cap: [
        pltpu.VMEM((n, cap, HALF), bf16),
        pltpu.VMEM((CHUNKS, SLICES, n * cap // CHUNKS, HALF), bf16),
        pltpu.VMEM((CHUNKS, SLICES, n * cap // CHUNKS, HALF), bf16),
        pltpu.VMEM((CHUNKS, 2, n * cap // CHUNKS, HALF), bf16),
        pltpu.VMEM((CHUNKS, n * cap // CHUNKS, HALF), bf16),
        pltpu.VMEM((CHUNKS, n * cap // CHUNKS, HALF), bf16),
        pltpu.VMEM((CHUNKS, n * cap // CHUNKS, HALF), bf16),
        pltpu.VMEM((n * cap, HALF), bf16),
        pltpu.SemaphoreType.DMA((n,)),
        pltpu.SemaphoreType.DMA((n,)),
        pltpu.SemaphoreType.DMA((3, CHUNKS)),
        pltpu.SemaphoreType.DMA((3, CHUNKS)),
        pltpu.SemaphoreType.DMA((3, CHUNKS)),
        pltpu.SemaphoreType.DMA((3, CHUNKS)),
        pltpu.SemaphoreType.DMA((n,)),
        pltpu.SemaphoreType.DMA((n,)),
    ]

    def __init__(self, n, cap, refs):
        self.n, self.cap = n, cap
        self.group = n // CHUNKS
        self.rows = self.group * cap
        (
            self.out,
            self.x,
            self.p,
            self.ra,
            self.sb,
            self.rb,
            self.ro,
            self.ret,
            self.as_,
            self.ar,
            self.fs,
            self.fr,
            self.ps,
            self.pr,
            self.rs,
            self.rr,
        ) = refs

    def slot(self, source):
        start = pl.multiple_of(lax.rem(source, self.group) * self.cap, 16)
        return source // self.group, pl.ds(start, self.cap)

    def out_copy(self, j, source, target):
        d, t, sib, far, opp = places()
        chunk, rows = self.slot(source)
        return remote(
            self.out.at[j], self.x.at[chunk, t, rows], self.as_.at[j], self.ar.at[source], (target, t)
        )

    def dispatch(self, make_block):
        d, t, sib, far, opp = places()
        chunk, rows = self.slot(d)
        self.x[chunk, t, rows] = make_block(d)

        def one(j, carry):
            e = lax.rem(d + j, self.n)
            self.out[j] = make_block(e)
            self.out_copy(j, d, e).start()
            return carry

        lax.fori_loop(1, self.n, one, 0)

    def spread_copies(self, chunk):
        d, t, sib, far, opp = places()
        mine, others = self.x.at[chunk, t], self.x.at[chunk, far]
        return [
            lambda: remote(mine, mine, self.fs.at[0, chunk], self.fr.at[0, chunk], (d, far)),
            lambda: remote(mine, mine, self.fs.at[1, chunk], self.fr.at[1, chunk], (d, sib)),
            lambda: remote(others, others, self.fs.at[2, chunk], self.fr.at[2, chunk], (d, sib)),
        ]

    def sum_copies(self, chunk):
        d, t, sib, far, opp = places()
        return [
            lambda: remote(
                self.p.at[chunk, opp], self.ra.at[chunk, 1], self.ps.at[0, chunk], self.pr.at[0, chunk], (d, sib)
            ),
            lambda: remote(
                self.p.at[chunk, sib], self.ra.at[chunk, 0], self.ps.at[1, chunk], self.pr.at[1, chunk], (d, sib)
            ),
            lambda: remote(self.sb.at[chunk], self.rb.at[chunk], self.ps.at[2, chunk], self.pr.at[2, chunk], (d, far)),
        ]

    def back_rows(self, expert):
        return pl.ds(pl.multiple_of(expert * self.cap, 16), self.cap)

    def back_copy(self, source, expert, target):
        d, t, sib, far, opp = places()
        chunk, rows = self.slot(source)
        return remote(
            self.ro.at[chunk, rows],
            self.ret.at[self.back_rows(expert)],
            self.rs.at[source],
            self.rr.at[expert],
            (target, t),
        )

    def chunk_of(self, i):
        d = lax.axis_index("dp")
        return lax.rem(d // self.group - i + 2 * CHUNKS, CHUNKS)

    def members(self, chunk, action):
        def one(j, carry):
            action(chunk * self.group + j)
            return carry

        lax.fori_loop(0, self.group, one, 0)

    def run(self, compute):
        d, t, sib, far, opp = places()

        def arrive(chunk):
            def wait(source):
                @pl.when(source != d)
                def _():
                    self.out_copy(0, source, source).wait_recv()

            self.members(chunk, wait)
            far_copy, near_copy, pass_copy = self.spread_copies(chunk)
            far_copy().start()
            near_copy().start()

        def forward(chunk):
            far_copy, near_copy, pass_copy = self.spread_copies(chunk)
            far_copy().wait_recv()
            pass_copy().start()

        def work(chunk):
            far_copy, near_copy, pass_copy = self.spread_copies(chunk)
            near_copy().wait_recv()
            pass_copy().wait_recv()
            rows = jnp.concatenate([self.x[chunk, q] for q in range(SLICES)], axis=1)
            products = compute(chunk, rows)
            for q in range(SLICES):
                self.p[chunk, q] = products[:, q * HALF : (q + 1) * HALF].astype(bf16)
            first, second, third = self.sum_copies(chunk)
            first().start()
            second().start()

        def add_near(chunk):
            first, second, third = self.sum_copies(chunk)
            first().wait_recv()
            self.sb[chunk] = (self.p[chunk, far].astype(f32) + self.ra[chunk, 1].astype(f32)).astype(bf16)
            third().start()

        def add_far(chunk):
            first, second, third = self.sum_copies(chunk)
            second().wait_recv()
            third().wait_recv()
            mine = self.p[chunk, t].astype(f32) + self.ra[chunk, 0].astype(f32)
            self.ro[chunk] = (mine + self.rb[chunk].astype(f32)).astype(bf16)

            def send(source):
                @pl.when(source != d)
                def _():
                    self.back_copy(source, d, source).start()

                @pl.when(source == d)
                def _():
                    spot, rows = self.slot(source)
                    self.ret[self.back_rows(d)] = self.ro[spot, rows]

            self.members(chunk, send)

        stages = ((arrive, 0), (forward, 1), (work, 2), (add_near, 3), (add_far, 4))

        def step(i, carry):
            for stage, lag in stages:

                @pl.when((i >= lag) & (i < CHUNKS + lag))
                def _(stage=stage, lag=lag):
                    stage(self.chunk_of(i - lag))

            return carry

        lax.fori_loop(0, CHUNKS + stages[-1][1], step, 0)

    def wait_back(self):
        d = lax.axis_index("dp")

        def one(j, carry):
            e = lax.rem(d + j, self.n)
            self.back_copy(d, e, e).wait_recv()
            return carry

        lax.fori_loop(1, self.n, one, 0)

    def wait_sends(self):
        d = lax.axis_index("dp")

        def one(j, carry):
            e = lax.rem(d + j, self.n)
            self.out_copy(j, d, e).wait_send()
            self.back_copy(e, d, e).wait_send()
            return carry

        lax.fori_loop(1, self.n, one, 0)

        def two(chunk, carry):
            for copy in self.spread_copies(chunk) + self.sum_copies(chunk):
                copy().wait_send()
            return carry

        lax.fori_loop(0, CHUNKS, two, 0)


gelu_c = 0.7978845608028654
gelu_a = 0.044715


def expert_forward_kernel(
    n,
    cap,
    layer,
    part,
    h,
    gains,
    router_t,
    targ_row,
    targ,
    routes_row,
    wg_f,
    wu_f,
    wd_f,
    mid,
    nt_out,
    r2,
    gates,
    picked,
    y_out,
    r1_next,
    hg_full,
    x_out,
    inner_out,
    act_out,
    slope_out,
    wg_out,
    wu_out,
    wd_out,
    wg_stage,
    wu_stage,
    wd_stage,
    wg,
    wu,
    wd,
    inner,
    act,
    slope,
    hot,
    load_sems,
    save_sems,
    chunk_sems,
    *rest,
):
    d, t, sib, far, opp = places()
    reduce = Reduce(part, rest[0:4])
    tiny_one = Tiny(rest[4:7])
    tiny_two = Tiny(rest[7:10])
    tiny_three = Tiny(rest[10:13])
    gather = Gather(rest[13:16])
    route = Route(n, cap, rest[16:])
    loads = [
        pltpu.make_async_copy(src.at[layer, 0], dst, load_sems.at[i])
        for i, (src, dst) in enumerate(((wg_f, wg_stage), (wu_f, wu_stage), (wd_f, wd_stage)))
    ]
    for copy in loads:
        copy.start()
    greet(n, True)
    reduce.start()
    middle = h[...] + reduce.total()
    mid[...] = middle
    tiny_one.start(to_row(jnp.sum(middle * middle, axis=1, keepdims=True)))
    scale = to_cols(lax.rsqrt(tiny_one.total() * (1.0 / D) + eps_norm))
    r2[...] = scale
    normed = (middle * scale[:, :1] * gains[0:1]).astype(bf16)
    nt_out[...] = normed
    tiny_two.start(nt(router_t[...], normed))

    def make_block(e):
        number = e * cap + lax.broadcasted_iota(jnp.int32, (cap, SEQ), 0)
        hit = (targ_row[0:1] == number) | (targ_row[1:2] == number)
        return nn(hit.astype(f32).astype(bf16), nt_out[...]).astype(bf16)

    route.dispatch(make_block)
    for copy in loads:
        copy.wait()

    def narrow(i, carry):
        rows = pl.ds(pl.multiple_of(i * 64, 64), 64)
        wg[rows] = wg_stage[rows].astype(bf16)
        wu[rows] = wu_stage[rows].astype(bf16)
        return carry

    def narrow_down(i, carry):
        rows = pl.ds(pl.multiple_of(i * 64, 64), 64)
        wd[rows] = wd_stage[rows].astype(bf16)
        return carry

    lax.fori_loop(0, D // 64, narrow, 0)
    lax.fori_loop(0, wd.shape[0] // 64, narrow_down, 0)
    saves = [
        pltpu.make_async_copy(src, dst, save_sems.at[i])
        for i, (src, dst) in enumerate(((wg, wg_out), (wu, wu_out), (wd, wd_out)))
    ]
    for copy in saves:
        copy.start()

    logits = tiny_two.total()
    expert_no = lax.broadcasted_iota(jnp.int32, logits.shape, 0)
    chosen = [
        jnp.sum(jnp.where(expert_no == routes_row[k : k + 1], logits, 0.0), axis=0, keepdims=True)
        for k in range(2)
    ]
    share = [1.0 / (1.0 + jnp.exp(chosen[1 - k] - chosen[k])) for k in range(2)]
    place = lax.broadcasted_iota(jnp.int32, (8, SEQ), 0)
    gates[...] = to_cols(jnp.where(place == 0, share[0], share[1]))

    def chunk_saves(chunk):
        return [
            pltpu.make_async_copy(src.at[chunk], dst.at[chunk], chunk_sems.at[i, chunk])
            for i, (src, dst) in enumerate(((route.x, x_out), (inner, inner_out), (act, act_out), (slope, slope_out)))
        ]

    def compute(chunk, rows):
        gate_pre = nn(rows, wg[...])
        up_pre = nn(rows, wu[...])
        square = gate_pre * gate_pre
        bent = jnp.tanh(gelu_c * gate_pre * (1.0 + gelu_a * square))
        half = 0.5 * (1.0 + bent)
        active = gate_pre * half
        steep = half + 0.5 * gate_pre * (1.0 - bent * bent) * (gelu_c * (1.0 + 3.0 * gelu_a * square))
        inner_rows = (active * up_pre).astype(bf16)
        inner[chunk] = inner_rows
        act[chunk] = active.astype(bf16)
        slope[chunk] = (up_pre * steep).astype(bf16)
        for copy in chunk_saves(chunk):
            copy.start()
        return nn(inner_rows, wd[...])

    route.run(compute)
    for k in range(2):
        hot[k] = hot_columns(targ, k, n * cap)
    route.wait_back()
    y = mid[...]
    for k in range(2):
        rows = nn(hot[k], route.ret[...])
        picked[k] = rows.astype(bf16)
        y = y + gates[:, k : k + 1] * rows
    y_out[...] = y
    tiny_three.start(to_row(jnp.sum(y * y, axis=1, keepdims=True)))
    gather.start((y * gains[1:2]).astype(bf16))
    r1_next[...] = to_cols(lax.rsqrt(tiny_three.total() * (1.0 / D) + eps_norm))
    gather.forward()
    gather.finish()
    stores = gather.store(hg_full, save_sems.at[pl.ds(3, SLICES)])
    route.wait_sends()
    for copy in saves + stores:
        copy.wait()

    def drain(chunk, carry):
        for copy in chunk_saves(chunk):
            copy.wait()
        return carry

    lax.fori_loop(0, CHUNKS, drain, 0)


def expert_forward(n, layer, part, h, gains, router_t, targ_row, targ, routes_row, w_gate, w_up, w_down):
    cap = 3 * SEQ // n
    rows = n * cap // CHUNKS
    hidden = w_gate.shape[3]
    experts = router_t.shape[0]
    outs = [
        (shaped((SEQ, HALF), f32), vmem_spec),
        (shaped((SEQ, HALF), bf16), vmem_spec),
        (shaped((SEQ, LANES), f32), vmem_spec),
        (shaped((SEQ, LANES), f32), vmem_spec),
        (shaped((2, SEQ, HALF), bf16), vmem_spec),
        (shaped((SEQ, HALF), f32), vmem_spec),
        (shaped((SEQ, LANES), f32), vmem_spec),
        (shaped((SEQ, D), bf16), any_spec),
        (shaped((CHUNKS, SLICES, rows, HALF), bf16), any_spec),
        (shaped((CHUNKS, rows, hidden), bf16), any_spec),
        (shaped((CHUNKS, rows, hidden), bf16), any_spec),
        (shaped((CHUNKS, rows, hidden), bf16), any_spec),
        (shaped((D, hidden), bf16), any_spec),
        (shaped((D, hidden), bf16), any_spec),
        (shaped((hidden, D), bf16), any_spec),
    ]
    return pl.pallas_call(
        functools.partial(expert_forward_kernel, n, cap, layer),
        out_shape=[one[0] for one in outs],
        in_specs=[vmem_spec] * 7 + [any_spec] * 3,
        out_specs=[one[1] for one in outs],
        scratch_shapes=[
            pltpu.VMEM((D, hidden), f32),
            pltpu.VMEM((D, hidden), f32),
            pltpu.VMEM((hidden, D), f32),
            pltpu.VMEM((D, hidden), bf16),
            pltpu.VMEM((D, hidden), bf16),
            pltpu.VMEM((hidden, D), bf16),
            pltpu.VMEM((CHUNKS, rows, hidden), bf16),
            pltpu.VMEM((CHUNKS, rows, hidden), bf16),
            pltpu.VMEM((CHUNKS, rows, hidden), bf16),
            pltpu.VMEM((2, SEQ, n * cap), bf16),
            pltpu.SemaphoreType.DMA((3,)),
            pltpu.SemaphoreType.DMA((3 + SLICES,)),
            pltpu.SemaphoreType.DMA((4, CHUNKS)),
        ]
        + Reduce.scratch(SEQ)
        + Tiny.scratch(8, SEQ)
        + Tiny.scratch(experts, SEQ)
        + Tiny.scratch(8, SEQ)
        + Gather.scratch(SEQ)
        + Route.scratch(n, cap),
        compiler_params=pltpu.CompilerParams(
            vmem_limit_bytes=vmem_bytes, collective_id=1 + layer, has_side_effects=True
        ),
    )(part, h, gains, router_t, targ_row, targ, routes_row, w_gate, w_up, w_down)


def gather_weights_kernel(n, qkv, out, small, qkv_all, out_all, small_all, qkv_low, out_low, copy_sems, send, recv):
    d, t, sib, far, opp = places()
    near = d + 1 - 2 * lax.rem(d, 2)
    rows = qkv.shape[2]
    greet(n, True)
    views = [(lambda i: small_all.at[i], small)]

    def qkv_view(layer):
        return lambda i: qkv_all.at[layer, :, pl.ds(pl.multiple_of(i * rows, 16), rows)]

    def out_view(layer):
        return lambda i: out_all.at[layer, pl.ds(pl.multiple_of(i * rows, 16), rows)]

    for layer in range(LAYERS):
        views.append((qkv_view(layer), qkv_low.at[layer]))
        views.append((out_view(layer), out_low.at[layer]))

    def copies(piece, k):
        view, src = views[piece]
        peer = lax.rem(d + 2 * k, n)
        source = lax.rem(d - 2 * k + n, n)
        return (
            lambda: remote(src, view(d), send.at[piece, 0, k], recv.at[piece, 0, k], (peer, t)),
            lambda: remote(view(source), view(source), send.at[piece, 1, k], recv.at[piece, 1, k], (near, t)),
        )

    def own(piece):
        view, src = views[piece]
        return remote(src, view(d), send.at[piece, 1, 0], recv.at[piece, 1, 0], (near, t))

    def keep(piece):
        view, src = views[piece]
        return pltpu.make_async_copy(src, view(d), copy_sems.at[piece])

    for piece in range(len(views)):
        if piece > 0:
            layer = (piece - 1) // 2
            if (piece - 1) % 2 == 0:
                qkv_low[layer] = qkv[layer].astype(bf16)
            else:
                out_low[layer] = out[layer].astype(bf16)
        for k in range(1, n // 2):
            copies(piece, k)[0]().start()
        own(piece).start()
        keep(piece).start()
    for piece in range(len(views)):
        for k in range(1, n // 2):
            direct, passed = copies(piece, k)
            direct().wait_recv()
            passed().start()
    for piece in range(len(views)):
        own(piece).wait()
        keep(piece).wait()
        for k in range(1, n // 2):
            direct, passed = copies(piece, k)
            passed().wait()
            direct().wait_send()


def gather_weights(n, qkv, out, small):
    width = qkv.shape[3]
    pieces = 1 + 2 * LAYERS
    return pl.pallas_call(
        functools.partial(gather_weights_kernel, n),
        out_shape=[
            shaped((LAYERS, 3, D, width), bf16),
            shaped((LAYERS, D, width), bf16),
            shaped((n,) + small.shape, f32),
        ],
        in_specs=[vmem_spec] * 3,
        out_specs=[any_spec] * 3,
        scratch_shapes=[
            pltpu.VMEM(qkv.shape, bf16),
            pltpu.VMEM(out.shape, bf16),
            pltpu.SemaphoreType.DMA((pieces,)),
            pltpu.SemaphoreType.DMA((pieces, 2, n // 2)),
            pltpu.SemaphoreType.DMA((pieces, 2, n // 2)),
        ],
        compiler_params=pltpu.CompilerParams(
            vmem_limit_bytes=vmem_bytes, collective_id=0, has_side_effects=True
        ),
    )(qkv, out, small)


class NormBack:
    scratch = lambda: Reduce.scratch(SEQ) + Tiny.scratch(8, SEQ)
    count = 4 + 3

    def __init__(self, part, refs):
        self.reduce = Reduce(part, refs[0:4])
        self.tiny = Tiny(refs[4:7])

    def start(self):
        self.reduce.start()

    def finish(self, h, r1, gain, midg):
        grad = self.reduce.total()
        return norm_backward(self.tiny, grad, h[...], r1[:, :1], gain, midg)


def norm_backward(tiny, grad, rows, scale, gain, upstream):
    weighted = grad * gain
    tiny.start(to_row(jnp.sum(weighted * rows, axis=1, keepdims=True)))
    gain_grad = jnp.sum(grad * rows * scale, axis=0, keepdims=True)
    base = upstream[...] + scale * weighted
    mean = to_cols(tiny.total())[:, :1] * (1.0 / D)
    return base - rows * (scale * scale * scale * mean), gain_grad


def expert_backward_kernel(n, cap, layer, last, *refs):
    refs = list(refs)

    def take(count):
        out = refs[:count]
        del refs[:count]
        return out

    (dy_in,) = take(1)
    if not last:
        part, h_next, r1_next = take(3)
    gains, router_t, targ_row, targ, routes_row, picked, gates, mid, normed, r2 = take(10)
    x_in, inner_in, act_in, slope_in, wg_in, wu_in, wd_in = take(7)
    if not last:
        take(3)
    midg, gain_rows, router_g, agf, wg_grad, wu_grad, wd_grad = take(7)
    wg, wu, wd, xs, inner, act, slope, gpg, upg, dy, pgs, hot, wg_stage, wu_stage, wd_stage = take(15)
    load_sems, save_sems, store_sems = take(3)
    d, t, sib, far, opp = places()
    tiny_one = Tiny(take(3))
    tiny_two = Tiny(take(3))
    gather = Gather(take(3))
    if not last:
        head = NormBack(part, take(NormBack.count))
    route = Route(n, cap, refs)
    loads = [
        pltpu.make_async_copy(src, dst, load_sems.at[i])
        for i, (src, dst) in enumerate(
            ((wd_in, wd), (act_in, act), (slope_in, slope), (wg_in, wg), (wu_in, wu), (inner_in, inner), (x_in, xs))
        )
    ]
    for copy in loads:
        copy.start()
    greet(n, True)
    place = lax.broadcasted_iota(jnp.int32, (8, SEQ), 0)
    gain_place = lax.broadcasted_iota(jnp.int32, (8, HALF), 0)
    if last:
        dy[...] = dy_in[...].astype(f32)
        gain_one = jnp.zeros((1, HALF), f32)
    else:
        head.start()
        value, gain_one = head.finish(h_next, r1_next, gains[1:2], dy_in)
        dy[...] = value

    for k in range(2):
        pgs[k * SEQ : (k + 1) * SEQ] = (gates[:, k : k + 1] * dy[...]).astype(bf16)

    def make_block(e):
        number = e * cap + lax.broadcasted_iota(jnp.int32, (cap, SEQ), 0)
        hits = [(targ_row[k : k + 1] == number).astype(f32).astype(bf16) for k in range(2)]
        return nn(jnp.concatenate(hits, axis=1), pgs[...]).astype(bf16)

    route.dispatch(make_block)
    shares = [to_row(jnp.sum(dy[...] * picked[k].astype(f32), axis=1, keepdims=True)) for k in range(2)]
    tiny_one.start(jnp.where(place == 0, shares[0], shares[1]))
    for copy in loads[:5]:
        copy.wait()
    share_grad = tiny_one.total()
    gate_rows = jnp.transpose(gates[...])[:8]
    product = gate_rows * share_grad
    both = product[0:1] + product[1:2]
    chosen = gate_rows * (share_grad - both)
    experts = router_t.shape[0]
    expert_no = lax.broadcasted_iota(jnp.int32, (experts, SEQ), 0)
    logit_g = jnp.zeros((experts, SEQ), f32)
    for k in range(2):
        logit_g = logit_g + jnp.where(expert_no == routes_row[k : k + 1], chosen[k : k + 1], 0.0)
    logit_low = logit_g.astype(bf16)
    router_g[...] = nn(logit_low, normed[...])

    def compute(chunk, rows):
        inner_grad = nt(rows, wd[...])
        up_low = (inner_grad * act[chunk].astype(f32)).astype(bf16)
        gate_low = (inner_grad * slope[chunk].astype(f32)).astype(bf16)
        upg[chunk] = up_low
        gpg[chunk] = gate_low
        return nt(gate_low, wg[...]) + nt(up_low, wu[...])

    route.run(compute)
    for copy in loads[5:]:
        copy.wait()
    rows = xs.shape[0] * xs.shape[2]
    hidden = wg.shape[1]
    hot[...] = hot_columns(targ, 0, n * cap) + hot_columns(targ, 1, n * cap)
    route.wait_back()
    grad = nn(hot[...], route.ret[...]) + tn(logit_low, router_t[...])
    value, gain_two = norm_backward(tiny_two, grad, mid[...], r2[:, :1], gains[0:1], dy)
    midg[...] = value
    gain_rows[...] = jnp.where(gain_place == 0, gain_two, jnp.where(gain_place == 1, gain_one, 0.0))
    gather.start(value.astype(bf16))

    def store(i, src, dst):
        copy = pltpu.make_async_copy(src, dst, store_sems.at[i])
        return copy

    def slice_copy(i, q, stage, out):
        span = pl.ds(pl.multiple_of(q * HALF, HALF), HALF)
        return pltpu.make_async_copy(stage.at[span], out.at[layer, 0, span], store_sems.at[i, q])

    def one_slice(q, carry):
        span = pl.ds(pl.multiple_of(q * HALF, HALF), HALF)
        features = xs[:, q].reshape(rows, HALF)
        wg_stage[span] = tn(features, gpg[...].reshape(rows, hidden))
        slice_copy(0, q, wg_stage, wg_grad).start()
        wu_stage[span] = tn(features, upg[...].reshape(rows, hidden))
        slice_copy(1, q, wu_stage, wu_grad).start()
        return carry

    lax.fori_loop(0, 2, one_slice, 0)
    gather.forward()
    lax.fori_loop(2, SLICES, one_slice, 0)
    gather.finish()
    stores = gather.store(agf, save_sems)

    tiles = []
    start = 0
    while start < hidden:
        tiles.append((start, min(HALF, hidden - start)))
        start += HALF
    down_copies = []
    for i, (start, size) in enumerate(tiles):
        left = inner[:, :, start : start + size].reshape(rows, size)
        for q in range(SLICES):
            wd_stage[start : start + size, q * HALF : (q + 1) * HALF] = tn(left, route.x[:, q].reshape(rows, HALF))
        copy = pltpu.make_async_copy(
            wd_stage.at[start : start + size], wd_grad.at[layer, 0, start : start + size], store_sems.at[2, i]
        )
        copy.start()
        down_copies.append(copy)
    route.wait_sends()
    for copy in stores + down_copies:
        copy.wait()

    def drain(q, carry):
        slice_copy(0, q, wg_stage, wg_grad).wait()
        slice_copy(1, q, wu_stage, wu_grad).wait()
        return carry

    lax.fori_loop(0, SLICES, drain, 0)


def expert_backward(n, layer, dy_in, before, gains, router_t, targ_row, targ, routes_row, state, grads):
    mid, normed, r2, gates, picked, y, r1_next, hg_full, x, inner, act, slope, wg, wu, wd = state
    last = not before
    cap = 3 * SEQ // n
    rows = n * cap // CHUNKS
    hidden = wg.shape[1]
    experts = router_t.shape[0]
    operands = [dy_in] + list(before)
    operands += [gains, router_t, targ_row, targ, routes_row, picked, gates, mid, normed, r2]
    specs = [vmem_spec] * len(operands)
    operands += [x, inner, act, slope, wg, wu, wd]
    specs += [any_spec] * 7
    aliases = {}
    if grads is not None:
        aliases = {len(operands) + i: 4 + i for i in range(3)}
        operands += list(grads)
        specs += [any_spec] * 3
    outs = [
        (shaped((SEQ, HALF), f32), vmem_spec),
        (shaped((8, HALF), f32), vmem_spec),
        (shaped((experts, HALF), f32), vmem_spec),
        (shaped((SEQ, D), bf16), any_spec),
        (shaped((LAYERS, 1, D, hidden), f32), any_spec),
        (shaped((LAYERS, 1, D, hidden), f32), any_spec),
        (shaped((LAYERS, 1, hidden, D), f32), any_spec),
    ]
    return pl.pallas_call(
        functools.partial(expert_backward_kernel, n, cap, layer, last),
        out_shape=[one[0] for one in outs],
        in_specs=specs,
        out_specs=[one[1] for one in outs],
        input_output_aliases=aliases,
        scratch_shapes=[
            pltpu.VMEM((D, hidden), bf16),
            pltpu.VMEM((D, hidden), bf16),
            pltpu.VMEM((hidden, D), bf16),
            pltpu.VMEM((CHUNKS, SLICES, rows, HALF), bf16),
            pltpu.VMEM((CHUNKS, rows, hidden), bf16),
            pltpu.VMEM((CHUNKS, rows, hidden), bf16),
            pltpu.VMEM((CHUNKS, rows, hidden), bf16),
            pltpu.VMEM((CHUNKS, rows, hidden), bf16),
            pltpu.VMEM((CHUNKS, rows, hidden), bf16),
            pltpu.VMEM((SEQ, HALF), f32),
            pltpu.VMEM((2 * SEQ, HALF), bf16),
            pltpu.VMEM((SEQ, n * cap), bf16),
            pltpu.VMEM((D, hidden), f32),
            pltpu.VMEM((D, hidden), f32),
            pltpu.VMEM((hidden, D), f32),
            pltpu.SemaphoreType.DMA((7,)),
            pltpu.SemaphoreType.DMA((SLICES,)),
            pltpu.SemaphoreType.DMA((3, SLICES)),
        ]
        + Tiny.scratch(8, SEQ)
        + Tiny.scratch(8, SEQ)
        + Gather.scratch(SEQ)
        + ([] if last else NormBack.scratch())
        + Route.scratch(n, cap),
        compiler_params=pltpu.CompilerParams(
            vmem_limit_bytes=vmem_bytes, collective_id=1 + LAYERS + layer, has_side_effects=True
        ),
    )(*operands)


class Scatter:
    scratch = lambda n, block: [
        pltpu.VMEM((n // 2,) + block, bf16),
        pltpu.VMEM((n // 2,) + block, bf16),
        pltpu.VMEM((n // 2,) + block, bf16),
        pltpu.SemaphoreType.DMA((2, n // 2)),
        pltpu.SemaphoreType.DMA((2, n // 2)),
    ]

    def __init__(self, n, block_of, out, refs):
        self.n, self.block_of, self.out = n, block_of, out
        self.near, self.sums, self.got, self.send, self.recv = refs

    def near_copy(self, k):
        d, t, sib, far, opp = places()
        parity = lax.rem(d, 2)
        src = self.block_of(2 * k + 1 - parity)
        return remote(src, self.near.at[k], self.send.at[0, k], self.recv.at[0, k], (d + 1 - 2 * parity, t))

    def owner_copy(self, k, source):
        d, t, sib, far, opp = places()
        return remote(
            self.sums.at[k],
            self.got.at[source],
            self.send.at[1, k],
            self.recv.at[1, source],
            (2 * k + lax.rem(d, 2), t),
        )

    def spot(self, j):
        d = lax.axis_index("dp")
        return lax.rem(d // 2 + j, self.n // 2)

    def start(self):
        def one(j, carry):
            self.near_copy(self.spot(j)).start()
            return carry

        lax.fori_loop(1, self.n // 2 + 1, one, 0)

    def middle(self):
        d = lax.axis_index("dp")

        def one(j, carry):
            k = self.spot(j)
            self.near_copy(k).wait_recv()
            mine = self.block_of(2 * k + lax.rem(d, 2))[...].astype(f32)
            self.sums[k] = (mine + self.near[k].astype(f32)).astype(bf16)

            @pl.when(k != d // 2)
            def _():
                self.owner_copy(k, d // 2).start()

            return carry

        lax.fori_loop(1, self.n // 2 + 1, one, 0)

    def finish(self):
        d = lax.axis_index("dp")
        self.out[...] = self.sums[d // 2].astype(f32)

        def one(j, carry):
            k = self.spot(j)
            self.owner_copy(k, k).wait_recv()
            self.out[...] = self.out[...] + self.got[k].astype(f32)
            return carry

        lax.fori_loop(1, self.n // 2, one, 0)

        def two(j, carry):
            k = self.spot(j)
            self.owner_copy(k, d // 2).wait_send()
            return carry

        lax.fori_loop(1, self.n // 2, two, 0)

        def three(k, carry):
            self.near_copy(k).wait_send()
            return carry

        lax.fori_loop(0, self.n // 2, three, 0)


def final_kernel(n, experts, *refs):
    refs = list(refs)

    def take(count):
        out = refs[:count]
        del refs[:count]
        return out

    part, h, r1, gain, midg = take(5)
    qkvgs = take(LAYERS)
    wogs = take(LAYERS)
    gain_rows = take(LAYERS)
    router_gs = take(LAYERS)
    tables = take(LAYERS)
    dx_full, qkv_out, wo_out, small_out = take(4)
    pack, packs, pack_send, pack_recv, all_send, all_recv, save_sems = take(7)
    d, t, sib, far, opp = places()
    head = NormBack(part, take(NormBack.count))
    gather = Gather(take(3))
    own = D // n
    scatters = []
    for layer in reversed(range(LAYERS)):

        def rows_of(e):
            return pl.ds(pl.multiple_of(e * own, 16), own)

        def qkv_block(e, ref=qkvgs[layer]):
            return ref.at[:, rows_of(e)]

        def out_block(e, ref=wogs[layer]):
            return ref.at[rows_of(e)]

        scatters.append(Scatter(n, qkv_block, qkv_out.at[layer], take(5)))
        scatters.append(Scatter(n, out_block, wo_out.at[layer], take(5)))
    greet(n, True)
    head.start()
    for one in scatters:
        one.start()
    dx, gain_one = head.finish(h, r1, gain[...], midg)
    gather.start(dx.astype(bf16))
    place = lax.broadcasted_iota(jnp.int32, (8, HALF), 0)
    pack[0:8] = jnp.where(
        place == 0,
        gain_one,
        jnp.where(
            place == 1,
            gain_rows[0][0:1],
            jnp.where(place == 2, gain_rows[0][1:2], jnp.where(place == 3, gain_rows[1][0:1], 0.0)),
        ),
    )
    pack[8:16] = jnp.concatenate([tables[0][...], tables[1][...]], axis=1)
    for layer in range(LAYERS):
        pack[16 + layer * experts : 16 + (layer + 1) * experts] = router_gs[layer][...]

    def pack_copy(j, source, target):
        return remote(pack, packs.at[source], pack_send.at[j], pack_recv.at[source], (target, t))

    def spread(j, carry):
        pack_copy(j, d, lax.rem(d + j, n)).start()
        return carry

    lax.fori_loop(1, n, spread, 0)
    gather.forward()
    for one in scatters:
        one.middle()
    packs[d] = pack[...]

    def collect(j, carry):
        source = lax.rem(d + j, n)
        pack_copy(j, source, source).wait_recv()
        return carry

    lax.fori_loop(1, n, collect, 0)

    def add(i, carry):
        return carry + packs[i]

    small_out[t] = lax.fori_loop(1, n, add, packs[0])

    def all_copies():
        return [
            remote(small_out.at[t], small_out.at[t], all_send.at[i], all_recv.at[i], (d, peer))
            for i, peer in enumerate((sib, far, opp))
        ]

    for copy in all_copies():
        copy.start()
    gather.finish()
    stores = gather.store(dx_full, save_sems)
    for one in scatters:
        one.finish()

    def sent(j, carry):
        pack_copy(j, d, lax.rem(d + j, n)).wait_send()
        return carry

    lax.fori_loop(1, n, sent, 0)
    for copy in all_copies():
        copy.wait()
    for copy in stores:
        copy.wait()


def final_exchange(n, experts, part, h, r1, gain, midg, qkvgs, wogs, gain_rows, router_gs, tables):
    own = D // n
    width = wogs[0].shape[1]
    pack_rows = 16 + LAYERS * experts
    operands = [part, h, r1, gain, midg] + qkvgs + wogs + gain_rows + router_gs + tables
    outs = [
        (shaped((SEQ, D), bf16), any_spec),
        (shaped((LAYERS, 3, own, width), f32), vmem_spec),
        (shaped((LAYERS, own, width), f32), vmem_spec),
        (shaped((SLICES, pack_rows, HALF), f32), vmem_spec),
    ]
    scatter_scratch = []
    for layer in range(LAYERS):
        scatter_scratch += Scatter.scratch(n, (3, own, width)) + Scatter.scratch(n, (own, width))
    return pl.pallas_call(
        functools.partial(final_kernel, n, experts),
        out_shape=[one[0] for one in outs],
        in_specs=[vmem_spec] * len(operands),
        out_specs=[one[1] for one in outs],
        scratch_shapes=[
            pltpu.VMEM((pack_rows, HALF), f32),
            pltpu.VMEM((n, pack_rows, HALF), f32),
            pltpu.SemaphoreType.DMA((n,)),
            pltpu.SemaphoreType.DMA((n,)),
            pltpu.SemaphoreType.DMA((3,)),
            pltpu.SemaphoreType.DMA((3,)),
            pltpu.SemaphoreType.DMA((SLICES,)),
        ]
        + NormBack.scratch()
        + Gather.scratch(SEQ)
        + scatter_scratch,
        compiler_params=pltpu.CompilerParams(
            vmem_limit_bytes=vmem_bytes, collective_id=1 + 2 * LAYERS, has_side_effects=True
        ),
    )(*operands)


def low(v):
    return v.astype(bf16).astype(f32)


def feature_slice(rows):
    t = lax.axis_index("tensor")
    return lax.dynamic_slice_in_dim(rows, t * HALF, HALF, rows.ndim - 1)


def local(tokens, cotangent, w_qkv, w_out, router, gains, rel_table, w_gate, w_up, w_down, routes, slots, segments):
    n = lax.axis_size("dp")
    own = D // n
    experts = router.shape[2]
    heads = rel_table.shape[2]
    cap = 3 * SEQ // n
    flat = jnp.concatenate([low(gains).reshape(-1), low(router).reshape(-1), low(rel_table).reshape(-1)])
    padded = -(-flat.shape[0] // (8 * LANES)) * 8 * LANES
    small = jnp.pad(flat, (0, padded - flat.shape[0])).reshape(-1, LANES)
    qkv_all, out_all, small_all = gather_weights(n, w_qkv, w_out, small)
    flat_all = small_all.reshape(n, -1)
    cut_one = 4 * own
    cut_two = cut_one + LAYERS * own * experts
    cut_three = cut_two + LAYERS * (BUCKETS // n) * heads
    gains_all = flat_all[:, :cut_one].reshape(n, LAYERS, 2, own).transpose(1, 2, 0, 3).reshape(LAYERS, 2, D)
    router_all = (
        flat_all[:, cut_one:cut_two].reshape(n, LAYERS, own, experts).transpose(1, 3, 0, 2).reshape(LAYERS, experts, D)
    ).astype(bf16)
    table_all = (
        flat_all[:, cut_two:cut_three].reshape(n, LAYERS, -1, heads).transpose(1, 3, 0, 2).reshape(LAYERS, heads, BUCKETS)
    )
    table_all = jnp.pad(table_all, ((0, 0), (0, 8 - heads), (0, 0))).astype(bf16)
    gain_mine = feature_slice(gains_all)
    router_mine = feature_slice(router_all)
    targ = routes * cap + slots
    targ_row = targ.transpose(0, 2, 1)
    routes_row = routes.transpose(0, 2, 1)
    seg_col = segments.reshape(SEQ, 1)
    seg_row = segments.reshape(1, SEQ)

    h = feature_slice(tokens).astype(f32)
    ones = jnp.ones((1, HALF), f32)
    kept = []
    hg, r1 = None, None
    for layer in range(LAYERS):
        first = layer == 0
        result = attention_forward(
            first,
            tokens if first else hg,
            gains_all[0, 0:1] if first else r1,
            qkv_all[layer],
            out_all[layer],
            table_all[layer],
            seg_col,
            seg_row,
        )
        if first:
            hg, r1 = result[:2]
            result = result[2:]
        proj, lse, ctx, part = result
        after = gain_mine[layer + 1, 0:1] if layer + 1 < LAYERS else ones
        two_gains = jnp.concatenate([gain_mine[layer, 1:2], after])
        state = expert_forward(
            n,
            layer,
            part,
            h,
            two_gains,
            router_mine[layer],
            targ_row[layer],
            targ[layer],
            routes_row[layer],
            w_gate,
            w_up,
            w_down,
        )
        kept.append((h, hg, r1, proj, lse, ctx, state))
        h, r1, hg = state[5], state[6], state[7]
    output = hg

    grads = None
    before = []
    upstream = feature_slice(cotangent)
    qkvgs, wogs, gain_rows, router_gs, tables = ([None] * LAYERS for i in range(5))
    for layer in reversed(range(LAYERS)):
        h, hg, r1, proj, lse, ctx, state = kept[layer]
        gain_next = gain_mine[layer + 1, 0:1] if layer + 1 < LAYERS else ones
        two_gains = jnp.concatenate([gain_mine[layer, 1:2], gain_next])
        midg, gain_rows[layer], router_gs[layer], agf, *grads = expert_backward(
            n,
            layer,
            upstream,
            before,
            two_gains,
            router_mine[layer],
            targ_row[layer],
            targ[layer],
            routes_row[layer],
            state,
            grads,
        )
        wogs[layer], qkvgs[layer], part, tables[layer] = attention_backward(
            agf, out_all[layer], ctx, proj, lse, table_all[layer], seg_col, seg_row, hg, r1, qkv_all[layer]
        )
        before = [part, h, r1]
        upstream = midg
    dx, qkv_grad, out_grad, small = final_exchange(
        n,
        experts,
        before[0],
        before[1],
        before[2],
        gain_mine[0, 0:1],
        upstream,
        qkvgs,
        wogs,
        gain_rows,
        router_gs,
        tables,
    )
    d, t = lax.axis_index("dp"), lax.axis_index("tensor")

    def rows_wide(start, count):
        wide = small[:, start : start + count].transpose(1, 0, 2).reshape(count, D)
        return lax.dynamic_slice_in_dim(wide, d * own, own, 1)

    gains_grad = rows_wide(0, 2 * LAYERS).reshape(LAYERS, 2, own)
    router_grad = rows_wide(16, LAYERS * experts).reshape(LAYERS, experts, own).transpose(0, 2, 1)
    table_rows = lax.dynamic_slice_in_dim(small, t, 1, 0)[0, 8 : 8 + heads].reshape(heads, LAYERS, LANES)
    bucket_count = BUCKETS // n
    table_grad = lax.dynamic_slice_in_dim(table_rows, d * bucket_count, bucket_count, 2).transpose(1, 2, 0)
    return (
        output,
        dx.astype(f32),
        qkv_grad,
        out_grad,
        router_grad,
        gains_grad,
        table_grad,
        grads[0],
        grads[1],
        grads[2],
    )


def solution(mesh):
    placed = (
        P("dp", None),
        P("dp", None),
        P(None, None, "dp", "tensor"),
        P(None, "dp", "tensor"),
        P(None, "dp", None),
        P(None, None, "dp"),
        P(None, "dp", "tensor"),
        P(None, "dp", None, "tensor"),
        P(None, "dp", None, "tensor"),
        P(None, "dp", "tensor", None),
        P(None, "dp", None),
        P(None, "dp", None),
        P("dp"),
    )
    return jax.shard_map(
        local,
        mesh=mesh,
        in_specs=placed,
        out_specs=(P("dp", None), P("dp", None)) + placed[2:10],
        check_vma=False,
    )
```

```python
import types

import jax
import jax.numpy as jnp
from jax import lax
from jax.experimental import pallas as pl
from jax.experimental.pallas import tpu as pltpu
from jax.sharding import PartitionSpec as P

D = 1024
HDIM = 64
SEQ = 512
LAYERS = 2
BUCKETS = 32
HALF = 256
SLICES = 4
WINDOW_CHUNKS = 2
STAGE_LAGS = (1, 2, 3, 4)
LANES = 128
WINDOW = 768

eps_norm = 1e-06
rise_points = (12, 16, 23, 32, 46, 64, 91)
masked_score = -1e30
vmem_bytes = 63 * 1024 * 1024
f32 = jnp.float32
bf16 = jnp.bfloat16
MESH = pl.DeviceIdType.MESH
nn_dims = (((1,), (0,)), ((), ()))
nt_dims = (((1,), (1,)), ((), ()))
tn_dims = (((0,), (0,)), ((), ()))
vmem_spec = pl.BlockSpec(memory_space=pltpu.VMEM)
any_spec = pl.BlockSpec(memory_space=pl.ANY)


def nn(a, b):
    return lax.dot_general(a, b, nn_dims, preferred_element_type=f32)


def nt(a, b):
    return lax.dot_general(a, b, nt_dims, preferred_element_type=f32)


def tn(a, b):
    return lax.dot_general(a, b, tn_dims, preferred_element_type=f32)


def shaped(shape, kind):
    return jax.ShapeDtypeStruct(shape, kind)


def bucket_index(offset):
    upward = jnp.where(offset > 0, BUCKETS // 2, 0)
    distance = jnp.abs(offset)
    far_part = 8 + sum(((distance >= rise_point).astype(jnp.int32) for rise_point in rise_points))
    return upward + jnp.where(distance < 8, distance, far_part)


def toeplitz_bias(row):
    tile = jnp.broadcast_to(row, (HALF, WINDOW))
    rolled = pltpu.roll(tile, WINDOW - HALF + 1, 1, stride=1, stride_axis=0)
    return rolled[:, : 2 * HALF]


def diagonal_sums(grad):
    rows = jnp.concatenate([grad, jnp.zeros((HALF, WINDOW - 2 * HALF), f32)], axis=1)
    count = HALF
    while count > 8:
        count //= 2
        rows = rows[:count] + pltpu.roll(rows[count:], WINDOW - count, 1)
    total = jnp.zeros((8, WINDOW), f32)
    place = lax.broadcasted_iota(jnp.int32, (8, WINDOW), 0)
    for i in range(8):
        moved = pltpu.roll(rows, (HALF - 1 - i) % WINDOW, 1)
        total = total + jnp.where(place == i, moved, 0.0)
    return total


def half_lanes(shape, which):
    lane = lax.broadcasted_iota(jnp.int32, shape, 1)
    return (lane < HDIM) if which == 0 else (lane >= HDIM)


def allowed_tile(seg_col, seg_row):
    i = lax.broadcasted_iota(jnp.int32, (HALF, HALF), 0)
    j = lax.broadcasted_iota(jnp.int32, (HALF, HALF), 1)
    return (j <= i) | ((seg_col == seg_row) & (seg_col > 0))


def masked_scores(query, keys, bias, allowed, block):
    raw = nt(query, keys)
    if block == 0:
        return jnp.where(allowed, raw + bias[:, HALF:], masked_score)
    left = raw[:, :HALF] + bias[:, :HALF]
    right = jnp.where(allowed, raw[:, HALF:] + bias[:, HALF:], masked_score)
    return jnp.concatenate([left, right], axis=1)


def bias_rows(table):
    place = lax.broadcasted_iota(jnp.int32, (BUCKETS, WINDOW), 1) - (SEQ - 1)
    hot = (bucket_index(place) == lax.broadcasted_iota(jnp.int32, (BUCKETS, WINDOW), 0)).astype(bf16)
    return nn(table, hot)


def block_rows(block):
    return slice(block * HALF, (block + 1) * HALF)


def attend_block(m, block, first_head):
    width = m.ctx.shape[1]
    rows = block_rows(block)
    count = (block + 1) * HALF
    lane = lax.broadcasted_iota(jnp.int32, (HALF, LANES), 1)
    allowed = allowed_tile(m.seg_col[rows, :1], m.seg_row[:, rows])
    lse = jnp.zeros((HALF, LANES), f32)
    for pair in range(width // LANES):
        cols = slice(pair * LANES, (pair + 1) * LANES)
        q2 = m.proj[rows, cols]
        k2 = m.proj[:count, width + pair * LANES : width + (pair + 1) * LANES]
        v2 = m.proj[:count, 2 * width + pair * LANES : 2 * width + (pair + 1) * LANES]
        outs = []
        for which in range(2):
            head = 2 * pair + which
            scaled = q2 * jnp.asarray(HDIM**-0.5, bf16)
            qm = jnp.where(half_lanes(q2.shape, which), scaled, jnp.zeros_like(q2))
            bias = toeplitz_bias(m.bias[first_head + head : first_head + head + 1])
            scores = masked_scores(qm, k2, bias, allowed, block)
            top = jnp.max(scores, axis=1, keepdims=True)
            powers = jnp.exp(scores - top)
            total = jnp.sum(powers, axis=1, keepdims=True)
            probs = (powers * (1.0 / total)).astype(bf16)
            outs.append(nn(probs, v2))
            lse = jnp.where(lane == head, top + jnp.log(total), lse)
        m.ctx[rows, cols] = jnp.where(half_lanes(outs[0].shape, 0), outs[0], outs[1]).astype(bf16)
    m.lse[rows, :] = lse


def wide_rows(ref, rows):
    return jnp.concatenate([ref[q, rows] for q in range(SLICES)], axis=1)


def project(m, block, c):
    width = m.ctx.shape[1]
    rows = block_rows(block)
    m.proj[rows, c * width : (c + 1) * width] = (
        nn(wide_rows(m.hg, rows), m.wqkv[c]) * m.r1[rows, :1]
    ).astype(bf16)


def project_out(m, block):
    rows = block_rows(block)
    for q in range(SLICES):
        m.part[q, rows] = nt(m.ctx[rows], m.wo[q * HALF : (q + 1) * HALF, :]).astype(bf16)


def attention_block(m, block, first_head):
    for c in range(3):
        project(m, block, c)
    attend_block(m, block, first_head)
    project_out(m, block)


def attention_back_block(m, block, first_head):
    width = m.ctx.shape[1]
    rows = block_rows(block)
    count = (block + 1) * HALF
    dctx = nn(wide_rows(m.ag, rows), m.wo[...]).astype(bf16)
    allowed = allowed_tile(m.seg_col[rows, :1], m.seg_row[:, rows])
    scale = jnp.asarray(HDIM**-0.5, bf16)
    for pair in range(width // LANES):
        cols = slice(pair * LANES, (pair + 1) * LANES)
        q2 = m.proj[rows, cols]
        k2 = m.proj[:count, width + pair * LANES : width + (pair + 1) * LANES]
        v2 = m.proj[:count, 2 * width + pair * LANES : 2 * width + (pair + 1) * LANES]
        g2 = dctx[:, cols]
        outs = []
        dk = None
        dv = None
        for which in range(2):
            head = 2 * pair + which
            mine = half_lanes(q2.shape, which)
            qm = jnp.where(mine, q2 * scale, jnp.zeros_like(q2))
            gm = jnp.where(mine, g2, jnp.zeros_like(g2))
            bias = toeplitz_bias(m.bias[first_head + head : first_head + head + 1])
            scores = masked_scores(qm, k2, bias, allowed, block)
            probs = jnp.exp(scores - m.lse[rows, head : head + 1])
            prob_grad = nt(gm, v2).astype(bf16).astype(f32)
            inner = jnp.sum(probs * prob_grad, axis=1, keepdims=True)
            grad_low = (probs * (prob_grad - inner)).astype(bf16)
            dv_one = tn(probs.astype(bf16), gm)
            dk_one = tn(grad_low, qm)
            dv = dv_one if dv is None else dv + dv_one
            dk = dk_one if dk is None else dk + dk_one
            outs.append(nn(grad_low, k2))
            wide = grad_low.astype(f32)
            if block == 1:
                m.bias_grad[head] = wide
            else:
                m.bias_grad[head, :, HALF:] = m.bias_grad[head, :, HALF:] + wide
        dq = jnp.where(half_lanes(outs[0].shape, 0), outs[0], outs[1]) * HDIM**-0.5
        if block == 1:
            m.dk[:, cols] = dk
            m.dv[:, cols] = dv
        else:
            m.dk[:HALF, cols] = m.dk[:HALF, cols] + dk
            m.dv[:HALF, cols] = m.dv[:HALF, cols] + dv
        m.pg[rows, cols] = dq.astype(bf16)
        m.pg[rows, width + pair * LANES : width + (pair + 1) * LANES] = m.dk[rows, cols].astype(bf16)
        m.pg[rows, 2 * width + pair * LANES : 2 * width + (pair + 1) * LANES] = m.dv[rows, cols].astype(bf16)
    for q in range(SLICES):
        total = None
        for c in range(3):
            one = nt(m.pg[rows, c * width : (c + 1) * width], m.wqkv[c, q * HALF : (q + 1) * HALF, :])
            total = one if total is None else total + one
        m.part[q, rows] = total.astype(bf16)


def table_gradient(m):
    place = lax.broadcasted_iota(jnp.int32, (8, WINDOW), 0)
    diag_all = jnp.zeros((8, WINDOW), f32)
    for head in range(m.bias_grad.shape[0]):
        sums = jnp.sum(diagonal_sums(m.bias_grad[head]), axis=0, keepdims=True)
        diag_all = jnp.where(place == head, sums, diag_all)
    spot = lax.broadcasted_iota(jnp.int32, (WINDOW, LANES), 0) - (SEQ - 1)
    hot = (bucket_index(spot) == lax.broadcasted_iota(jnp.int32, (WINDOW, LANES), 1)).astype(f32)
    return lax.dot_general(
        diag_all, hot, nn_dims, precision=lax.Precision.HIGHEST, preferred_element_type=f32
    )


def out_gradient(m):
    for q in range(SLICES):
        m.wog[q * HALF : (q + 1) * HALF] = tn(m.ag[q], m.ctx[...]).astype(bf16)


def qkv_gradient(m):
    width = m.ctx.shape[1]
    for q in range(SLICES):
        normed = (m.hg[q].astype(f32) * m.r1[:, :1]).astype(bf16)
        for c in range(3):
            m.qkvg[c, q * HALF : (q + 1) * HALF] = tn(normed, m.pg[:, c * width : (c + 1) * width]).astype(bf16)


def places():
    d = lax.axis_index("dp")
    t = lax.axis_index("tensor")
    sib = t + 1 - 2 * lax.rem(t, 2)
    far = lax.rem(t + 2, SLICES)
    opp = SLICES - 1 - t
    return d, t, sib, far, opp


def remote(src, dst, send, recv, device):
    return pltpu.make_async_remote_copy(
        src_ref=src, dst_ref=dst, send_sem=send, recv_sem=recv, device_id=device, device_id_type=MESH
    )


def greet(n, with_dp):
    d, t, sib, far, opp = places()
    barrier = pltpu.get_barrier_semaphore()
    for peer in (sib, far, opp):
        pl.semaphore_signal(barrier, inc=1, device_id=(d, peer), device_id_type=MESH)
    if with_dp:

        def hello(j, carry):
            pl.semaphore_signal(barrier, inc=1, device_id=(lax.rem(d + j, n), t), device_id_type=MESH)
            return carry

        lax.fori_loop(1, n, hello, 0)
    pl.semaphore_wait(barrier, 3 + (n - 1 if with_dp else 0))


class Tiny:
    scratch = lambda rows, cols: [
        pltpu.VMEM((SLICES, rows, cols), f32),
        pltpu.SemaphoreType.DMA((3,)),
        pltpu.SemaphoreType.DMA((3,)),
    ]

    def __init__(self, refs):
        self.buf, self.send, self.recv = refs

    def copies(self):
        d, t, sib, far, opp = places()
        return [
            remote(self.buf.at[t], self.buf.at[t], self.send.at[i], self.recv.at[i], (d, peer))
            for i, peer in enumerate((sib, far, opp))
        ]

    def start(self, tile):
        d, t, sib, far, opp = places()
        self.buf[t] = tile
        for copy in self.copies():
            copy.start()

    def finish(self):
        for copy in self.copies():
            copy.wait()

    def total(self):
        self.finish()
        return (self.buf[0] + self.buf[1]) + (self.buf[2] + self.buf[3])


class Gather:
    scratch = [pltpu.SemaphoreType.DMA((2, 3)), pltpu.SemaphoreType.DMA((2, 3))]

    def __init__(self, buf, refs):
        self.buf = buf
        self.send, self.recv = refs

    def copies(self, b):
        d, t, sib, far, opp = places()
        rows = pl.ds(b * HALF, HALF)
        mine, others = self.buf.at[t, rows], self.buf.at[far, rows]
        return [
            lambda: remote(mine, mine, self.send.at[b, 0], self.recv.at[b, 0], (d, far)),
            lambda: remote(mine, mine, self.send.at[b, 1], self.recv.at[b, 1], (d, sib)),
            lambda: remote(others, others, self.send.at[b, 2], self.recv.at[b, 2], (d, sib)),
        ]

    def start(self, b, tile):
        d, t, sib, far, opp = places()
        self.buf[t, pl.ds(b * HALF, HALF)] = tile
        far_copy, near_copy, pass_copy = self.copies(b)
        far_copy().start()
        near_copy().start()

    def forward(self, b):
        far_copy, near_copy, pass_copy = self.copies(b)
        far_copy().wait_recv()
        pass_copy().start()

    def finish(self, b):
        far_copy, near_copy, pass_copy = self.copies(b)
        near_copy().wait_recv()
        pass_copy().wait_recv()

    def wait_sends(self):
        for b in range(2):
            for copy in self.copies(b):
                copy().wait_send()


class Reduce:
    scratch = [
        pltpu.VMEM((2, SEQ, HALF), bf16),
        pltpu.VMEM((2, SEQ, HALF), bf16),
        pltpu.SemaphoreType.DMA((2, 3)),
        pltpu.SemaphoreType.DMA((2, 3)),
    ]

    def __init__(self, part, refs):
        self.part = part
        self.near, self.across, self.send, self.recv = refs

    def copies(self, b):
        d, t, sib, far, opp = places()
        rows = pl.ds(b * HALF, HALF)

        def one(i, src, dst, peer):
            return lambda: remote(src, dst, self.send.at[b, i], self.recv.at[b, i], (d, peer))

        return [
            one(0, self.part.at[opp, rows], self.near.at[1, rows], sib),
            one(1, self.part.at[sib, rows], self.near.at[0, rows], sib),
            one(2, self.across.at[0, rows], self.across.at[1, rows], far),
        ]

    def start(self, b):
        first, second, third = self.copies(b)
        first().start()
        second().start()

    def middle(self, b):
        d, t, sib, far, opp = places()
        rows = pl.ds(b * HALF, HALF)
        first, second, third = self.copies(b)
        first().wait_recv()
        self.across[0, rows] = (self.part[far, rows].astype(f32) + self.near[1, rows].astype(f32)).astype(bf16)
        third().start()

    def finish(self, b):
        d, t, sib, far, opp = places()
        rows = pl.ds(b * HALF, HALF)
        first, second, third = self.copies(b)
        second().wait_recv()
        mine = self.part[t, rows].astype(f32) + self.near[0, rows].astype(f32)
        third().wait_recv()
        return mine + self.across[1, rows].astype(f32)

    def wait_sends(self):
        for b in range(2):
            for copy in self.copies(b):
                copy().wait_send()


class Saves:
    def __init__(self, sems):
        self.sems, self.copies = sems, []

    def start(self, src, dst):
        copy = pltpu.make_async_copy(src, dst, self.sems.at[len(self.copies)])
        copy.start()
        self.copies.append(copy)
        return copy

    def wait(self):
        for copy in self.copies:
            copy.wait()


def to_row(col):
    return jnp.transpose(jnp.broadcast_to(col, (col.shape[0], LANES)))[:8]


def to_cols(rows8):
    return jnp.transpose(jnp.concatenate([rows8] * (LANES // 8), axis=0))


def int_cols(rows):
    whole = jnp.concatenate([rows.astype(f32)] * (8 // rows.shape[0]), axis=0)
    return to_cols(whole).astype(jnp.int32)


def pick_slice(wide):
    t = lax.axis_index("tensor")
    out = wide[:, :HALF]
    for q in range(1, SLICES):
        out = jnp.where(t == q, wide[:, q * HALF : (q + 1) * HALF], out)
    return out


def hot_columns(targ, k, count):
    return (targ[:, k : k + 1] == lax.broadcasted_iota(jnp.int32, (SEQ, count), 1)).astype(f32).astype(bf16)


class Route:
    @staticmethod
    def piece(cap):
        return 32 if cap % 32 == 0 else 16

    @staticmethod
    def shape(n, cap):
        piece = Route.piece(cap)
        return cap // piece, n * piece

    @staticmethod
    def slots(chunks, rounds):
        return chunks if rounds == 1 else max(chunks, STAGE_LAGS[3] + 1)

    @staticmethod
    def scratch(n, cap, rounds):
        chunks, rows = Route.shape(n, cap)
        slots = Route.slots(chunks, rounds)
        total = chunks * rounds
        return [
            pltpu.VMEM((total, rows, HALF), bf16),
            pltpu.VMEM((total, SLICES, rows, HALF), bf16),
            pltpu.VMEM((slots, SLICES, rows, HALF), bf16),
            pltpu.VMEM((slots, 2, rows, HALF), bf16),
            pltpu.VMEM((slots, rows, HALF), bf16),
            pltpu.VMEM((slots, rows, HALF), bf16),
            pltpu.VMEM((slots, rows, HALF), bf16),
            pltpu.VMEM((total, rows, HALF), bf16),
            pltpu.SemaphoreType.DMA((total, n)),
            pltpu.SemaphoreType.DMA((total, n)),
            pltpu.SemaphoreType.DMA((3, total)),
            pltpu.SemaphoreType.DMA((3, total)),
            pltpu.SemaphoreType.DMA((3, total)),
            pltpu.SemaphoreType.DMA((3, total)),
            pltpu.SemaphoreType.DMA((total, n)),
            pltpu.SemaphoreType.DMA((total, n)),
        ]

    def __init__(self, n, cap, rounds, refs):
        self.n = n
        self.size = Route.piece(cap)
        self.chunks, self.rows = Route.shape(n, cap)
        self.slot_count = Route.slots(self.chunks, rounds)
        self.total = self.chunks * rounds
        (
            self.out,
            self.x,
            self.p,
            self.ra,
            self.sb,
            self.rb,
            self.ro,
            self.ret,
            self.as_,
            self.ar,
            self.fs,
            self.fr,
            self.ps,
            self.pr,
            self.rs,
            self.rr,
        ) = refs

    def span(self, place):
        return pl.ds(pl.multiple_of(place * self.size, 16), self.size)

    def peers(self, action):
        d = lax.axis_index("dp")

        def one(j, carry):
            action(lax.rem(d + j, self.n))
            return carry

        lax.fori_loop(1, self.n, one, 0)

    def out_copy(self, chunk, source, expert):
        d, t, sib, far, opp = places()
        return remote(
            self.out.at[chunk, self.span(expert)],
            self.x.at[chunk, t, self.span(source)],
            self.as_.at[chunk, expert],
            self.ar.at[chunk, source],
            (expert, t),
        )

    def back_copy(self, chunk, source, expert):
        d, t, sib, far, opp = places()
        return remote(
            self.ro.at[self.slot(chunk), self.span(source)],
            self.ret.at[chunk, self.span(expert)],
            self.rs.at[chunk, source],
            self.rr.at[chunk, expert],
            (source, t),
        )

    def spread_copies(self, chunk):
        d, t, sib, far, opp = places()
        mine, others = self.x.at[chunk, t], self.x.at[chunk, far]
        return [
            lambda: remote(mine, mine, self.fs.at[0, chunk], self.fr.at[0, chunk], (d, far)),
            lambda: remote(mine, mine, self.fs.at[1, chunk], self.fr.at[1, chunk], (d, sib)),
            lambda: remote(others, others, self.fs.at[2, chunk], self.fr.at[2, chunk], (d, sib)),
        ]

    def slot(self, chunk):
        return chunk if self.slot_count == self.total else lax.rem(chunk, self.slot_count)

    def reused(self, chunk, action):
        if self.slot_count < self.total:

            @pl.when(chunk >= self.slot_count)
            def _():
                action(chunk - self.slot_count)

    def sum_copies(self, chunk):
        d, t, sib, far, opp = places()
        p, ps, pr = self.p, self.ps, self.pr
        slot = self.slot(chunk)
        return [
            lambda: remote(p.at[slot, opp], self.ra.at[slot, 1], ps.at[0, chunk], pr.at[0, chunk], (d, sib)),
            lambda: remote(p.at[slot, sib], self.ra.at[slot, 0], ps.at[1, chunk], pr.at[1, chunk], (d, sib)),
            lambda: remote(self.sb.at[slot], self.rb.at[slot], ps.at[2, chunk], pr.at[2, chunk], (d, far)),
        ]

    def send(self, chunk, fill):
        d, t, sib, far, opp = places()
        fill(chunk)
        self.peers(lambda e: self.out_copy(chunk, d, e).start())
        self.x[chunk, t, self.span(d)] = self.out[chunk, self.span(d)]

    def begin(self, fill_first, fill):
        self.fill = fill
        for chunk in range(WINDOW_CHUNKS):
            self.send(chunk, fill_first)

    def put(self, chunk, products):
        for q in range(SLICES):
            self.p[self.slot(chunk), q] = products[:, q * HALF : (q + 1) * HALF].astype(bf16)

    def run(self, compute, hook):
        d, t, sib, far, opp = places()

        def more(chunk):
            self.send(chunk, self.fill)

        def arrive(chunk):
            self.peers(lambda s: self.out_copy(chunk, s, s).wait_recv())
            far_copy, near_copy, pass_copy = self.spread_copies(chunk)
            far_copy().start()
            near_copy().start()

        def forward(chunk):
            far_copy, near_copy, pass_copy = self.spread_copies(chunk)
            far_copy().wait_recv()
            pass_copy().start()

        def work(chunk):
            far_copy, near_copy, pass_copy = self.spread_copies(chunk)
            near_copy().wait_recv()
            pass_copy().wait_recv()
            rows = jnp.concatenate([self.x[chunk, q] for q in range(SLICES)], axis=1)

            def sent(old):
                first, second, third = self.sum_copies(old)
                first().wait_send()
                second().wait_send()

            self.reused(chunk, sent)
            compute(chunk, rows)
            first, second, third = self.sum_copies(chunk)
            first().start()
            second().start()

        def add_near(chunk):
            first, second, third = self.sum_copies(chunk)
            first().wait_recv()
            slot = self.slot(chunk)
            self.reused(chunk, lambda old: self.sum_copies(old)[2]().wait_send())
            self.sb[slot] = (self.p[slot, far].astype(f32) + self.ra[slot, 1].astype(f32)).astype(bf16)
            third().start()

        def add_far(chunk):
            first, second, third = self.sum_copies(chunk)
            second().wait_recv()
            third().wait_recv()
            slot = self.slot(chunk)
            self.reused(chunk, lambda old: self.peers(lambda s: self.back_copy(old, s, d).wait_send()))
            mine = self.p[slot, t].astype(f32) + self.ra[slot, 0].astype(f32)
            self.ro[slot] = (mine + self.rb[slot].astype(f32)).astype(bf16)
            self.peers(lambda s: self.back_copy(chunk, s, d).start())
            self.ret[chunk, self.span(d)] = self.ro[slot, self.span(d)]

        stages = (
            (more, -WINDOW_CHUNKS),
            (arrive, 0),
            (forward, STAGE_LAGS[0]),
            (work, STAGE_LAGS[1]),
            (add_near, STAGE_LAGS[2]),
            (add_far, STAGE_LAGS[3]),
        )

        def step(i, carry):
            for stage, lag in stages:

                @pl.when((i >= lag) & (i < self.total + lag))
                def _(stage=stage, lag=lag):
                    stage(i - lag)

            if hook is not None:
                hook(i)
            return carry

        lax.fori_loop(0, self.total + stages[-1][1], step, 0)

    def wait_back(self, first):
        d = lax.axis_index("dp")

        def one(chunk, carry):
            self.peers(lambda e: self.back_copy(chunk, d, e).wait_recv())
            return carry

        lax.fori_loop(first, first + self.chunks, one, 0)

    def returned(self, first):
        return self.ret[first : first + self.chunks].reshape(self.chunks * self.rows, HALF)

    def arrived(self, first, q):
        return self.x[first : first + self.chunks, q].reshape(self.chunks * self.rows, HALF)

    def wait_sends(self):
        d = lax.axis_index("dp")

        def one(chunk, carry):
            self.peers(lambda e: self.out_copy(chunk, d, e).wait_send())
            for copy in self.spread_copies(chunk):
                copy().wait_send()
            return carry

        lax.fori_loop(0, self.total, one, 0)

        def two(chunk, carry):
            self.peers(lambda e: self.back_copy(chunk, e, d).wait_send())
            for copy in self.sum_copies(chunk):
                copy().wait_send()
            return carry

        lax.fori_loop(self.total - self.slot_count, self.total, two, 0)


gelu_c = 0.7978845608028654
gelu_a = 0.044715


class Named:
    def __getattr__(self, name):
        return lambda *rest: (name, *rest)


named = Named()


def call(fn, ins, outs, scratch, collective_id):
    def kernel(*refs):
        refs = list(refs)
        m = types.SimpleNamespace()
        for name, *rest in list(ins) + list(outs):
            setattr(m, name, refs.pop(0))
        for name, kinds in scratch:
            if isinstance(kinds, list):
                setattr(m, name, [refs.pop(0) for one in kinds])
            else:
                setattr(m, name, refs.pop(0))
        fn(m)

    flat = []
    for name, kinds in scratch:
        flat += kinds if isinstance(kinds, list) else [kinds]
    results = pl.pallas_call(
        kernel,
        name=fn.__name__,
        out_shape=[shaped(one[1], one[2]) for one in outs],
        in_specs=[one[2] for one in ins],
        out_specs=[one[3] for one in outs],
        scratch_shapes=flat,
        compiler_params=pltpu.CompilerParams(
            vmem_limit_bytes=vmem_bytes, collective_id=collective_id, has_side_effects=True
        ),
    )(*[one[1] for one in ins])
    return types.SimpleNamespace(**{one[0]: result for one, result in zip(outs, results)})


def gain_of(m, layer, which):
    t = lax.axis_index("tensor")
    return m.wide[t, 2 * layer + which : 2 * layer + which + 1].astype(f32)


def router_of(m, layer, experts):
    t = lax.axis_index("tensor")
    start = 2 * LAYERS + layer * experts
    return m.wide[t][start : start + experts]


def cap_count(cap):
    return 3 * SEQ // cap


def set_targets(m, layer, cap):
    piece = Route.piece(cap)
    chunks, rows = Route.shape(cap_count(cap), cap)
    slots = m.slots_row[layer]
    m.targ_row[...] = (slots // piece) * rows + m.routes_row[layer] * piece + lax.rem(slots, piece)
    m.targ_col[...] = int_cols(m.targ_row[...])


def set_attention_tables(m):
    m.seg_col[...] = int_cols(m.seg_row[...])
    m.bias[...] = bias_rows(m.tab[:, :BUCKETS].astype(bf16))


attention_scratch = [
    named.seg_col(pltpu.VMEM((SEQ, LANES), jnp.int32)),
    named.bias(pltpu.VMEM((8, WINDOW), f32)),
    named.part(pltpu.VMEM((SLICES, SEQ, HALF), bf16)),
    named.reduce(Reduce.scratch),
]


def attention_outs(width):
    return [
        named.proj((SEQ, 3 * width), bf16, vmem_spec),
        named.lse((SEQ, LANES), f32, vmem_spec),
        named.ctx((SEQ, width), bf16, vmem_spec),
        named.r1((SEQ, LANES), f32, vmem_spec),
    ]


def forward_outs(n, cap, hidden):
    chunks, rows = Route.shape(n, cap)
    return [
        named.mid((SEQ, HALF), f32, vmem_spec),
        named.normed((SEQ, HALF), bf16, vmem_spec),
        named.r2((SEQ, LANES), f32, vmem_spec),
        named.gates((SEQ, LANES), f32, vmem_spec),
        named.picked((2, SEQ, HALF), bf16, vmem_spec),
        named.y((SEQ, HALF), f32, vmem_spec),
        named.x_out((chunks, SLICES, rows, HALF), bf16, any_spec),
        named.inner_out((chunks, rows, hidden), bf16, any_spec),
        named.act_out((chunks, rows, hidden), bf16, any_spec),
        named.slope_out((chunks, rows, hidden), bf16, any_spec),
        named.wg_out((hidden, D), bf16, any_spec),
        named.wu_out((hidden, D), bf16, any_spec),
        named.wd_out((hidden, D), bf16, any_spec),
    ]


def forward_scratch(n, cap, hidden, experts):
    chunks, rows = Route.shape(n, cap)
    return [
        named.wg_stage(pltpu.VMEM((hidden, D), f32)),
        named.wu_stage(pltpu.VMEM((hidden, D), f32)),
        named.wd_stage(pltpu.VMEM((hidden, D), f32)),
        named.wg(pltpu.VMEM((hidden, D), bf16)),
        named.wu(pltpu.VMEM((hidden, D), bf16)),
        named.wd(pltpu.VMEM((hidden, D), bf16)),
        named.inner(pltpu.VMEM((chunks, rows, hidden), bf16)),
        named.act(pltpu.VMEM((chunks, rows, hidden), bf16)),
        named.slope(pltpu.VMEM((chunks, rows, hidden), bf16)),
        named.hot(pltpu.VMEM((2, SEQ, n * cap), bf16)),
        named.targ_row(pltpu.VMEM((2, SEQ), jnp.int32)),
        named.targ_col(pltpu.VMEM((SEQ, LANES), jnp.int32)),
        named.load_sems(pltpu.SemaphoreType.DMA((3,))),
        named.save_sems(pltpu.SemaphoreType.DMA((16,))),
        named.chunk_sems(pltpu.SemaphoreType.DMA((4, chunks))),
        named.tiny_one(Tiny.scratch(8, SEQ)),
        named.tiny_two(Tiny.scratch(experts, SEQ)),
        named.route(Route.scratch(n, cap, 1)),
    ]


def start_weight_loads(m, layer):
    loads = [
        pltpu.make_async_copy(src.at[layer, 0], dst, m.load_sems.at[i])
        for i, (src, dst) in enumerate(((m.gate_f, m.wg_stage), (m.up_f, m.wu_stage), (m.down_f, m.wd_stage)))
    ]
    for copy in loads:
        copy.start()
    return loads


def forward_rows(m, layer, experts, tiny_one, tiny_two, route):
    tiny_one.start(to_row(jnp.sum(m.mid[...] * m.mid[...], axis=1, keepdims=True)))
    scale = to_cols(lax.rsqrt(tiny_one.total() * (1.0 / D) + eps_norm))
    m.r2[...] = scale
    m.normed[...] = (m.mid[...] * scale[:, :1] * gain_of(m, layer, 1)).astype(bf16)

    def fill(chunk):
        number = chunk * route.rows + lax.broadcasted_iota(jnp.int32, (route.rows, SEQ), 0)
        hit = (m.targ_row[0:1] == number) | (m.targ_row[1:2] == number)
        route.out[chunk] = nn(hit.astype(f32).astype(bf16), m.normed[...]).astype(bf16)

    return fill


def narrow_weights(stage, low):
    def narrow(i, carry):
        rows = pl.ds(pl.multiple_of(i * 64, 64), 64)
        low[rows] = stage[rows].astype(bf16)
        return carry

    lax.fori_loop(0, low.shape[0] // 64, narrow, 0)


def router_gates(m, layer, tiny_two):
    logits = tiny_two.total()
    expert_no = lax.broadcasted_iota(jnp.int32, logits.shape, 0)
    chosen = [
        jnp.sum(jnp.where(expert_no == m.routes_row[layer, k : k + 1], logits, 0.0), axis=0, keepdims=True)
        for k in range(2)
    ]
    share = [1.0 / (1.0 + jnp.exp(chosen[1 - k] - chosen[k])) for k in range(2)]
    place = lax.broadcasted_iota(jnp.int32, (8, SEQ), 0)
    m.gates[...] = to_cols(jnp.where(place == 0, share[0], share[1]))


def forward_products(m, chunk, rows):
    gate_pre = nt(rows, m.wg[...])
    up_pre = nt(rows, m.wu[...])
    square = gate_pre * gate_pre
    bent = jnp.tanh(gelu_c * gate_pre * (1.0 + gelu_a * square))
    half = 0.5 * (1.0 + bent)
    active = gate_pre * half
    steep = half + 0.5 * gate_pre * (1.0 - bent * bent) * (gelu_c * (1.0 + 3.0 * gelu_a * square))
    inner_rows = (active * up_pre).astype(bf16)
    m.inner[chunk] = inner_rows
    m.act[chunk] = active.astype(bf16)
    m.slope[chunk] = (up_pre * steep).astype(bf16)
    return nn(inner_rows, m.wd[...])


def set_hot(m, count):
    for k in range(2):
        m.hot[k] = hot_columns(m.targ_col, k, count)


def forward_combine(m, route):
    route.wait_back(0)
    y = m.mid[...]
    for k in range(2):
        rows = nn(m.hot[k], route.returned(0))
        m.picked[k] = rows.astype(bf16)
        y = y + m.gates[:, k : k + 1] * rows
    m.y[...] = y


def forward_experts(m, n, cap, layer, experts, loads, saves, hook):
    tiny_one = Tiny(m.tiny_one)
    tiny_two = Tiny(m.tiny_two)
    route = Route(n, cap, 1, m.route)
    fill = forward_rows(m, layer, experts, tiny_one, tiny_two, route)
    route.begin(fill, fill)
    tiny_two.start(nt(router_of(m, layer, experts), m.normed[...]))
    stages = (m.wg_stage, m.wu_stage, m.wd_stage)
    lows = (m.wg, m.wu, m.wd)
    for copy, stage, low, out in zip(loads, stages, lows, (m.wg_out, m.wu_out, m.wd_out)):
        copy.wait()
        narrow_weights(stage, low)
        saves.start(low, out)
    router_gates(m, layer, tiny_two)

    def chunk_saves(chunk):
        pairs = ((route.x, m.x_out), (m.inner, m.inner_out), (m.act, m.act_out), (m.slope, m.slope_out))
        return [
            pltpu.make_async_copy(src.at[chunk], dst.at[chunk], m.chunk_sems.at[i, chunk])
            for i, (src, dst) in enumerate(pairs)
        ]

    def compute(chunk, rows):
        products = forward_products(m, chunk, rows)
        for copy in chunk_saves(chunk):
            copy.start()
        route.put(chunk, products)

    def hook_all(i):
        @pl.when(i == 2)
        def _():
            set_hot(m, n * cap)

        if hook is not None:
            hook(i)

    route.run(compute, hook_all)
    forward_combine(m, route)
    route.wait_sends()

    def drain(chunk, carry):
        for copy in chunk_saves(chunk):
            copy.wait()
        return carry

    lax.fori_loop(0, route.chunks, drain, 0)


class Pieces:
    def __init__(self, n, pieces, send, recv):
        self.n, self.pieces, self.send, self.recv = n, pieces, send, recv

    def copies(self, piece, k):
        d, t, sib, far, opp = places()
        n = self.n
        near = d + 1 - 2 * lax.rem(d, 2)
        view, src = self.pieces[piece]
        peer = lax.rem(d + 2 * k, n)
        source = lax.rem(d - 2 * k + n, n)
        send, recv = self.send, self.recv
        return (
            lambda: remote(src, view(d), send.at[piece, 0, k], recv.at[piece, 0, k], (peer, t)),
            lambda: remote(view(source), view(source), send.at[piece, 1, k], recv.at[piece, 1, k], (near, t)),
        )

    def own(self, piece):
        d, t, sib, far, opp = places()
        near = d + 1 - 2 * lax.rem(d, 2)
        view, src = self.pieces[piece]
        return remote(src, view(d), self.send.at[piece, 1, 0], self.recv.at[piece, 1, 0], (near, t))

    def loop(self, action):
        def one(k, carry):
            action(k)
            return carry

        lax.fori_loop(1, self.n // 2, one, 0)

    def start(self, piece):
        self.loop(lambda k: self.copies(piece, k)[0]().start())
        self.own(piece).start()

    def forward(self, piece):
        def one(k):
            direct, passed = self.copies(piece, k)
            direct().wait_recv()
            passed().start()

        self.loop(one)

    def finish(self, piece):
        self.own(piece).wait_recv()
        self.loop(lambda k: self.copies(piece, k)[1]().wait_recv())

    def wait_sends(self, piece):
        self.own(piece).wait_send()

        def one(k):
            direct, passed = self.copies(piece, k)
            direct().wait_send()
            passed().wait_send()

        self.loop(one)


def place_small(n, small_all, rows):
    own = small_all.shape[2]
    if own == LANES:
        return [
            jnp.concatenate([small_all[2 * q].astype(f32), small_all[2 * q + 1].astype(f32)], axis=1)
            for q in range(SLICES)
        ]
    out = []
    for q in range(SLICES):
        total = jnp.zeros((rows, HALF), f32)
        for i in range(HALF // own):
            lane = lax.broadcasted_iota(jnp.int32, (own, HALF), 1)
            spot = lax.broadcasted_iota(jnp.int32, (own, HALF), 0)
            hot = (lane == spot + i * own).astype(f32).astype(bf16)
            total = total + nn(small_all[q * (HALF // own) + i], hot)
        out.append(total)
    return out


def first_program(n, cap, experts, heads):
    buckets = BUCKETS // n

    def first_kernel(m):
        d, t, sib, far, opp = places()
        own = D // n
        saves = Saves(m.save_sems)
        loads = start_weight_loads(m, 0)
        reduce = Reduce(m.part, m.reduce)

        def span(i):
            return pl.ds(pl.multiple_of(i * own, 16), own)

        views = [
            (lambda i: m.small_all.at[i], m.small),
            (lambda i: m.wqkv.at[0, span(i)], m.qkv_low.at[0, 0]),
            (lambda i: m.wqkv.at[1, span(i)], m.qkv_low.at[0, 1]),
            (lambda i: m.wqkv.at[2, span(i)], m.qkv_low.at[0, 2]),
            (lambda i: m.wo.at[span(i)], m.out_low.at[0]),
            (lambda i: m.wqkv_next.at[:, span(i)], m.qkv_low.at[1]),
            (lambda i: m.wo_next.at[span(i)], m.out_low.at[1]),
        ]
        pieces = Pieces(n, views, m.piece_send, m.piece_recv)
        m.qkv_low[0] = m.qkv[0].astype(bf16)
        greet(n, True)
        pieces.start(0)
        pieces.start(1)
        pieces.start(2)
        m.out_low[0] = m.out[0].astype(bf16)
        m.small_all[d] = m.small[...]
        m.wqkv[:, span(d)] = m.qkv_low[0]
        m.wo[span(d)] = m.out_low[0]
        m.qkv_low[1] = m.qkv[1].astype(bf16)
        m.out_low[1] = m.out[1].astype(bf16)
        saves.start(m.qkv_low.at[1], m.wqkv_next.at[:, span(d)])
        saves.start(m.out_low.at[1], m.wo_next.at[span(d)])
        set_targets(m, 0, cap)
        pieces.forward(0)
        pieces.finish(0)
        rows = m.small.shape[0]
        slices = place_small(n, m.small_all, rows)
        for q in range(SLICES):
            m.wide[q] = slices[q].astype(bf16)
        first = 2 * LAYERS + LAYERS * experts
        table = jnp.zeros((LAYERS * heads, LANES), f32)
        width = m.small_all.shape[2]
        for i in range(n):
            lane = lax.broadcasted_iota(jnp.int32, (width, LANES), 1)
            spot = lax.broadcasted_iota(jnp.int32, (width, LANES), 0)
            hot = ((lane == spot + i * buckets) & (spot < buckets)).astype(f32).astype(bf16)
            table = table + nn(m.small_all[i][first : first + LAYERS * heads], hot)
        m.tab[...] = table
        set_attention_tables(m)
        total = None
        for q in range(SLICES):
            x = m.tok[:, q * HALF : (q + 1) * HALF].astype(f32)
            m.hg[q] = (x * m.wide[q, 0:1].astype(f32)).astype(bf16)
            squares = jnp.sum(x * x, axis=1, keepdims=True)
            total = squares if total is None else total + squares
        m.r1[...] = jnp.broadcast_to(lax.rsqrt(total * (1.0 / D) + eps_norm), (SEQ, LANES))
        saves.start(m.hg, m.hg_out)
        pieces.forward(1)
        pieces.start(3)
        pieces.forward(2)
        pieces.start(4)
        pieces.finish(1)
        for b in range(2):
            project(m, b, 0)
        pieces.forward(3)
        pieces.finish(2)
        for b in range(2):
            project(m, b, 1)
        pieces.forward(4)
        for piece in (5, 6):
            pieces.start(piece)
        pieces.finish(3)
        for b in range(2):
            project(m, b, 2)
        saves.start(m.wqkv, m.wqkv_out)
        for b in range(2):
            attend_block(m, b, 0)
            if b == 0:
                pieces.finish(4)
                saves.start(m.wo, m.wo_out)
            project_out(m, b)
            reduce.start(b)
        for b in range(2):
            reduce.middle(b)
        for b in range(2):
            span_b = block_rows(b)
            m.mid[span_b] = pick_slice(m.tok[span_b].astype(f32)) + reduce.finish(b)

        def hook(i):
            @pl.when(i == 4)
            def _():
                for piece in (5, 6):
                    pieces.forward(piece)

        forward_experts(m, n, cap, 0, experts, loads, saves, hook)
        for piece in (5, 6):
            pieces.finish(piece)
        for piece in range(7):
            pieces.wait_sends(piece)
        reduce.wait_sends()
        saves.wait()

    return first_kernel


def norm_backward(tiny, grad, rows, scale, gain, upstream):
    weighted = grad * gain
    tiny.start(to_row(jnp.sum(weighted * rows, axis=1, keepdims=True)))
    gain_grad = jnp.sum(grad * rows * scale, axis=0, keepdims=True)
    base = upstream + scale * weighted
    mean = to_cols(tiny.total())[:, :1] * (1.0 / D)
    return base - rows * (scale * scale * scale * mean), gain_grad


def backward_outs(n, cap, hidden, experts):
    return [
        named.midg((SEQ, HALF), f32, vmem_spec),
        named.gain_rows((8, HALF), f32, vmem_spec),
        named.router_g((experts, HALF), f32, vmem_spec),
        named.wg_grad((hidden, D), bf16, any_spec),
        named.wu_grad((hidden, D), bf16, any_spec),
        named.wd_grad((hidden, D), bf16, any_spec),
    ]


def backward_ins(state):
    return [
        named.picked(state.picked, vmem_spec),
        named.gates(state.gates, vmem_spec),
        named.mid(state.mid, vmem_spec),
        named.normed(state.normed, vmem_spec),
        named.r2(state.r2, vmem_spec),
        named.x_in(state.x_out, any_spec),
        named.inner_in(state.inner_out, any_spec),
        named.act_in(state.act_out, any_spec),
        named.slope_in(state.slope_out, any_spec),
        named.wg_in(state.wg_out, any_spec),
        named.wu_in(state.wu_out, any_spec),
        named.wd_in(state.wd_out, any_spec),
    ]


def backward_scratch(n, cap, hidden, experts):
    chunks, rows = Route.shape(n, cap)
    return [
        named.wg(pltpu.VMEM((hidden, D), bf16)),
        named.wu(pltpu.VMEM((hidden, D), bf16)),
        named.wd(pltpu.VMEM((hidden, D), bf16)),
        named.xs(pltpu.VMEM((chunks, SLICES, rows, HALF), bf16)),
        named.inner(pltpu.VMEM((chunks, rows, hidden), bf16)),
        named.act(pltpu.VMEM((chunks, rows, hidden), bf16)),
        named.slope(pltpu.VMEM((chunks, rows, hidden), bf16)),
        named.gpg(pltpu.VMEM((chunks, rows, hidden), bf16)),
        named.upg(pltpu.VMEM((chunks, rows, hidden), bf16)),
        named.dy(pltpu.VMEM((SEQ, HALF), f32)),
        named.pgs(pltpu.VMEM((2 * SEQ, HALF), bf16)),
        named.hot(pltpu.VMEM((2, SEQ, n * cap), bf16)),
        named.logit_g(pltpu.VMEM((experts, SEQ), f32)),
        named.targ_row(pltpu.VMEM((2, SEQ), jnp.int32)),
        named.targ_col(pltpu.VMEM((SEQ, LANES), jnp.int32)),
        named.load_sems(pltpu.SemaphoreType.DMA((7,))),
        named.save_sems(pltpu.SemaphoreType.DMA((16,))),
        named.tiny_one(Tiny.scratch(8, SEQ)),
        named.tiny_two(Tiny.scratch(8, SEQ)),
        named.route(Route.scratch(n, cap, 1)),
    ]


def start_backward_loads(m):
    pairs = (
        (m.wd_in, m.wd),
        (m.act_in, m.act),
        (m.slope_in, m.slope),
        (m.wg_in, m.wg),
        (m.wu_in, m.wu),
        (m.inner_in, m.inner),
        (m.x_in, m.xs),
    )
    loads = [pltpu.make_async_copy(src, dst, m.load_sems.at[i]) for i, (src, dst) in enumerate(pairs)]
    for copy in loads:
        copy.start()
    return loads


def backward_rows(m, route):
    for k in range(2):
        m.pgs[k * SEQ : (k + 1) * SEQ] = (m.gates[:, k : k + 1] * m.dy[...]).astype(bf16)

    def fill(chunk, place):
        number = chunk * route.rows + lax.broadcasted_iota(jnp.int32, (route.rows, SEQ), 0)
        hits = [(m.targ_row[k : k + 1] == number).astype(f32).astype(bf16) for k in range(2)]
        route.out[place] = nn(jnp.concatenate(hits, axis=1), m.pgs[...]).astype(bf16)

    return fill


def start_shares(m, tiny):
    place = lax.broadcasted_iota(jnp.int32, (8, SEQ), 0)
    shares = [to_row(jnp.sum(m.dy[...] * m.picked[k].astype(f32), axis=1, keepdims=True)) for k in range(2)]
    tiny.start(jnp.where(place == 0, shares[0], shares[1]))


def logit_gradient(m, layer, experts, tiny):
    share_grad = tiny.total()
    gate_rows = jnp.transpose(m.gates[...])[:8]
    product = gate_rows * share_grad
    both = product[0:1] + product[1:2]
    chosen = gate_rows * (share_grad - both)
    expert_no = lax.broadcasted_iota(jnp.int32, (experts, SEQ), 0)
    logit_g = jnp.zeros((experts, SEQ), f32)
    for k in range(2):
        logit_g = logit_g + jnp.where(expert_no == m.routes_row[layer, k : k + 1], chosen[k : k + 1], 0.0)
    m.logit_g[...] = logit_g
    m.router_g[...] = nn(logit_g.astype(bf16), m.normed[...])


def backward_products(m, chunk, rows):
    inner_grad = nt(rows, m.wd[...])
    up_low = (inner_grad * m.act[chunk].astype(f32)).astype(bf16)
    gate_low = (inner_grad * m.slope[chunk].astype(f32)).astype(bf16)
    m.upg[chunk] = up_low
    m.gpg[chunk] = gate_low
    return nn(gate_low, m.wg[...]) + nn(up_low, m.wu[...])


def backward_tail(m, layer, experts, tiny, route, first, inputs_of, saves, gain_one):
    count = route.chunks * route.rows
    hidden = m.wg.shape[0]

    def product_of(left_ref, right_of, stage, out):
        right = jnp.concatenate([right_of(q) for q in range(SLICES)], axis=1)
        for start in range(0, hidden, HALF):
            size = min(HALF, hidden - start)
            left = left_ref[:, :, start : start + size].reshape(count, size)
            stage[start : start + size] = tn(left, right).astype(bf16)
            saves.start(stage.at[start : start + size], out.at[start : start + size])

    product_of(m.gpg, inputs_of, m.wg, m.wg_grad)
    route.wait_back(first)
    grad = tn(m.logit_g[...].astype(bf16), router_of(m, layer, experts))
    for k in range(2):
        grad = grad + nn(m.hot[k], route.returned(first))
    value, gain_two = norm_backward(tiny, grad, m.mid[...], m.r2[:, :1], gain_of(m, layer, 1), m.dy[...])
    m.midg[...] = value
    gain_place = lax.broadcasted_iota(jnp.int32, (8, HALF), 0)
    m.gain_rows[...] = jnp.where(gain_place == 0, gain_two, jnp.where(gain_place == 1, gain_one, 0.0))
    product_of(m.upg, inputs_of, m.wu, m.wu_grad)
    product_of(m.inner, lambda q: route.arrived(first, q), m.wd, m.wd_grad)
    route.wait_sends()


def backward_experts(m, n, cap, layer, experts, loads, saves, gain_one, hook):
    tiny_one = Tiny(m.tiny_one)
    tiny_two = Tiny(m.tiny_two)
    route = Route(n, cap, 1, m.route)
    fill_one = backward_rows(m, route)

    def fill(chunk):
        fill_one(chunk, chunk)

    route.begin(fill, fill)
    start_shares(m, tiny_one)
    for copy in loads[:5]:
        copy.wait()
    logit_gradient(m, layer, experts, tiny_one)

    def compute(chunk, rows):
        route.put(chunk, backward_products(m, chunk, rows))

    def hook_all(i):
        @pl.when(i == 1)
        def _():
            set_hot(m, n * cap)

        hook(i)

    route.run(compute, hook_all)
    for copy in loads[5:]:
        copy.wait()
    count = route.chunks * route.rows
    backward_tail(
        m, layer, experts, tiny_two, route, 0, lambda q: m.xs[:, q].reshape(count, HALF), saves, gain_one
    )


def top_program(n, cap, experts, heads, layer):
    def top_kernel(m):
        saves = Saves(m.save_sems)
        weight_copies = [
            pltpu.make_async_copy(m.wqkv_in, m.wqkv, m.weight_sems.at[0]),
            pltpu.make_async_copy(m.wo_in, m.wo, m.weight_sems.at[1]),
        ]
        expert_weights = [
            pltpu.make_async_copy(src.at[layer, 0], m.stage, m.load_sems.at[i])
            for i, src in enumerate((m.gate_f, m.up_f, m.down_f))
        ]
        expert_weights[0].start()
        for copy in weight_copies:
            copy.start()
        reduce = Reduce(m.part, m.reduce)
        gather = Gather(m.hg, m.gather)
        tiny = Tiny(m.tiny_zero)
        greet(n, True)
        gain = gain_of(m, layer, 0)
        for b in range(2):
            gather.start(b, (m.h[block_rows(b)] * gain).astype(bf16))
        tiny.start(to_row(jnp.sum(m.h[...] * m.h[...], axis=1, keepdims=True)))
        set_attention_tables(m)
        set_targets(m, layer, cap)
        m.dy[...] = pick_slice(m.cot[...].astype(f32))
        m.r1[...] = to_cols(lax.rsqrt(tiny.total() * (1.0 / D) + eps_norm))
        lows = (m.wg, m.wu, m.wd)
        expert_weights[0].wait()
        narrow_weights(m.stage, lows[0])
        expert_weights[1].start()
        for copy in weight_copies:
            copy.wait()
        gather.forward(0)
        gather.finish(0)
        gather.forward(1)
        attention_block(m, 0, layer * heads)
        reduce.start(0)
        gather.finish(1)
        attention_block(m, 1, layer * heads)
        reduce.start(1)
        reduce.middle(0)
        saves.start(m.hg, m.hg_out)
        reduce.middle(1)
        expert_weights[1].wait()
        narrow_weights(m.stage, lows[1])
        expert_weights[2].start()
        for b in range(2):
            span_b = block_rows(b)
            m.mid[span_b] = m.h[span_b] + reduce.finish(b)
        tiny_one = Tiny(m.tiny_one)
        tiny_two = Tiny(m.tiny_two)
        tiny_three = Tiny(m.tiny_three)
        tiny_four = Tiny(m.tiny_four)
        route = Route(n, cap, 2, m.route)
        chunks = route.chunks
        fill_forward = forward_rows(m, layer, experts, tiny_one, tiny_two, route)

        def fill(chunk):
            @pl.when(chunk < chunks)
            def _():
                fill_forward(chunk)

            @pl.when(chunk >= chunks)
            def _():
                fill_backward(chunk - chunks, chunk)

        route.begin(fill_forward, fill)
        tiny_two.start(nt(router_of(m, layer, experts), m.normed[...]))
        expert_weights[2].wait()
        narrow_weights(m.stage, lows[2])
        router_gates(m, layer, tiny_two)
        fill_backward = backward_rows(m, route)

        def compute(chunk, rows):
            @pl.when(chunk < chunks)
            def _():
                route.put(chunk, forward_products(m, chunk, rows))

            @pl.when(chunk >= chunks)
            def _():
                route.put(chunk, backward_products(m, chunk - chunks, rows))

        def hook(i):
            @pl.when(i == 2)
            def _():
                set_hot(m, n * cap)

            @pl.when(i == chunks + STAGE_LAGS[3] + 1)
            def _():
                forward_combine(m, route)
                start_shares(m, tiny_three)

        route.run(compute, hook)
        logit_gradient(m, layer, experts, tiny_three)
        backward_tail(
            m,
            layer,
            experts,
            tiny_four,
            route,
            chunks,
            lambda q: route.arrived(0, q),
            saves,
            jnp.zeros((1, HALF), f32),
        )
        gather.wait_sends()
        reduce.wait_sends()
        saves.wait()

    return top_kernel


def attention_back_ins(kept, midg):
    return [
        named.midg_in(midg, vmem_spec),
        named.a_ctx(kept.ctx, vmem_spec),
        named.a_proj(kept.proj, vmem_spec),
        named.a_lse(kept.lse, vmem_spec),
        named.a_r1(kept.r1, vmem_spec),
        named.a_hg(kept.hg, vmem_spec),
        named.a_wqkv(kept.wqkv, vmem_spec),
        named.a_wo(kept.wo, vmem_spec),
        named.a_h(kept.h, vmem_spec),
    ]


def attention_back_scratch(width, heads):
    return attention_scratch + [
        named.pg(pltpu.VMEM((SEQ, 3 * width), bf16)),
        named.dk(pltpu.VMEM((SEQ, width), f32)),
        named.dv(pltpu.VMEM((SEQ, width), f32)),
        named.bias_grad(pltpu.VMEM((heads, HALF, 2 * HALF), f32)),
        named.ag(pltpu.VMEM((SLICES, SEQ, HALF), bf16)),
        named.gather(Gather.scratch),
        named.tiny_zero(Tiny.scratch(8, SEQ)),
    ]


def attention_view(m):
    return types.SimpleNamespace(
        seg_col=m.seg_col,
        seg_row=m.seg_row,
        bias=m.bias,
        part=m.part,
        ctx=m.a_ctx,
        proj=m.a_proj,
        lse=m.a_lse,
        r1=m.a_r1,
        hg=m.a_hg,
        wqkv=m.a_wqkv,
        wo=m.a_wo,
        pg=m.pg,
        dk=m.dk,
        dv=m.dv,
        bias_grad=m.bias_grad,
        ag=m.ag,
        wog=m.wog,
        qkvg=m.qkvg,
    )


def attention_back(m, layer, heads, after_out, after_qkv):
    gather = Gather(m.ag, m.gather)
    reduce = Reduce(m.part, m.reduce)
    tiny = Tiny(m.tiny_zero)
    a = attention_view(m)
    for b in (1, 0):
        gather.start(b, m.midg_in[block_rows(b)].astype(bf16))
    set_attention_tables(m)
    gather.forward(1)
    gather.finish(1)
    gather.forward(0)
    attention_back_block(a, 1, layer * heads)
    reduce.start(1)
    gather.finish(0)
    attention_back_block(a, 0, layer * heads)
    reduce.start(0)
    reduce.middle(1)
    out_gradient(a)
    after_out()
    reduce.middle(0)
    qkv_gradient(a)
    after_qkv()
    m.table[...] = table_gradient(a)
    grad = jnp.concatenate([reduce.finish(0), reduce.finish(1)], axis=0)
    h = m.a_h[...] if m.a_h.shape[1] == HALF else pick_slice(m.a_h[...].astype(f32))
    result = norm_backward(tiny, grad, h, m.a_r1[:, :1], gain_of(m, layer, 0), m.midg_in[...])
    gather.wait_sends()
    reduce.wait_sends()
    return result


def back_program(n, cap, experts, heads, layer):
    def back_next_kernel(m):
        saves = Saves(m.save_sems)
        loads = start_backward_loads(m)
        greet(n, True)
        set_targets(m, layer, cap)
        own = D // n

        def rows_of(e):
            return pl.ds(pl.multiple_of(e * own, 16), own)

        late_qkv = Scatter(n, lambda e: m.qkvg.at[:, rows_of(e)], m.qkv_sums, m.near_a, None, None)
        late_out = Scatter(n, lambda e: m.wog.at[rows_of(e)], m.out_sums, m.near_b, None, None)
        half = n // 2
        value, gain_one = attention_back(
            m,
            layer + 1,
            heads,
            lambda: None,
            lambda: None,
        )
        m.dy[...] = value
        share = max(1, half // 4)

        def hook(i):
            for one in (late_out, late_qkv):

                @pl.when((i >= 2) & (i < 2 + half // share))
                def _(one=one):
                    one.near_start(1 + (i - 2) * share, 1 + (i - 1) * share)

                @pl.when((i >= 4) & (i < 4 + half // share))
                def _(one=one):
                    one.loop(1 + (i - 4) * share, 1 + (i - 3) * share, one.near_sum)

        backward_experts(m, n, cap, layer, experts, loads, saves, gain_one, hook)
        late_out.near_wait_sends()
        late_qkv.near_wait_sends()
        saves.wait()

    return back_next_kernel


class Scatter:
    @staticmethod
    def near_scratch(n, block):
        return [
            pltpu.VMEM((n // 2,) + block, bf16),
            pltpu.SemaphoreType.DMA((n // 2,)),
            pltpu.SemaphoreType.DMA((n // 2,)),
        ]

    @staticmethod
    def far_scratch(n, block):
        return [
            pltpu.VMEM((n // 2,) + block, bf16),
            pltpu.SemaphoreType.DMA((n // 2,)),
            pltpu.SemaphoreType.DMA((n // 2,)),
        ]

    def __init__(self, n, block_of, sums, near_refs, out, far_refs):
        self.n, self.block_of, self.sums, self.out = n, block_of, sums, out
        if near_refs is not None:
            self.near, self.near_send, self.near_recv = near_refs
        if far_refs is not None:
            self.got, self.far_send, self.far_recv = far_refs

    def near_copy(self, k):
        d, t, sib, far, opp = places()
        parity = lax.rem(d, 2)
        src = self.block_of(2 * k + 1 - parity)
        return remote(src, self.near.at[k], self.near_send.at[k], self.near_recv.at[k], (d + 1 - 2 * parity, t))

    def far_copy(self, k, source):
        d, t, sib, far, opp = places()
        return remote(
            self.sums.at[k], self.got.at[source], self.far_send.at[k], self.far_recv.at[source], (2 * k + lax.rem(d, 2), t)
        )

    def spot(self, j):
        d = lax.axis_index("dp")
        return lax.rem(d // 2 + j, self.n // 2)

    def loop(self, first, last, action):
        def one(j, carry):
            action(self.spot(j))
            return carry

        lax.fori_loop(first, last, one, 0)

    def near_start(self, first, last):
        self.loop(first, last, lambda k: self.near_copy(k).start())

    def near_sum(self, k):
        d = lax.axis_index("dp")
        self.near_copy(k).wait_recv()
        mine = self.block_of(2 * k + lax.rem(d, 2))[...].astype(f32)
        self.sums[k] = (mine + self.near[k].astype(f32)).astype(bf16)

    def near_sums(self):
        self.loop(1, self.n // 2 + 1, self.near_sum)

    def near_wait_sends(self):
        self.loop(0, self.n // 2, lambda k: self.near_copy(k).wait_send())

    def far_start(self):
        d = lax.axis_index("dp")
        self.loop(1, self.n // 2, lambda k: self.far_copy(k, d // 2).start())

    def both(self, ahead):
        d = lax.axis_index("dp")
        total = self.n // 2

        def one(j, carry):
            k = self.spot(j)

            @pl.when(j + ahead <= total)
            def _():
                self.near_copy(self.spot(j + ahead)).start()

            self.near_sum(k)

            @pl.when(k != d // 2)
            def _():
                self.far_copy(k, d // 2).start()

            return carry

        lax.fori_loop(1, total + 1, one, 0)

    def finish(self):
        d = lax.axis_index("dp")
        total = self.sums[d // 2].astype(f32)

        def one(j, carry):
            k = self.spot(j)
            self.far_copy(k, k).wait_recv()
            return carry + self.got[k].astype(f32)

        self.out[...] = lax.fori_loop(1, self.n // 2, one, total)
        self.loop(1, self.n // 2, lambda k: self.far_copy(k, d // 2).wait_send())


def final_program(n, experts, heads):
    own = D // n

    def final_kernel(m):
        d, t, sib, far, opp = places()
        saves = Saves(m.save_sems)

        def rows_of(e):
            return pl.ds(pl.multiple_of(e * own, 16), own)

        late_qkv = Scatter(n, None, m.qkv_sums_next, None, m.qkv_grad.at[1], m.far_a)
        late_out = Scatter(n, None, m.out_sums_next, None, m.out_grad.at[1], m.far_b)
        early_qkv = Scatter(n, lambda e: m.qkvg.at[:, rows_of(e)], m.qkv_sums, m.near_c, m.qkv_grad.at[0], m.far_c)
        early_out = Scatter(n, lambda e: m.wog.at[rows_of(e)], m.out_sums, m.near_d, m.out_grad.at[0], m.far_d)
        half = n // 2
        output = Gather(m.output_buf, m.output_gather)
        dx_all = Gather(m.dx_buf, m.dx_gather)
        greet(n, True)
        late_out.far_start()
        late_qkv.far_start()

        def after_out():
            early_out.near_start(1, half + 1)

        def after_qkv():
            early_qkv.near_start(1, 3)
            early_out.both(half)
            for b in range(2):
                output.start(b, m.y_last[block_rows(b)].astype(bf16))

        dx, gain_one = attention_back(m, 0, heads, after_out, after_qkv)
        for b in range(2):
            dx_all.start(b, dx[block_rows(b)].astype(bf16))
        place = lax.broadcasted_iota(jnp.int32, (8, HALF), 0)
        m.pack[0:8] = jnp.where(
            place == 0,
            gain_one,
            jnp.where(
                place == 1,
                m.gain_rows_0[0:1],
                jnp.where(place == 2, m.gain_rows_0[1:2], jnp.where(place == 3, m.gain_rows_1[0:1], 0.0)),
            ),
        )
        m.pack[8:16] = jnp.concatenate([m.table[...], m.table_next[...]], axis=1)
        m.pack[16 : 16 + experts] = m.router_g_0[...]
        m.pack[16 + experts : 16 + 2 * experts] = m.router_g_1[...]

        def pack_copy(j, source, target):
            return remote(m.pack, m.packs.at[source], m.pack_send.at[j], m.pack_recv.at[source], (target, t))

        def spread(j, carry):
            pack_copy(j, d, lax.rem(d + j, n)).start()
            return carry

        lax.fori_loop(1, n, spread, 0)
        early_qkv.both(2)
        for b in range(2):
            output.forward(b)
        for b in range(2):
            dx_all.forward(b)
        m.packs[d] = m.pack[...]

        def collect(j, carry):
            source = lax.rem(d + j, n)
            pack_copy(j, source, source).wait_recv()
            return carry

        lax.fori_loop(1, n, collect, 0)

        def add(i, carry):
            return carry + m.packs[i]

        m.small_out[t] = lax.fori_loop(1, n, add, m.packs[0])

        def all_copies():
            return [
                remote(m.small_out.at[t], m.small_out.at[t], m.all_send.at[i], m.all_recv.at[i], (d, peer))
                for i, peer in enumerate((sib, far, opp))
            ]

        for copy in all_copies():
            copy.start()
        for gather, out in ((output, m.output), (dx_all, m.dx_full)):
            for b in range(2):
                gather.finish(b)
            for q in range(SLICES):
                saves.start(gather.buf.at[q], out.at[:, pl.ds(q * HALF, HALF)])
        for one in (late_out, late_qkv, early_out, early_qkv):
            one.finish()
        early_out.near_wait_sends()
        early_qkv.near_wait_sends()

        def sent(j, carry):
            pack_copy(j, d, lax.rem(d + j, n)).wait_send()
            return carry

        lax.fori_loop(1, n, sent, 0)
        for copy in all_copies():
            copy.wait()
        output.wait_sends()
        dx_all.wait_sends()
        saves.wait()

    return final_kernel


def widen_kernel(*refs):
    ins, outs = refs[: 3 * LAYERS + 4], refs[3 * LAYERS + 4 :]
    for i in range(3):
        for layer in range(LAYERS):
            outs[i][layer, 0] = ins[3 * layer + i][...].astype(f32)
    for i in range(4):
        outs[3 + i][...] = ins[3 * LAYERS + i][...].astype(outs[3 + i].dtype)


def widen(grads, others):
    hidden = grads[0][0].shape[0]
    steps = 4
    tile = hidden // steps
    specs = []
    shapes = []
    for one in others:
        dim = one.ndim - 2
        block = one.shape[:dim] + (one.shape[dim] // steps,) + one.shape[dim + 1 :]
        specs.append(pl.BlockSpec(block, lambda i, dim=dim: (0,) * dim + (i, 0)))
        shapes.append(one.shape)
    return pl.pallas_call(
        widen_kernel,
        grid=(steps,),
        out_shape=[shaped((LAYERS, 1, hidden, D), f32)] * 3
        + [shaped(shapes[0], bf16)]
        + [shaped(shape, f32) for shape in shapes[1:]],
        in_specs=[pl.BlockSpec((tile, D), lambda i: (i, 0))] * (3 * LAYERS) + specs,
        out_specs=[pl.BlockSpec((LAYERS, 1, tile, D), lambda i: (0, 0, i, 0))] * 3 + specs,
        compiler_params=pltpu.CompilerParams(vmem_limit_bytes=vmem_bytes),
    )(*[one for layer in grads for one in layer], *others)


def local(tokens, cotangent, w_qkv, w_out, router, gains, rel_table, w_gate, w_up, w_down, routes, slots, segments):
    n = lax.axis_size("dp")
    own = D // n
    experts = router.shape[2]
    heads = rel_table.shape[2]
    width = w_qkv.shape[3]
    hidden = w_down.shape[2]
    cap = 3 * SEQ // n
    rows = 2 * LAYERS + LAYERS * experts + LAYERS * heads
    table_rows = rel_table.astype(bf16).transpose(0, 2, 1).reshape(LAYERS * heads, BUCKETS // n)
    small = jnp.concatenate(
        [
            gains.astype(bf16).reshape(2 * LAYERS, own),
            router.astype(bf16).transpose(0, 2, 1).reshape(LAYERS * experts, own),
            jnp.pad(table_rows, ((0, 0), (0, own - BUCKETS // n))),
        ]
    )
    small = jnp.pad(small, ((0, -rows % 16), (0, 0)))
    rows = small.shape[0]
    gate_t = w_gate.transpose(0, 1, 3, 2)
    up_t = w_up.transpose(0, 1, 3, 2)
    routes_row = routes.transpose(0, 2, 1)
    slots_row = slots.transpose(0, 2, 1)
    seg_row = segments.reshape(1, SEQ)
    index_ins = [
        named.routes_row(routes_row, vmem_spec),
        named.slots_row(slots_row, vmem_spec),
        named.seg_row(seg_row, vmem_spec),
    ]
    weight_ins = [named.gate_f(gate_t, any_spec), named.up_f(up_t, any_spec), named.down_f(w_down, any_spec)]
    attention_weights = [
        named.wqkv(pltpu.VMEM((3, D, width), bf16)),
        named.wo(pltpu.VMEM((D, width), bf16)),
        named.hg(pltpu.VMEM((SLICES, SEQ, HALF), bf16)),
    ]
    pieces = 5 + 2 * (LAYERS - 1)
    first = call(
        first_program(n, cap, experts, heads),
        [named.tok(tokens, vmem_spec), named.qkv(w_qkv, vmem_spec), named.out(w_out, vmem_spec), named.small(small, vmem_spec)]
        + index_ins
        + weight_ins,
        [
            named.wide((SLICES, rows, HALF), bf16, vmem_spec),
            named.tab((8, LANES), f32, vmem_spec),
            named.wqkv_out((3, D, width), bf16, any_spec),
            named.wo_out((D, width), bf16, any_spec),
            named.wqkv_next((3, D, width), bf16, any_spec),
            named.wo_next((D, width), bf16, any_spec),
            named.hg_out((SLICES, SEQ, HALF), bf16, any_spec),
        ]
        + attention_outs(width)
        + forward_outs(n, cap, hidden),
        attention_weights
        + attention_scratch
        + [
            named.small_all(pltpu.VMEM((n, rows, own), bf16)),
            named.qkv_low(pltpu.VMEM((LAYERS, 3, own, width), bf16)),
            named.out_low(pltpu.VMEM((LAYERS, own, width), bf16)),
            named.piece_send(pltpu.SemaphoreType.DMA((pieces, 2, n // 2))),
            named.piece_recv(pltpu.SemaphoreType.DMA((pieces, 2, n // 2))),
        ]
        + forward_scratch(n, cap, hidden, experts),
        0,
    )
    wide_ins = [named.wide(first.wide, vmem_spec), named.tab(first.tab, vmem_spec)]
    chunks, route_rows = Route.shape(n, cap)
    chunk_rows = pltpu.VMEM((chunks, route_rows, hidden), bf16)
    top = call(
        top_program(n, cap, experts, heads, 1),
        [
            named.h(first.y, vmem_spec),
            named.cot(cotangent, vmem_spec),
            named.wqkv_in(first.wqkv_next, any_spec),
            named.wo_in(first.wo_next, any_spec),
        ]
        + wide_ins
        + index_ins
        + weight_ins,
        [named.hg_out((SLICES, SEQ, HALF), bf16, any_spec), named.y((SEQ, HALF), f32, vmem_spec)]
        + attention_outs(width)
        + backward_outs(n, cap, hidden, experts),
        attention_weights
        + attention_scratch
        + [
            named.gather(Gather.scratch),
            named.tiny_zero(Tiny.scratch(8, SEQ)),
            named.tiny_one(Tiny.scratch(8, SEQ)),
            named.tiny_two(Tiny.scratch(experts, SEQ)),
            named.tiny_three(Tiny.scratch(8, SEQ)),
            named.tiny_four(Tiny.scratch(8, SEQ)),
            named.weight_sems(pltpu.SemaphoreType.DMA((2,))),
            named.load_sems(pltpu.SemaphoreType.DMA((3,))),
            named.save_sems(pltpu.SemaphoreType.DMA((16,))),
            named.stage(pltpu.VMEM((hidden, D), f32)),
            named.wg(pltpu.VMEM((hidden, D), bf16)),
            named.wu(pltpu.VMEM((hidden, D), bf16)),
            named.wd(pltpu.VMEM((hidden, D), bf16)),
            named.inner(chunk_rows),
            named.act(chunk_rows),
            named.slope(chunk_rows),
            named.gpg(chunk_rows),
            named.upg(chunk_rows),
            named.mid(pltpu.VMEM((SEQ, HALF), f32)),
            named.normed(pltpu.VMEM((SEQ, HALF), bf16)),
            named.r2(pltpu.VMEM((SEQ, LANES), f32)),
            named.gates(pltpu.VMEM((SEQ, LANES), f32)),
            named.picked(pltpu.VMEM((2, SEQ, HALF), bf16)),
            named.dy(pltpu.VMEM((SEQ, HALF), f32)),
            named.pgs(pltpu.VMEM((2 * SEQ, HALF), bf16)),
            named.hot(pltpu.VMEM((2, SEQ, n * cap), bf16)),
            named.logit_g(pltpu.VMEM((experts, SEQ), f32)),
            named.targ_row(pltpu.VMEM((2, SEQ), jnp.int32)),
            named.targ_col(pltpu.VMEM((SEQ, LANES), jnp.int32)),
            named.route(Route.scratch(n, cap, 2)),
        ],
        1,
    )

    def kept_of(state, wqkv, wo, h):
        return types.SimpleNamespace(
            ctx=state.ctx, proj=state.proj, lse=state.lse, r1=state.r1, hg=state.hg_out, wqkv=wqkv, wo=wo, h=h
        )

    gradient_scratch = [named.wog(pltpu.VMEM((D, width), bf16)), named.qkvg(pltpu.VMEM((3, D, width), bf16))]
    fourth = call(
        back_program(n, cap, experts, heads, 0),
        wide_ins
        + index_ins
        + attention_back_ins(kept_of(top, first.wqkv_next, first.wo_next, first.y), top.midg)
        + backward_ins(first),
        backward_outs(n, cap, hidden, experts)
        + [
            named.qkv_sums((n // 2, 3, own, width), bf16, vmem_spec),
            named.out_sums((n // 2, own, width), bf16, vmem_spec),
            named.table((8, LANES), f32, vmem_spec),
        ],
        gradient_scratch
        + [
            named.near_a(Scatter.near_scratch(n, (3, own, width))),
            named.near_b(Scatter.near_scratch(n, (own, width))),
        ]
        + attention_back_scratch(width, heads)
        + backward_scratch(n, cap, hidden, experts),
        3,
    )
    pack_rows = 16 + LAYERS * experts
    big, less = (3, own, width), (own, width)
    scatter_scratch = [
        named.far_a(Scatter.far_scratch(n, big)),
        named.far_b(Scatter.far_scratch(n, less)),
        named.near_c(Scatter.near_scratch(n, big)),
        named.near_d(Scatter.near_scratch(n, less)),
        named.far_c(Scatter.far_scratch(n, big)),
        named.far_d(Scatter.far_scratch(n, less)),
        named.qkv_sums(pltpu.VMEM((n // 2,) + big, bf16)),
        named.out_sums(pltpu.VMEM((n // 2,) + less, bf16)),
    ]
    final = call(
        final_program(n, experts, heads),
        wide_ins
        + index_ins[2:]
        + attention_back_ins(kept_of(first, first.wqkv_out, first.wo_out, tokens), fourth.midg)
        + [
            named.qkv_sums_next(fourth.qkv_sums, vmem_spec),
            named.out_sums_next(fourth.out_sums, vmem_spec),
            named.y_last(top.y, vmem_spec),
            named.gain_rows_0(fourth.gain_rows, vmem_spec),
            named.gain_rows_1(top.gain_rows, vmem_spec),
            named.router_g_0(fourth.router_g, vmem_spec),
            named.router_g_1(top.router_g, vmem_spec),
            named.table_next(fourth.table, vmem_spec),
        ],
        [
            named.output((SEQ, D), bf16, any_spec),
            named.dx_full((SEQ, D), bf16, any_spec),
            named.qkv_grad((LAYERS, 3, own, width), f32, vmem_spec),
            named.out_grad((LAYERS, own, width), f32, vmem_spec),
            named.small_out((SLICES, pack_rows, HALF), f32, vmem_spec),
        ],
        gradient_scratch
        + attention_back_scratch(width, heads)
        + scatter_scratch
        + [
            named.table(pltpu.VMEM((8, LANES), f32)),
            named.output_buf(pltpu.VMEM((SLICES, SEQ, HALF), bf16)),
            named.output_gather(Gather.scratch),
            named.dx_buf(pltpu.VMEM((SLICES, SEQ, HALF), bf16)),
            named.dx_gather(Gather.scratch),
            named.pack(pltpu.VMEM((pack_rows, HALF), f32)),
            named.packs(pltpu.VMEM((n, pack_rows, HALF), f32)),
            named.pack_send(pltpu.SemaphoreType.DMA((n,))),
            named.pack_recv(pltpu.SemaphoreType.DMA((n,))),
            named.all_send(pltpu.SemaphoreType.DMA((3,))),
            named.all_recv(pltpu.SemaphoreType.DMA((3,))),
            named.save_sems(pltpu.SemaphoreType.DMA((16,))),
        ],
        4,
    )
    grads = [[one.wg_grad, one.wu_grad, one.wd_grad] for one in (fourth, top)]
    gate_g, up_g, down_g, output, dx_wide, qkv_grad, out_grad = widen(
        grads, [final.output, final.dx_full, final.qkv_grad, final.out_grad]
    )
    d, t = lax.axis_index("dp"), lax.axis_index("tensor")
    small_sum = final.small_out

    def rows_wide(start, count):
        wide = small_sum[:, start : start + count].transpose(1, 0, 2).reshape(count, D)
        return lax.dynamic_slice_in_dim(wide, d * own, own, 1)

    gains_grad = rows_wide(0, 2 * LAYERS).reshape(LAYERS, 2, own)
    router_grad = rows_wide(16, LAYERS * experts).reshape(LAYERS, experts, own).transpose(0, 2, 1)
    table_all = lax.dynamic_slice_in_dim(small_sum, t, 1, 0)[0, 8 : 8 + heads].reshape(heads, LAYERS, LANES)
    table_grad = lax.dynamic_slice_in_dim(table_all, d * (BUCKETS // n), BUCKETS // n, 2).transpose(1, 2, 0)
    return (
        output,
        dx_wide,
        qkv_grad,
        out_grad,
        router_grad,
        gains_grad,
        table_grad,
        gate_g.transpose(0, 1, 3, 2),
        up_g.transpose(0, 1, 3, 2),
        down_g,
    )


def solution(mesh):
    placed = (
        P("dp", None),
        P("dp", None),
        P(None, None, "dp", "tensor"),
        P(None, "dp", "tensor"),
        P(None, "dp", None),
        P(None, None, "dp"),
        P(None, "dp", "tensor"),
        P(None, "dp", None, "tensor"),
        P(None, "dp", None, "tensor"),
        P(None, "dp", "tensor", None),
        P(None, "dp", None),
        P(None, "dp", None),
        P("dp"),
    )
    return jax.shard_map(
        local,
        mesh=mesh,
        in_specs=placed,
        out_specs=(P("dp", None), P("dp", None)) + placed[2:10],
        check_vma=False,
    )
```

```python
import types

import jax
import jax.numpy as jnp
from jax import lax
from jax.experimental import pallas as pl
from jax.experimental.pallas import tpu as pltpu
from jax.sharding import PartitionSpec as P

D = 1024
HDIM = 64
SEQ = 512
LAYERS = 2
BUCKETS = 32
HALF = 256
SLICES = 4
WINDOW_CHUNKS = 2
STAGE_LAGS = (1, 2, 3, 4)
LANES = 128
WINDOW = 768

eps_norm = 1e-06
rise_points = (12, 16, 23, 32, 46, 64, 91)
masked_score = -1e30
vmem_bytes = 63 * 1024 * 1024
f32 = jnp.float32
bf16 = jnp.bfloat16
MESH = pl.DeviceIdType.MESH
nn_dims = (((1,), (0,)), ((), ()))
nt_dims = (((1,), (1,)), ((), ()))
tn_dims = (((0,), (0,)), ((), ()))
vmem_spec = pl.BlockSpec(memory_space=pltpu.VMEM)
any_spec = pl.BlockSpec(memory_space=pl.ANY)
late_spec = pl.BlockSpec(memory_space=pl.ANY)
saved_spec = pl.BlockSpec(memory_space=pl.ANY)


def nn(a, b):
    return lax.dot_general(a, b, nn_dims, preferred_element_type=f32)


def nt(a, b):
    return lax.dot_general(a, b, nt_dims, preferred_element_type=f32)


def tn(a, b):
    return lax.dot_general(a, b, tn_dims, preferred_element_type=f32)


def shaped(shape, kind):
    return jax.ShapeDtypeStruct(shape, kind)


def bucket_index(offset):
    upward = jnp.where(offset > 0, BUCKETS // 2, 0)
    distance = jnp.abs(offset)
    far_part = 8 + sum(((distance >= rise_point).astype(jnp.int32) for rise_point in rise_points))
    return upward + jnp.where(distance < 8, distance, far_part)


def toeplitz_bias(row):
    tile = jnp.broadcast_to(row, (HALF, WINDOW))
    rolled = pltpu.roll(tile, WINDOW - HALF + 1, 1, stride=1, stride_axis=0)
    return rolled[:, : 2 * HALF]


def diagonal_sums(grad):
    rows = jnp.concatenate([grad, jnp.zeros((HALF, WINDOW - 2 * HALF), f32)], axis=1)
    count = HALF
    while count > 8:
        count //= 2
        rows = rows[:count] + pltpu.roll(rows[count:], WINDOW - count, 1)
    total = jnp.zeros((8, WINDOW), f32)
    place = lax.broadcasted_iota(jnp.int32, (8, WINDOW), 0)
    for i in range(8):
        moved = pltpu.roll(rows, (HALF - 1 - i) % WINDOW, 1)
        total = total + jnp.where(place == i, moved, 0.0)
    return total


def half_lanes(shape, which):
    lane = lax.broadcasted_iota(jnp.int32, shape, 1)
    return (lane < HDIM) if which == 0 else (lane >= HDIM)


def allowed_tile(seg_col, seg_row):
    i = lax.broadcasted_iota(jnp.int32, (HALF, HALF), 0)
    j = lax.broadcasted_iota(jnp.int32, (HALF, HALF), 1)
    return (j <= i) | ((seg_col == seg_row) & (seg_col > 0))


def masked_scores(query, keys, bias, allowed, block):
    raw = nt(query, keys)
    if block == 0:
        return jnp.where(allowed, raw + bias[:, HALF:], masked_score)
    left = raw[:, :HALF] + bias[:, :HALF]
    right = jnp.where(allowed, raw[:, HALF:] + bias[:, HALF:], masked_score)
    return jnp.concatenate([left, right], axis=1)


def bias_rows(table):
    place = lax.broadcasted_iota(jnp.int32, (BUCKETS, WINDOW), 1) - (SEQ - 1)
    hot = (bucket_index(place) == lax.broadcasted_iota(jnp.int32, (BUCKETS, WINDOW), 0)).astype(bf16)
    return nn(table, hot)


def block_rows(block):
    return slice(block * HALF, (block + 1) * HALF)


def attend_block(m, block, first_head):
    width = m.ctx.shape[1]
    rows = block_rows(block)
    count = (block + 1) * HALF
    lane = lax.broadcasted_iota(jnp.int32, (HALF, LANES), 1)
    allowed = allowed_tile(m.seg_col[rows, :1], m.seg_row[:, rows])
    lse = jnp.zeros((HALF, LANES), f32)
    for pair in range(width // LANES):
        cols = slice(pair * LANES, (pair + 1) * LANES)
        q2 = m.proj[rows, cols]
        k2 = m.proj[:count, width + pair * LANES : width + (pair + 1) * LANES]
        v2 = m.proj[:count, 2 * width + pair * LANES : 2 * width + (pair + 1) * LANES]
        outs = []
        for which in range(2):
            head = 2 * pair + which
            scaled = q2 * jnp.asarray(HDIM**-0.5, bf16)
            qm = jnp.where(half_lanes(q2.shape, which), scaled, jnp.zeros_like(q2))
            bias = toeplitz_bias(m.bias[first_head + head : first_head + head + 1])
            scores = masked_scores(qm, k2, bias, allowed, block)
            top = jnp.max(scores, axis=1, keepdims=True)
            powers = jnp.exp(scores - top)
            total = jnp.sum(powers, axis=1, keepdims=True)
            probs = (powers * (1.0 / total)).astype(bf16)
            outs.append(nn(probs, v2))
            lse = jnp.where(lane == head, top + jnp.log(total), lse)
        m.ctx[rows, cols] = jnp.where(half_lanes(outs[0].shape, 0), outs[0], outs[1]).astype(bf16)
    m.lse[rows, :] = lse


def wide_rows(ref, rows):
    return jnp.concatenate([ref[q, rows] for q in range(SLICES)], axis=1)


def project(m, block, c):
    width = m.ctx.shape[1]
    rows = block_rows(block)
    m.proj[rows, c * width : (c + 1) * width] = (
        nn(wide_rows(m.hg, rows), m.wqkv[c]) * m.r1[rows, :1]
    ).astype(bf16)


def project_out(m, block):
    rows = block_rows(block)
    for q in range(SLICES):
        m.part[q, rows] = nt(m.ctx[rows], m.wo[q * HALF : (q + 1) * HALF, :]).astype(bf16)


def attention_block(m, block, first_head, between):
    for c in range(3):
        project(m, block, c)
    between()
    attend_block(m, block, first_head)
    project_out(m, block)


def prob_cols(block):
    return slice(0, HALF) if block == 0 else slice(HALF, 3 * HALF)


def attention_probs(m, block, first_head):
    width = m.ctx.shape[1]
    rows = block_rows(block)
    count = (block + 1) * HALF
    allowed = allowed_tile(m.seg_col[rows, :1], m.seg_row[:, rows])
    scale = jnp.asarray(HDIM**-0.5, bf16)
    for head in range(width // HDIM):
        pair, which = head // 2, head % 2
        q2 = m.proj[rows, pair * LANES : (pair + 1) * LANES]
        k2 = m.proj[:count, width + pair * LANES : width + (pair + 1) * LANES]
        qm = jnp.where(half_lanes(q2.shape, which), q2 * scale, jnp.zeros_like(q2))
        bias = toeplitz_bias(m.bias[first_head + head : first_head + head + 1])
        scores = masked_scores(qm, k2, bias, allowed, block)
        m.probs[head, :, prob_cols(block)] = jnp.exp(scores - m.lse[rows, head : head + 1])


def attention_back_block(m, block, between):
    width = m.ctx.shape[1]
    rows = block_rows(block)
    count = (block + 1) * HALF
    dctx = nn(wide_rows(m.ag, rows), m.wo[...]).astype(bf16)
    scale = jnp.asarray(HDIM**-0.5, bf16)
    for pair in range(width // LANES):
        if pair == 1:
            between()
        cols = slice(pair * LANES, (pair + 1) * LANES)
        q2 = m.proj[rows, cols]
        k2 = m.proj[:count, width + pair * LANES : width + (pair + 1) * LANES]
        v2 = m.proj[:count, 2 * width + pair * LANES : 2 * width + (pair + 1) * LANES]
        g2 = dctx[:, cols]
        outs = []
        dk = None
        dv = None
        for which in range(2):
            head = 2 * pair + which
            mine = half_lanes(q2.shape, which)
            qm = jnp.where(mine, q2 * scale, jnp.zeros_like(q2))
            gm = jnp.where(mine, g2, jnp.zeros_like(g2))
            probs = m.probs[head, :, prob_cols(block)]
            prob_grad = nt(gm, v2).astype(bf16).astype(f32)
            inner = jnp.sum(probs * prob_grad, axis=1, keepdims=True)
            grad_low = (probs * (prob_grad - inner)).astype(bf16)
            dv_one = tn(probs.astype(bf16), gm)
            dk_one = tn(grad_low, qm)
            dv = dv_one if dv is None else dv + dv_one
            dk = dk_one if dk is None else dk + dk_one
            outs.append(nn(grad_low, k2))
            wide = grad_low.astype(f32)
            if block == 1:
                m.bias_grad[head] = wide
            else:
                m.bias_grad[head, :, HALF:] = m.bias_grad[head, :, HALF:] + wide
        dq = jnp.where(half_lanes(outs[0].shape, 0), outs[0], outs[1]) * HDIM**-0.5
        if block == 1:
            m.dk[:, cols] = dk
            m.dv[:, cols] = dv
        else:
            m.dk[:HALF, cols] = m.dk[:HALF, cols] + dk
            m.dv[:HALF, cols] = m.dv[:HALF, cols] + dv
        m.pg[rows, cols] = dq.astype(bf16)
        m.pg[rows, width + pair * LANES : width + (pair + 1) * LANES] = m.dk[rows, cols].astype(bf16)
        m.pg[rows, 2 * width + pair * LANES : 2 * width + (pair + 1) * LANES] = m.dv[rows, cols].astype(bf16)
    dots = None
    for q in range(SLICES):
        total = None
        for c in range(3):
            one = nt(m.pg[rows, c * width : (c + 1) * width], m.wqkv[c, q * HALF : (q + 1) * HALF, :])
            total = one if total is None else total + one
        m.part[q, rows] = total.astype(bf16)
        product = jnp.sum(total * m.hg[q, rows].astype(f32), axis=1, keepdims=True)
        dots = product if dots is None else dots + product
    return dots


def table_gradient(m):
    place = lax.broadcasted_iota(jnp.int32, (8, WINDOW), 0)
    diag_all = jnp.zeros((8, WINDOW), f32)
    for head in range(m.bias_grad.shape[0]):
        sums = jnp.sum(diagonal_sums(m.bias_grad[head]), axis=0, keepdims=True)
        diag_all = jnp.where(place == head, sums, diag_all)
    spot = lax.broadcasted_iota(jnp.int32, (WINDOW, LANES), 0) - (SEQ - 1)
    hot = (bucket_index(spot) == lax.broadcasted_iota(jnp.int32, (WINDOW, LANES), 1)).astype(f32)
    return lax.dot_general(
        diag_all, hot, nn_dims, precision=lax.Precision.HIGHEST, preferred_element_type=f32
    )


def out_gradient(m):
    for q in range(SLICES):
        m.wog[q * HALF : (q + 1) * HALF] = tn(m.ag[q], m.ctx[...]).astype(bf16)


def qkv_gradient(m):
    width = m.ctx.shape[1]
    for q in range(SLICES):
        normed = (m.hg[q].astype(f32) * m.r1[:, :1]).astype(bf16)
        for c in range(3):
            m.qkvg[c, q * HALF : (q + 1) * HALF] = tn(normed, m.pg[:, c * width : (c + 1) * width]).astype(bf16)


def places():
    d = lax.axis_index("dp")
    t = lax.axis_index("tensor")
    sib = t + 1 - 2 * lax.rem(t, 2)
    far = lax.rem(t + 2, SLICES)
    opp = SLICES - 1 - t
    return d, t, sib, far, opp


def remote(src, dst, send, recv, device):
    return pltpu.make_async_remote_copy(
        src_ref=src, dst_ref=dst, send_sem=send, recv_sem=recv, device_id=device, device_id_type=MESH
    )


def greet(n, with_dp):
    d, t, sib, far, opp = places()
    barrier = pltpu.get_barrier_semaphore()
    for peer in (sib, far, opp):
        pl.semaphore_signal(barrier, inc=1, device_id=(d, peer), device_id_type=MESH)
    if with_dp:

        def hello(j, carry):
            pl.semaphore_signal(barrier, inc=1, device_id=(lax.rem(d + j, n), t), device_id_type=MESH)
            return carry

        lax.fori_loop(1, n, hello, 0)
    pl.semaphore_wait(barrier, 3 + (n - 1 if with_dp else 0))


class Tiny:
    scratch = lambda rows, cols: [
        pltpu.VMEM((SLICES, rows, cols), f32),
        pltpu.SemaphoreType.DMA((3,)),
        pltpu.SemaphoreType.DMA((3,)),
    ]

    def __init__(self, refs):
        self.buf, self.send, self.recv = refs

    def copies(self):
        d, t, sib, far, opp = places()
        return [
            remote(self.buf.at[t], self.buf.at[t], self.send.at[i], self.recv.at[i], (d, peer))
            for i, peer in enumerate((sib, far, opp))
        ]

    def start(self, tile):
        d, t, sib, far, opp = places()
        self.buf[t] = tile
        for copy in self.copies():
            copy.start()

    def finish(self):
        for copy in self.copies():
            copy.wait()

    def total(self):
        self.finish()
        return (self.buf[0] + self.buf[1]) + (self.buf[2] + self.buf[3])


class Gather:
    scratch = [pltpu.SemaphoreType.DMA((2, 3)), pltpu.SemaphoreType.DMA((2, 3))]

    def __init__(self, buf, refs):
        self.buf = buf
        self.send, self.recv = refs

    def copies(self, b):
        d, t, sib, far, opp = places()
        rows = pl.ds(b * HALF, HALF)
        mine, others = self.buf.at[t, rows], self.buf.at[far, rows]
        return [
            lambda: remote(mine, mine, self.send.at[b, 0], self.recv.at[b, 0], (d, far)),
            lambda: remote(mine, mine, self.send.at[b, 1], self.recv.at[b, 1], (d, sib)),
            lambda: remote(others, others, self.send.at[b, 2], self.recv.at[b, 2], (d, sib)),
        ]

    def start(self, b, tile):
        d, t, sib, far, opp = places()
        self.buf[t, pl.ds(b * HALF, HALF)] = tile
        far_copy, near_copy, pass_copy = self.copies(b)
        far_copy().start()
        near_copy().start()

    def forward(self, b):
        far_copy, near_copy, pass_copy = self.copies(b)
        far_copy().wait_recv()
        pass_copy().start()

    def finish(self, b):
        far_copy, near_copy, pass_copy = self.copies(b)
        near_copy().wait_recv()
        pass_copy().wait_recv()

    def wait_sends(self):
        for b in range(2):
            for copy in self.copies(b):
                copy().wait_send()


class Reduce:
    scratch = [
        pltpu.VMEM((2, SEQ, HALF), bf16),
        pltpu.VMEM((2, SEQ, HALF), bf16),
        pltpu.SemaphoreType.DMA((2, 3)),
        pltpu.SemaphoreType.DMA((2, 3)),
    ]

    def __init__(self, part, refs):
        self.part = part
        self.near, self.across, self.send, self.recv = refs

    def copies(self, b):
        d, t, sib, far, opp = places()
        rows = pl.ds(b * HALF, HALF)

        def one(i, src, dst, peer):
            return lambda: remote(src, dst, self.send.at[b, i], self.recv.at[b, i], (d, peer))

        return [
            one(0, self.part.at[opp, rows], self.near.at[1, rows], sib),
            one(1, self.part.at[sib, rows], self.near.at[0, rows], sib),
            one(2, self.across.at[0, rows], self.across.at[1, rows], far),
        ]

    def start(self, b):
        first, second, third = self.copies(b)
        first().start()
        second().start()

    def middle(self, b):
        d, t, sib, far, opp = places()
        rows = pl.ds(b * HALF, HALF)
        first, second, third = self.copies(b)
        first().wait_recv()
        self.across[0, rows] = (self.part[far, rows].astype(f32) + self.near[1, rows].astype(f32)).astype(bf16)
        third().start()

    def finish(self, b):
        d, t, sib, far, opp = places()
        rows = pl.ds(b * HALF, HALF)
        first, second, third = self.copies(b)
        second().wait_recv()
        mine = self.part[t, rows].astype(f32) + self.near[0, rows].astype(f32)
        third().wait_recv()
        return mine + self.across[1, rows].astype(f32)

    def wait_sends(self):
        for b in range(2):
            for copy in self.copies(b):
                copy().wait_send()


class Saves:
    def __init__(self, sems):
        self.sems, self.copies = sems, []

    def start(self, src, dst, span=None):
        place = len(self.copies)

        def copy():
            if span is None:
                return pltpu.make_async_copy(src, dst, self.sems.at[place])
            return pltpu.make_async_copy(src.at[span], dst.at[span], self.sems.at[place])

        copy().start()
        self.copies.append(copy)

    def wait(self):
        for copy in self.copies:
            copy().wait()


def to_row(col):
    return jnp.transpose(jnp.broadcast_to(col, (col.shape[0], LANES)))[:8]


def to_cols(rows8):
    return jnp.transpose(jnp.concatenate([rows8] * (LANES // 8), axis=0))


def int_cols(rows):
    whole = jnp.concatenate([rows.astype(f32)] * (8 // rows.shape[0]), axis=0)
    return to_cols(whole).astype(jnp.int32)


def pick_slice(wide):
    t = lax.axis_index("tensor")
    out = wide[:, :HALF]
    for q in range(1, SLICES):
        out = jnp.where(t == q, wide[:, q * HALF : (q + 1) * HALF], out)
    return out


def hot_columns(targ, k, count):
    return (targ[:, k : k + 1] == lax.broadcasted_iota(jnp.int32, (SEQ, count), 1)).astype(f32).astype(bf16)


class Route:
    @staticmethod
    def piece(cap):
        return 32 if cap % 32 == 0 else 16

    @staticmethod
    def shape(n, cap):
        piece = Route.piece(cap)
        return cap // piece, n * piece

    @staticmethod
    def slots(chunks, rounds):
        return chunks if rounds == 1 else max(chunks, STAGE_LAGS[3] + 1)

    @staticmethod
    def scratch(n, cap, rounds):
        chunks, rows = Route.shape(n, cap)
        slots = Route.slots(chunks, rounds)
        total = chunks * rounds
        return [
            pltpu.VMEM((total, rows, HALF), bf16),
            pltpu.VMEM((total, SLICES, rows, HALF), bf16),
            pltpu.VMEM((slots, SLICES, rows, HALF), bf16),
            pltpu.VMEM((slots, 2, rows, HALF), bf16),
            pltpu.VMEM((slots, rows, HALF), bf16),
            pltpu.VMEM((slots, rows, HALF), bf16),
            pltpu.VMEM((slots, rows, HALF), bf16),
            pltpu.VMEM((total, rows, HALF), bf16),
            pltpu.SemaphoreType.DMA((total, n)),
            pltpu.SemaphoreType.DMA((total, n)),
            pltpu.SemaphoreType.DMA((3, total)),
            pltpu.SemaphoreType.DMA((3, total)),
            pltpu.SemaphoreType.DMA((3, total)),
            pltpu.SemaphoreType.DMA((3, total)),
            pltpu.SemaphoreType.DMA((total, n)),
            pltpu.SemaphoreType.DMA((total, n)),
        ]

    def __init__(self, n, cap, rounds, refs):
        self.n = n
        self.size = Route.piece(cap)
        self.chunks, self.rows = Route.shape(n, cap)
        self.slot_count = Route.slots(self.chunks, rounds)
        self.total = self.chunks * rounds
        (
            self.out,
            self.x,
            self.p,
            self.ra,
            self.sb,
            self.rb,
            self.ro,
            self.ret,
            self.as_,
            self.ar,
            self.fs,
            self.fr,
            self.ps,
            self.pr,
            self.rs,
            self.rr,
        ) = refs

    def span(self, place):
        return pl.ds(pl.multiple_of(place * self.size, 16), self.size)

    def peers(self, action):
        d = lax.axis_index("dp")

        def one(j, carry):
            action(lax.rem(d + j, self.n))
            return carry

        lax.fori_loop(1, self.n, one, 0)

    def out_copy(self, chunk, source, expert):
        d, t, sib, far, opp = places()
        return remote(
            self.out.at[chunk, self.span(expert)],
            self.x.at[chunk, t, self.span(source)],
            self.as_.at[chunk, expert],
            self.ar.at[chunk, source],
            (expert, t),
        )

    def back_copy(self, chunk, source, expert):
        d, t, sib, far, opp = places()
        return remote(
            self.ro.at[self.slot(chunk), self.span(source)],
            self.ret.at[chunk, self.span(expert)],
            self.rs.at[chunk, source],
            self.rr.at[chunk, expert],
            (source, t),
        )

    def spread_copies(self, chunk):
        d, t, sib, far, opp = places()
        mine, others = self.x.at[chunk, t], self.x.at[chunk, far]
        return [
            lambda: remote(mine, mine, self.fs.at[0, chunk], self.fr.at[0, chunk], (d, far)),
            lambda: remote(mine, mine, self.fs.at[1, chunk], self.fr.at[1, chunk], (d, sib)),
            lambda: remote(others, others, self.fs.at[2, chunk], self.fr.at[2, chunk], (d, sib)),
        ]

    def slot(self, chunk):
        return chunk if self.slot_count == self.total else lax.rem(chunk, self.slot_count)

    def reused(self, chunk, action):
        if self.slot_count < self.total:

            @pl.when(chunk >= self.slot_count)
            def _():
                action(chunk - self.slot_count)

    def sum_copies(self, chunk):
        d, t, sib, far, opp = places()
        p, ps, pr = self.p, self.ps, self.pr
        slot = self.slot(chunk)
        return [
            lambda: remote(p.at[slot, opp], self.ra.at[slot, 1], ps.at[0, chunk], pr.at[0, chunk], (d, sib)),
            lambda: remote(p.at[slot, sib], self.ra.at[slot, 0], ps.at[1, chunk], pr.at[1, chunk], (d, sib)),
            lambda: remote(self.sb.at[slot], self.rb.at[slot], ps.at[2, chunk], pr.at[2, chunk], (d, far)),
        ]

    def send(self, chunk, fill):
        d, t, sib, far, opp = places()
        fill(chunk)
        self.peers(lambda e: self.out_copy(chunk, d, e).start())
        self.x[chunk, t, self.span(d)] = self.out[chunk, self.span(d)]

    def begin(self, fill_first, fill):
        self.fill = fill
        for chunk in range(WINDOW_CHUNKS):
            self.send(chunk, fill_first)

    def put(self, chunk, products):
        for q in range(SLICES):
            self.p[self.slot(chunk), q] = products[:, q * HALF : (q + 1) * HALF].astype(bf16)

    def run(self, compute, hook):
        d, t, sib, far, opp = places()

        def more(chunk):
            self.send(chunk, self.fill)

        def arrive(chunk):
            self.peers(lambda s: self.out_copy(chunk, s, s).wait_recv())
            far_copy, near_copy, pass_copy = self.spread_copies(chunk)
            far_copy().start()
            near_copy().start()

        def forward(chunk):
            far_copy, near_copy, pass_copy = self.spread_copies(chunk)
            far_copy().wait_recv()
            pass_copy().start()

        def work(chunk):
            far_copy, near_copy, pass_copy = self.spread_copies(chunk)
            near_copy().wait_recv()
            pass_copy().wait_recv()
            rows = jnp.concatenate([self.x[chunk, q] for q in range(SLICES)], axis=1)

            def sent(old):
                first, second, third = self.sum_copies(old)
                first().wait_send()
                second().wait_send()

            self.reused(chunk, sent)
            compute(chunk, rows)
            first, second, third = self.sum_copies(chunk)
            first().start()
            second().start()

        def add_near(chunk):
            first, second, third = self.sum_copies(chunk)
            first().wait_recv()
            slot = self.slot(chunk)
            self.reused(chunk, lambda old: self.sum_copies(old)[2]().wait_send())
            self.sb[slot] = (self.p[slot, far].astype(f32) + self.ra[slot, 1].astype(f32)).astype(bf16)
            third().start()

        def add_far(chunk):
            first, second, third = self.sum_copies(chunk)
            second().wait_recv()
            third().wait_recv()
            slot = self.slot(chunk)
            self.reused(chunk, lambda old: self.peers(lambda s: self.back_copy(old, s, d).wait_send()))
            mine = self.p[slot, t].astype(f32) + self.ra[slot, 0].astype(f32)
            self.ro[slot] = (mine + self.rb[slot].astype(f32)).astype(bf16)
            self.peers(lambda s: self.back_copy(chunk, s, d).start())
            self.ret[chunk, self.span(d)] = self.ro[slot, self.span(d)]

        stages = (
            (more, -WINDOW_CHUNKS),
            (arrive, 0),
            (forward, STAGE_LAGS[0]),
            (work, STAGE_LAGS[1]),
            (add_near, STAGE_LAGS[2]),
            (add_far, STAGE_LAGS[3]),
        )

        def step(i, carry):
            for stage, lag in stages:

                @pl.when((i >= lag) & (i < self.total + lag))
                def _(stage=stage, lag=lag):
                    stage(i - lag)

            if hook is not None:
                hook(i)
            return carry

        lax.fori_loop(0, self.total + stages[-1][1], step, 0)

    def wait_back(self, first):
        d = lax.axis_index("dp")

        def one(chunk, carry):
            self.peers(lambda e: self.back_copy(chunk, d, e).wait_recv())
            return carry

        lax.fori_loop(first, first + self.chunks, one, 0)

    def returned(self, first):
        return self.ret[first : first + self.chunks].reshape(self.chunks * self.rows, HALF)

    def arrived(self, first, q):
        return self.x[first : first + self.chunks, q].reshape(self.chunks * self.rows, HALF)

    def wait_sends(self):
        d = lax.axis_index("dp")

        def one(chunk, carry):
            self.peers(lambda e: self.out_copy(chunk, d, e).wait_send())
            for copy in self.spread_copies(chunk):
                copy().wait_send()
            return carry

        lax.fori_loop(0, self.total, one, 0)

        def two(chunk, carry):
            self.peers(lambda e: self.back_copy(chunk, e, d).wait_send())
            for copy in self.sum_copies(chunk):
                copy().wait_send()
            return carry

        lax.fori_loop(self.total - self.slot_count, self.total, two, 0)


gelu_c = 0.7978845608028654
gelu_a = 0.044715


class Named:
    def __getattr__(self, name):
        return lambda *rest: (name, *rest)


named = Named()


def call(fn, ins, outs, scratch, collective_id):
    late = [one for one in ins if one[2] is late_spec]
    saved = [one for one in outs if one[3] is saved_spec]

    def kernel(*refs):
        refs = list(refs)
        m = types.SimpleNamespace(outs=types.SimpleNamespace())
        late_refs = []
        for one in ins:
            ref = refs.pop(0)
            if one[2] is late_spec:
                late_refs.append(ref)
            else:
                setattr(m, one[0], ref)
        for one in outs:
            setattr(m.outs if one[3] is saved_spec else m, one[0], refs.pop(0))
        copies = []
        if late:
            sems = refs.pop(0)
            for i, one in enumerate(late):
                buffer = refs.pop(0)
                setattr(m, one[0], buffer)
                copies.append(pltpu.make_async_copy(late_refs[i], buffer, sems.at[i]))
        for one in saved:
            setattr(m, one[0], refs.pop(0))
        for name, kinds in scratch:
            if isinstance(kinds, list):
                setattr(m, name, [refs.pop(0) for one in kinds])
            else:
                setattr(m, name, refs.pop(0))

        def late_wait():
            for copy in copies:
                copy.wait()

        m.late_wait = late_wait
        for copy in copies:
            copy.start()
        fn(m)

    flat = []
    if late:
        flat.append(pltpu.SemaphoreType.DMA((len(late),)))
        flat += [pltpu.VMEM(one[1].shape, one[1].dtype) for one in late]
    flat += [pltpu.VMEM(one[1], one[2]) for one in saved]
    for name, kinds in scratch:
        flat += kinds if isinstance(kinds, list) else [kinds]
    results = pl.pallas_call(
        kernel,
        name=fn.__name__,
        out_shape=[shaped(one[1], one[2]) for one in outs],
        in_specs=[one[2] for one in ins],
        out_specs=[one[3] for one in outs],
        scratch_shapes=flat,
        compiler_params=pltpu.CompilerParams(
            vmem_limit_bytes=vmem_bytes, collective_id=collective_id, has_side_effects=True
        ),
    )(*[one[1] for one in ins])
    return types.SimpleNamespace(**{one[0]: result for one, result in zip(outs, results)})


def gain_of(m, layer, which):
    t = lax.axis_index("tensor")
    return m.wide[t, 2 * layer + which : 2 * layer + which + 1].astype(f32)


def router_of(m, layer, experts):
    t = lax.axis_index("tensor")
    start = 2 * LAYERS + layer * experts
    return m.wide[t][start : start + experts]


def cap_count(cap):
    return 3 * SEQ // cap


def save_attention(m, saves):
    for buffer, out in ((m.proj, m.outs.proj), (m.lse, m.outs.lse), (m.ctx, m.outs.ctx), (m.r1, m.outs.r1)):
        saves.start(buffer, out)


def set_targets(m, layer, cap):
    piece = Route.piece(cap)
    chunks, rows = Route.shape(cap_count(cap), cap)
    slots = m.slots_row[layer]
    m.targ_row[...] = (slots // piece) * rows + m.routes_row[layer] * piece + lax.rem(slots, piece)
    m.targ_col[...] = int_cols(m.targ_row[...])


def set_attention_tables(m):
    m.seg_col[...] = int_cols(m.seg_row[...])
    m.bias[...] = bias_rows(m.tab[:, :BUCKETS].astype(bf16))


attention_scratch = [
    named.seg_col(pltpu.VMEM((SEQ, LANES), jnp.int32)),
    named.bias(pltpu.VMEM((8, WINDOW), f32)),
    named.part(pltpu.VMEM((SLICES, SEQ, HALF), bf16)),
    named.reduce(Reduce.scratch),
]


def attention_outs(width):
    return [
        named.proj((SEQ, 3 * width), bf16, saved_spec),
        named.lse((SEQ, LANES), f32, saved_spec),
        named.ctx((SEQ, width), bf16, saved_spec),
        named.r1((SEQ, LANES), f32, saved_spec),
    ]


def forward_outs(n, cap, hidden):
    chunks, rows = Route.shape(n, cap)
    return [
        named.mid((SEQ, HALF), f32, saved_spec),
        named.normed((SEQ, HALF), bf16, saved_spec),
        named.r2((SEQ, LANES), f32, saved_spec),
        named.gates((SEQ, LANES), f32, saved_spec),
        named.picked((2, SEQ, HALF), bf16, saved_spec),
        named.y((SEQ, HALF), f32, saved_spec),
        named.x_out((chunks, SLICES, rows, HALF), bf16, any_spec),
        named.inner_out((chunks, rows, hidden), bf16, any_spec),
        named.act_out((chunks, rows, hidden), bf16, any_spec),
        named.slope_out((chunks, rows, hidden), bf16, any_spec),
        named.wg_out((hidden, D), bf16, any_spec),
        named.wu_out((hidden, D), bf16, any_spec),
        named.wd_out((hidden, D), bf16, any_spec),
    ]


def forward_scratch(n, cap, hidden, experts):
    chunks, rows = Route.shape(n, cap)
    return [
        named.wg_stage(pltpu.VMEM((hidden, D), f32)),
        named.wu_stage(pltpu.VMEM((hidden, D), f32)),
        named.wd_stage(pltpu.VMEM((hidden, D), f32)),
        named.wg(pltpu.VMEM((hidden, D), bf16)),
        named.wu(pltpu.VMEM((hidden, D), bf16)),
        named.wd(pltpu.VMEM((hidden, D), bf16)),
        named.inner(pltpu.VMEM((chunks, rows, hidden), bf16)),
        named.act(pltpu.VMEM((chunks, rows, hidden), bf16)),
        named.slope(pltpu.VMEM((chunks, rows, hidden), bf16)),
        named.hot(pltpu.VMEM((2, SEQ, n * cap), bf16)),
        named.targ_row(pltpu.VMEM((2, SEQ), jnp.int32)),
        named.targ_col(pltpu.VMEM((SEQ, LANES), jnp.int32)),
        named.load_sems(pltpu.SemaphoreType.DMA((3,))),
        named.save_sems(pltpu.SemaphoreType.DMA((32,))),
        named.chunk_sems(pltpu.SemaphoreType.DMA((4, chunks))),
        named.tiny_one(Tiny.scratch(8, SEQ)),
        named.tiny_two(Tiny.scratch(experts, SEQ)),
        named.route(Route.scratch(n, cap, 1)),
    ]


def start_weight_loads(m, layer):
    loads = [
        pltpu.make_async_copy(src.at[layer, 0], dst, m.load_sems.at[i])
        for i, (src, dst) in enumerate(((m.gate_f, m.wg_stage), (m.up_f, m.wu_stage), (m.down_f, m.wd_stage)))
    ]
    for copy in loads:
        copy.start()
    return loads


def forward_rows(m, layer, experts, tiny_one, tiny_two, route):
    tiny_one.start(to_row(jnp.sum(m.mid[...] * m.mid[...], axis=1, keepdims=True)))
    scale = to_cols(lax.rsqrt(tiny_one.total() * (1.0 / D) + eps_norm))
    m.r2[...] = scale
    m.normed[...] = (m.mid[...] * scale[:, :1] * gain_of(m, layer, 1)).astype(bf16)

    def fill(chunk):
        number = chunk * route.rows + lax.broadcasted_iota(jnp.int32, (route.rows, SEQ), 0)
        hit = (m.targ_row[0:1] == number) | (m.targ_row[1:2] == number)
        route.out[chunk] = nn(hit.astype(f32).astype(bf16), m.normed[...]).astype(bf16)

    return fill


def narrow_weights(stage, low):
    def narrow(i, carry):
        rows = pl.ds(pl.multiple_of(i * 64, 64), 64)
        low[rows] = stage[rows].astype(bf16)
        return carry

    lax.fori_loop(0, low.shape[0] // 64, narrow, 0)


def router_gates(m, layer, tiny_two):
    logits = tiny_two.total()
    expert_no = lax.broadcasted_iota(jnp.int32, logits.shape, 0)
    chosen = [
        jnp.sum(jnp.where(expert_no == m.routes_row[layer, k : k + 1], logits, 0.0), axis=0, keepdims=True)
        for k in range(2)
    ]
    share = [1.0 / (1.0 + jnp.exp(chosen[1 - k] - chosen[k])) for k in range(2)]
    place = lax.broadcasted_iota(jnp.int32, (8, SEQ), 0)
    m.gates[...] = to_cols(jnp.where(place == 0, share[0], share[1]))


def forward_products(m, chunk, rows):
    gate_pre = nt(rows, m.wg[...])
    up_pre = nt(rows, m.wu[...])
    square = gate_pre * gate_pre
    bent = jnp.tanh(gelu_c * gate_pre * (1.0 + gelu_a * square))
    half = 0.5 * (1.0 + bent)
    active = gate_pre * half
    steep = half + 0.5 * gate_pre * (1.0 - bent * bent) * (gelu_c * (1.0 + 3.0 * gelu_a * square))
    inner_rows = (active * up_pre).astype(bf16)
    m.inner[chunk] = inner_rows
    m.act[chunk] = active.astype(bf16)
    m.slope[chunk] = (up_pre * steep).astype(bf16)
    return nn(inner_rows, m.wd[...])


def set_hot(m, count):
    for k in range(2):
        m.hot[k] = hot_columns(m.targ_col, k, count)


def forward_combine(m, route):
    route.wait_back(0)
    y = m.mid[...]
    for k in range(2):
        rows = nn(m.hot[k], route.returned(0))
        m.picked[k] = rows.astype(bf16)
        y = y + m.gates[:, k : k + 1] * rows
    m.y[...] = y


def forward_experts(m, n, cap, layer, experts, loads, saves, hook):
    tiny_one = Tiny(m.tiny_one)
    tiny_two = Tiny(m.tiny_two)
    route = Route(n, cap, 1, m.route)
    fill = forward_rows(m, layer, experts, tiny_one, tiny_two, route)
    route.begin(fill, fill)
    tiny_two.start(nt(router_of(m, layer, experts), m.normed[...]))
    for buffer, out in ((m.mid, m.outs.mid), (m.normed, m.outs.normed), (m.r2, m.outs.r2)):
        saves.start(buffer, out)
    stages = (m.wg_stage, m.wu_stage, m.wd_stage)
    lows = (m.wg, m.wu, m.wd)
    for copy, stage, low, out in zip(loads, stages, lows, (m.wg_out, m.wu_out, m.wd_out)):
        copy.wait()
        narrow_weights(stage, low)
        saves.start(low, out)
    router_gates(m, layer, tiny_two)
    saves.start(m.gates, m.outs.gates)

    def chunk_saves(chunk):
        pairs = ((route.x, m.x_out), (m.inner, m.inner_out), (m.act, m.act_out), (m.slope, m.slope_out))
        return [
            pltpu.make_async_copy(src.at[chunk], dst.at[chunk], m.chunk_sems.at[i, chunk])
            for i, (src, dst) in enumerate(pairs)
        ]

    def compute(chunk, rows):
        products = forward_products(m, chunk, rows)
        for copy in chunk_saves(chunk):
            copy.start()
        route.put(chunk, products)

    def hook_all(i):
        @pl.when(i == 2)
        def _():
            set_hot(m, n * cap)

        if hook is not None:
            hook(i)

    route.run(compute, hook_all)
    forward_combine(m, route)
    saves.start(m.picked, m.outs.picked)
    saves.start(m.y, m.outs.y)
    route.wait_sends()

    def drain(chunk, carry):
        for copy in chunk_saves(chunk):
            copy.wait()
        return carry

    lax.fori_loop(0, route.chunks, drain, 0)


class Pieces:
    def __init__(self, n, pieces, send, recv):
        self.n, self.pieces, self.send, self.recv = n, pieces, send, recv

    def copies(self, piece, k):
        d, t, sib, far, opp = places()
        n = self.n
        near = d + 1 - 2 * lax.rem(d, 2)
        view, src = self.pieces[piece]
        peer = lax.rem(d + 2 * k, n)
        source = lax.rem(d - 2 * k + n, n)
        send, recv = self.send, self.recv
        return (
            lambda: remote(src, view(d), send.at[piece, 0, k], recv.at[piece, 0, k], (peer, t)),
            lambda: remote(view(source), view(source), send.at[piece, 1, k], recv.at[piece, 1, k], (near, t)),
        )

    def own(self, piece):
        d, t, sib, far, opp = places()
        near = d + 1 - 2 * lax.rem(d, 2)
        view, src = self.pieces[piece]
        return remote(src, view(d), self.send.at[piece, 1, 0], self.recv.at[piece, 1, 0], (near, t))

    def loop(self, action):
        def one(k, carry):
            action(k)
            return carry

        lax.fori_loop(1, self.n // 2, one, 0)

    def start(self, piece):
        self.loop(lambda k: self.copies(piece, k)[0]().start())
        self.own(piece).start()

    def forward_one(self, piece, k):
        direct, passed = self.copies(piece, k)
        direct().wait_recv()
        passed().start()

    def forward(self, piece):
        self.loop(lambda k: self.forward_one(piece, k))

    def finish(self, piece):
        self.own(piece).wait_recv()
        self.loop(lambda k: self.copies(piece, k)[1]().wait_recv())

    def wait_sends(self, piece):
        self.own(piece).wait_send()

        def one(k):
            direct, passed = self.copies(piece, k)
            direct().wait_send()
            passed().wait_send()

        self.loop(one)


def place_small(n, small_all, rows):
    own = small_all.shape[2]
    if own == LANES:
        return [
            jnp.concatenate([small_all[2 * q].astype(f32), small_all[2 * q + 1].astype(f32)], axis=1)
            for q in range(SLICES)
        ]
    out = []
    for q in range(SLICES):
        total = jnp.zeros((rows, HALF), f32)
        for i in range(HALF // own):
            lane = lax.broadcasted_iota(jnp.int32, (own, HALF), 1)
            spot = lax.broadcasted_iota(jnp.int32, (own, HALF), 0)
            hot = (lane == spot + i * own).astype(f32).astype(bf16)
            total = total + nn(small_all[q * (HALF // own) + i], hot)
        out.append(total)
    return out


def first_program(n, cap, experts, heads):
    buckets = BUCKETS // n

    def first_kernel(m):
        d, t, sib, far, opp = places()
        own = D // n
        saves = Saves(m.save_sems)
        loads = start_weight_loads(m, 0)
        reduce = Reduce(m.part, m.reduce)

        def span(i):
            return pl.ds(pl.multiple_of(i * own, 16), own)

        views = [
            (lambda i: m.small_all.at[i], m.small),
            (lambda i: m.wqkv.at[0, span(i)], m.qkv_low.at[0, 0]),
            (lambda i: m.wqkv.at[1, span(i)], m.qkv_low.at[0, 1]),
            (lambda i: m.wqkv.at[2, span(i)], m.qkv_low.at[0, 2]),
            (lambda i: m.wo.at[span(i)], m.out_low.at[0]),
            (lambda i: m.wqkv_next.at[:, span(i)], m.qkv_low.at[1]),
            (lambda i: m.wo_next.at[span(i)], m.out_low.at[1]),
        ]
        pieces = Pieces(n, views, m.piece_send, m.piece_recv)
        m.qkv_low[0] = m.qkv[0].astype(bf16)
        greet(n, True)
        pieces.start(0)
        pieces.start(1)
        pieces.start(2)
        m.out_low[0] = m.out[0].astype(bf16)
        m.small_all[d] = m.small[...]
        m.wqkv[:, span(d)] = m.qkv_low[0]
        m.wo[span(d)] = m.out_low[0]
        m.qkv_low[1] = m.qkv[1].astype(bf16)
        m.out_low[1] = m.out[1].astype(bf16)
        saves.start(m.qkv_low.at[1], m.wqkv_next.at[:, span(d)])
        saves.start(m.out_low.at[1], m.wo_next.at[span(d)])
        set_targets(m, 0, cap)
        pieces.forward(0)
        pieces.finish(0)
        rows = m.small.shape[0]
        slices = place_small(n, m.small_all, rows)
        for q in range(SLICES):
            m.wide[q] = slices[q].astype(bf16)
        first = 2 * LAYERS + LAYERS * experts
        table = jnp.zeros((LAYERS * heads, LANES), f32)
        width = m.small_all.shape[2]
        for i in range(n):
            lane = lax.broadcasted_iota(jnp.int32, (width, LANES), 1)
            spot = lax.broadcasted_iota(jnp.int32, (width, LANES), 0)
            hot = ((lane == spot + i * buckets) & (spot < buckets)).astype(f32).astype(bf16)
            table = table + nn(m.small_all[i][first : first + LAYERS * heads], hot)
        m.tab[...] = table
        set_attention_tables(m)
        total = None
        for q in range(SLICES):
            x = m.tok[:, q * HALF : (q + 1) * HALF].astype(f32)
            m.hg[q] = (x * m.wide[q, 0:1].astype(f32)).astype(bf16)
            squares = jnp.sum(x * x, axis=1, keepdims=True)
            total = squares if total is None else total + squares
        m.r1[...] = jnp.broadcast_to(lax.rsqrt(total * (1.0 / D) + eps_norm), (SEQ, LANES))
        saves.start(m.hg, m.hg_out)
        pieces.forward(1)
        pieces.start(3)
        pieces.forward(2)
        pieces.start(4)
        pieces.finish(1)
        for b in range(2):
            project(m, b, 0)
        pieces.forward(3)
        pieces.finish(2)
        for b in range(2):
            project(m, b, 1)
        pieces.forward(4)
        for piece in (5, 6):
            pieces.start(piece)
        pieces.finish(3)
        for b in range(2):
            project(m, b, 2)
        saves.start(m.wqkv, m.wqkv_out)
        for b in range(2):
            attend_block(m, b, 0)
            if b == 0:
                pieces.finish(4)
                saves.start(m.wo, m.wo_out)
            project_out(m, b)
            reduce.start(b)
            reduce.middle(b)
        save_attention(m, saves)
        for b in range(2):
            span_b = block_rows(b)
            m.mid[span_b] = pick_slice(m.tok[span_b].astype(f32)) + reduce.finish(b)

        half = n // 2
        share = max(1, half // 4)

        def pass_on(first):
            def one(k, carry):
                for piece in (5, 6):
                    pieces.forward_one(piece, k)
                return carry

            lax.fori_loop(first, min(first + share, half), one, 0)

        def hook(i):
            for event in range(3):

                @pl.when(i == 2 * event + 1)
                def _(event=event):
                    pass_on(1 + event * share)

        forward_experts(m, n, cap, 0, experts, loads, saves, hook)
        if 1 + 3 * share < half:
            pass_on(1 + 3 * share)
        for piece in (5, 6):
            pieces.finish(piece)
        for piece in range(7):
            pieces.wait_sends(piece)
        reduce.wait_sends()
        saves.wait()

    return first_kernel


def norm_backward(tiny, grad, rows, scale, gain, upstream):
    weighted = grad * gain
    tiny.start(to_row(jnp.sum(weighted * rows, axis=1, keepdims=True)))
    gain_grad = jnp.sum(grad * rows * scale, axis=0, keepdims=True)
    base = upstream + scale * weighted
    mean = to_cols(tiny.total())[:, :1] * (1.0 / D)
    return base - rows * (scale * scale * scale * mean), gain_grad


def backward_outs(n, cap, hidden, experts):
    return [
        named.midg((SEQ, HALF), f32, vmem_spec),
        named.gain_rows((8, HALF), f32, vmem_spec),
        named.router_g((experts, HALF), f32, vmem_spec),
        named.wg_grad((hidden, D), bf16, any_spec),
        named.wu_grad((hidden, D), bf16, any_spec),
        named.wd_grad((hidden, D), bf16, any_spec),
    ]


def backward_ins(state):
    return [
        named.picked(state.picked, late_spec),
        named.gates(state.gates, late_spec),
        named.mid(state.mid, late_spec),
        named.normed(state.normed, late_spec),
        named.r2(state.r2, late_spec),
        named.x_in(state.x_out, any_spec),
        named.inner_in(state.inner_out, any_spec),
        named.act_in(state.act_out, any_spec),
        named.slope_in(state.slope_out, any_spec),
        named.wg_in(state.wg_out, any_spec),
        named.wu_in(state.wu_out, any_spec),
        named.wd_in(state.wd_out, any_spec),
    ]


def backward_scratch(n, cap, hidden, experts):
    chunks, rows = Route.shape(n, cap)
    return [
        named.wg(pltpu.VMEM((hidden, D), bf16)),
        named.wu(pltpu.VMEM((hidden, D), bf16)),
        named.wd(pltpu.VMEM((hidden, D), bf16)),
        named.xs(pltpu.VMEM((chunks, SLICES, rows, HALF), bf16)),
        named.inner(pltpu.VMEM((chunks, rows, hidden), bf16)),
        named.act(pltpu.VMEM((chunks, rows, hidden), bf16)),
        named.slope(pltpu.VMEM((chunks, rows, hidden), bf16)),
        named.gpg(pltpu.VMEM((chunks, rows, hidden), bf16)),
        named.upg(pltpu.VMEM((chunks, rows, hidden), bf16)),
        named.dy(pltpu.VMEM((SEQ, HALF), f32)),
        named.pgs(pltpu.VMEM((2 * SEQ, HALF), bf16)),
        named.hot(pltpu.VMEM((2, SEQ, n * cap), bf16)),
        named.logit_g(pltpu.VMEM((experts, SEQ), f32)),
        named.targ_row(pltpu.VMEM((2, SEQ), jnp.int32)),
        named.targ_col(pltpu.VMEM((SEQ, LANES), jnp.int32)),
        named.load_sems(pltpu.SemaphoreType.DMA((7,))),
        named.save_sems(pltpu.SemaphoreType.DMA((32,))),
        named.tiny_one(Tiny.scratch(8, SEQ)),
        named.tiny_two(Tiny.scratch(8, SEQ)),
        named.route(Route.scratch(n, cap, 1)),
    ]


def start_backward_loads(m):
    pairs = (
        (m.wd_in, m.wd),
        (m.act_in, m.act),
        (m.slope_in, m.slope),
        (m.wg_in, m.wg),
        (m.wu_in, m.wu),
        (m.inner_in, m.inner),
        (m.x_in, m.xs),
    )
    loads = [pltpu.make_async_copy(src, dst, m.load_sems.at[i]) for i, (src, dst) in enumerate(pairs)]
    for copy in loads:
        copy.start()
    return loads


def backward_rows(m, route):
    for k in range(2):
        m.pgs[k * SEQ : (k + 1) * SEQ] = (m.gates[:, k : k + 1] * m.dy[...]).astype(bf16)

    def fill(chunk, place):
        number = chunk * route.rows + lax.broadcasted_iota(jnp.int32, (route.rows, SEQ), 0)
        hits = [(m.targ_row[k : k + 1] == number).astype(f32).astype(bf16) for k in range(2)]
        route.out[place] = nn(jnp.concatenate(hits, axis=1), m.pgs[...]).astype(bf16)

    return fill


def start_shares(m, tiny):
    place = lax.broadcasted_iota(jnp.int32, (8, SEQ), 0)
    shares = [to_row(jnp.sum(m.dy[...] * m.picked[k].astype(f32), axis=1, keepdims=True)) for k in range(2)]
    tiny.start(jnp.where(place == 0, shares[0], shares[1]))


def logit_gradient(m, layer, experts, tiny):
    share_grad = tiny.total()
    gate_rows = jnp.transpose(m.gates[...])[:8]
    product = gate_rows * share_grad
    both = product[0:1] + product[1:2]
    chosen = gate_rows * (share_grad - both)
    expert_no = lax.broadcasted_iota(jnp.int32, (experts, SEQ), 0)
    logit_g = jnp.zeros((experts, SEQ), f32)
    for k in range(2):
        logit_g = logit_g + jnp.where(expert_no == m.routes_row[layer, k : k + 1], chosen[k : k + 1], 0.0)
    m.logit_g[...] = logit_g
    m.router_g[...] = nn(logit_g.astype(bf16), m.normed[...])


def backward_products(m, chunk, rows):
    inner_grad = nt(rows, m.wd[...])
    up_low = (inner_grad * m.act[chunk].astype(f32)).astype(bf16)
    gate_low = (inner_grad * m.slope[chunk].astype(f32)).astype(bf16)
    m.upg[chunk] = up_low
    m.gpg[chunk] = gate_low
    return nn(gate_low, m.wg[...]) + nn(up_low, m.wu[...])


class Products:
    def __init__(self, m, route, first, inputs_of, saves):
        self.m, self.route, self.first, self.inputs_of, self.saves = m, route, first, inputs_of, saves

    def one(self, left_ref, right_of, stage, out):
        count = self.route.chunks * self.route.rows
        hidden = stage.shape[0]
        right = jnp.concatenate([right_of(q) for q in range(SLICES)], axis=1)
        for start in range(0, hidden, HALF):
            size = min(HALF, hidden - start)
            left = left_ref[:, :, start : start + size].reshape(count, size)
            stage[start : start + size] = tn(left, right).astype(bf16)
            self.saves.start(stage, out, slice(start, start + size))

    def step(self):
        return self.route.total + STAGE_LAGS[2] - 1

    def in_loop(self, i):
        @pl.when(i == self.step())
        def _():
            self.one(self.m.gpg, self.inputs_of, self.m.wg, self.m.wg_grad)

    def after(self):
        self.one(self.m.upg, self.inputs_of, self.m.wu, self.m.wu_grad)
        self.one(self.m.inner, lambda q: self.route.arrived(self.first, q), self.m.wd, self.m.wd_grad)


def backward_tail(m, layer, experts, tiny, route, first, gain_one):
    route.wait_back(first)
    grad = tn(m.logit_g[...].astype(bf16), router_of(m, layer, experts))
    for k in range(2):
        grad = grad + nn(m.hot[k], route.returned(first))
    value, gain_two = norm_backward(tiny, grad, m.mid[...], m.r2[:, :1], gain_of(m, layer, 1), m.dy[...])
    m.midg[...] = value
    gain_place = lax.broadcasted_iota(jnp.int32, (8, HALF), 0)
    m.gain_rows[...] = jnp.where(gain_place == 0, gain_two, jnp.where(gain_place == 1, gain_one, 0.0))
    route.wait_sends()


def backward_experts(m, n, cap, layer, experts, loads, saves, gain_one, hook, hook_end):
    tiny_one = Tiny(m.tiny_one)
    tiny_two = Tiny(m.tiny_two)
    route = Route(n, cap, 1, m.route)
    fill_one = backward_rows(m, route)

    def fill(chunk):
        fill_one(chunk, chunk)

    route.begin(fill, fill)
    start_shares(m, tiny_one)
    for copy in loads[:5]:
        copy.wait()
    logit_gradient(m, layer, experts, tiny_one)

    def compute(chunk, rows):
        route.put(chunk, backward_products(m, chunk, rows))

    def hook_all(i):
        @pl.when(i == 1)
        def _():
            set_hot(m, n * cap)

        hook(i)
        products.in_loop(i)

    count = route.chunks * route.rows
    products = Products(m, route, 0, lambda q: m.xs[:, q].reshape(count, HALF), saves)
    for copy in loads[5:]:
        copy.wait()
    route.run(compute, hook_all)
    products.after()
    hook_end()
    backward_tail(m, layer, experts, tiny_two, route, 0, gain_one)


def top_program(n, cap, experts, heads, layer):
    def top_kernel(m):
        saves = Saves(m.save_sems)
        weight_copies = [
            pltpu.make_async_copy(m.wqkv_in, m.wqkv, m.weight_sems.at[0]),
            pltpu.make_async_copy(m.wo_in, m.wo, m.weight_sems.at[1]),
        ]
        expert_weights = [
            pltpu.make_async_copy(src.at[layer, 0], m.stage, m.load_sems.at[i])
            for i, src in enumerate((m.gate_f, m.up_f, m.down_f))
        ]
        expert_weights[0].start()
        for copy in weight_copies:
            copy.start()
        reduce = Reduce(m.part, m.reduce)
        gather = Gather(m.hg, m.gather)
        tiny = Tiny(m.tiny_zero)
        greet(n, True)
        gain = gain_of(m, layer, 0)
        for b in range(2):
            gather.start(b, (m.h[block_rows(b)] * gain).astype(bf16))
        tiny.start(to_row(jnp.sum(m.h[...] * m.h[...], axis=1, keepdims=True)))
        set_attention_tables(m)
        set_targets(m, layer, cap)
        m.r1[...] = to_cols(lax.rsqrt(tiny.total() * (1.0 / D) + eps_norm))
        m.late_wait()
        m.dy[...] = pick_slice(m.cot[...].astype(f32))
        lows = (m.wg, m.wu, m.wd)
        expert_weights[0].wait()
        narrow_weights(m.stage, lows[0])
        expert_weights[1].start()
        for copy in weight_copies:
            copy.wait()
        gather.forward(0)
        gather.finish(0)
        gather.forward(1)
        attention_block(m, 0, layer * heads, lambda: None)
        reduce.start(0)
        gather.finish(1)
        attention_block(m, 1, layer * heads, lambda: reduce.middle(0))
        reduce.start(1)
        saves.start(m.hg, m.hg_out)
        save_attention(m, saves)
        reduce.middle(1)
        expert_weights[1].wait()
        narrow_weights(m.stage, lows[1])
        expert_weights[2].start()
        for b in range(2):
            span_b = block_rows(b)
            m.mid[span_b] = m.h[span_b] + reduce.finish(b)
        tiny_one = Tiny(m.tiny_one)
        tiny_two = Tiny(m.tiny_two)
        tiny_three = Tiny(m.tiny_three)
        tiny_four = Tiny(m.tiny_four)
        route = Route(n, cap, 2, m.route)
        chunks = route.chunks
        fill_forward = forward_rows(m, layer, experts, tiny_one, tiny_two, route)

        def fill(chunk):
            @pl.when(chunk < chunks)
            def _():
                fill_forward(chunk)

            @pl.when(chunk >= chunks)
            def _():
                fill_backward(chunk - chunks, chunk)

        route.begin(fill_forward, fill)
        tiny_two.start(nt(router_of(m, layer, experts), m.normed[...]))
        expert_weights[2].wait()
        narrow_weights(m.stage, lows[2])
        router_gates(m, layer, tiny_two)
        fill_backward = backward_rows(m, route)

        def compute(chunk, rows):
            @pl.when(chunk < chunks)
            def _():
                route.put(chunk, forward_products(m, chunk, rows))

            @pl.when(chunk >= chunks)
            def _():
                route.put(chunk, backward_products(m, chunk - chunks, rows))

        def hook(i):
            @pl.when(i == 2)
            def _():
                set_hot(m, n * cap)

            @pl.when(i == chunks + STAGE_LAGS[3] + 1)
            def _():
                forward_combine(m, route)
                saves.start(m.y, m.outs.y)
                start_shares(m, tiny_three)

            products.in_loop(i)

        products = Products(m, route, chunks, lambda q: route.arrived(0, q), saves)
        route.run(compute, hook)
        logit_gradient(m, layer, experts, tiny_three)
        products.after()
        backward_tail(m, layer, experts, tiny_four, route, chunks, jnp.zeros((1, HALF), f32))
        gather.wait_sends()
        reduce.wait_sends()
        saves.wait()

    return top_kernel


def attention_back_ins(kept, midg):
    return [
        named.midg_in(midg, vmem_spec),
        named.a_ctx(kept.ctx, late_spec),
        named.a_proj(kept.proj, late_spec),
        named.a_lse(kept.lse, late_spec),
        named.a_r1(kept.r1, late_spec),
        named.a_hg(kept.hg, late_spec),
        named.a_wqkv(kept.wqkv, late_spec),
        named.a_wo(kept.wo, late_spec),
        named.a_h(kept.h, late_spec),
    ]


def attention_back_scratch(width, heads):
    return attention_scratch + [
        named.pg(pltpu.VMEM((SEQ, 3 * width), bf16)),
        named.dk(pltpu.VMEM((SEQ, width), f32)),
        named.dv(pltpu.VMEM((SEQ, width), f32)),
        named.bias_grad(pltpu.VMEM((heads, HALF, 2 * HALF), f32)),
        named.probs(pltpu.VMEM((heads, HALF, 3 * HALF), f32)),
        named.ag(pltpu.VMEM((SLICES, SEQ, HALF), bf16)),
        named.gather(Gather.scratch),
        named.tiny_zero(Tiny.scratch(8, SEQ)),
    ]


def attention_view(m):
    return types.SimpleNamespace(
        seg_col=m.seg_col,
        seg_row=m.seg_row,
        bias=m.bias,
        part=m.part,
        ctx=m.a_ctx,
        proj=m.a_proj,
        lse=m.a_lse,
        r1=m.a_r1,
        hg=m.a_hg,
        wqkv=m.a_wqkv,
        wo=m.a_wo,
        pg=m.pg,
        dk=m.dk,
        dv=m.dv,
        bias_grad=m.bias_grad,
        probs=m.probs,
        ag=m.ag,
        wog=m.wog,
        qkvg=m.qkvg,
    )


def attention_back(m, layer, heads, after_gather, after_out, after_qkv):
    gather = Gather(m.ag, m.gather)
    reduce = Reduce(m.part, m.reduce)
    tiny = Tiny(m.tiny_zero)
    a = attention_view(m)
    for b in (1, 0):
        gather.start(b, m.midg_in[block_rows(b)].astype(bf16))
    set_attention_tables(m)
    m.late_wait()
    attention_probs(a, 1, layer * heads)
    gather.forward(1)
    attention_probs(a, 0, layer * heads)
    gather.forward(0)
    gather.finish(1)
    late_dots = attention_back_block(a, 1, lambda: None)
    reduce.start(1)
    gather.finish(0)
    after_gather()
    early_dots = attention_back_block(a, 0, lambda: reduce.middle(1))
    reduce.start(0)
    tiny.start(to_row(jnp.concatenate([early_dots, late_dots], axis=0)))
    out_gradient(a)
    after_out()
    reduce.middle(0)
    qkv_gradient(a)
    after_qkv()
    m.table[...] = table_gradient(a)
    grad = jnp.concatenate([reduce.finish(0), reduce.finish(1)], axis=0)
    h = m.a_h[...] if m.a_h.shape[1] == HALF else pick_slice(m.a_h[...].astype(f32))
    scale = m.a_r1[:, :1]
    gain_grad = jnp.sum(grad * h * scale, axis=0, keepdims=True)
    base = m.midg_in[...] + scale * (grad * gain_of(m, layer, 0))
    mean = to_cols(tiny.total())[:, :1] * (1.0 / D)
    gather.wait_sends()
    reduce.wait_sends()
    return base - h * (scale * scale * scale * mean), gain_grad


def back_program(n, cap, experts, heads, layer):
    def back_next_kernel(m):
        saves = Saves(m.save_sems)
        loads = start_backward_loads(m)
        greet(n, True)
        set_targets(m, layer, cap)
        own = D // n

        def rows_of(e):
            return pl.ds(pl.multiple_of(e * own, 16), own)

        late_qkv = Scatter(n, lambda e: m.qkvg.at[:, rows_of(e)], m.qkv_sums, m.near_a, None, None)
        late_out = Scatter(n, lambda e: m.wog.at[rows_of(e)], m.out_sums, m.near_b, None, None)
        half = n // 2
        share = max(1, half // 4)
        value, gain_one = attention_back(
            m,
            layer + 1,
            heads,
            lambda: None,
            lambda: late_out.near_start(1, half + 1),
            lambda: late_qkv.near_start(1, 1 + share),
        )
        m.dy[...] = value

        def hook(i):
            for event in range(1, half // share):

                @pl.when(i == 2 * event - 1)
                def _(event=event):
                    late_qkv.near_start(1 + event * share, 1 + (event + 1) * share)

                @pl.when(i == 2 * event)
                def _(event=event):
                    late_qkv.loop(1 + (event - 1) * share, 1 + event * share, late_qkv.near_sum)

            @pl.when(i == 3)
            def _():
                late_out.near_sums()

        def hook_end():
            late_qkv.loop(1 + half - share, 1 + half, late_qkv.near_sum)
            saves.start(m.qkv_sums, m.outs.qkv_sums)
            saves.start(m.out_sums, m.outs.out_sums)

        backward_experts(m, n, cap, layer, experts, loads, saves, gain_one, hook, hook_end)
        late_out.near_wait_sends()
        late_qkv.near_wait_sends()
        saves.wait()

    return back_next_kernel


class Scatter:
    @staticmethod
    def near_scratch(n, block):
        return [
            pltpu.VMEM((n // 2,) + block, bf16),
            pltpu.SemaphoreType.DMA((n // 2,)),
            pltpu.SemaphoreType.DMA((n // 2,)),
        ]

    @staticmethod
    def far_scratch(n, block):
        return [
            pltpu.VMEM((n // 2,) + block, bf16),
            pltpu.SemaphoreType.DMA((n // 2,)),
            pltpu.SemaphoreType.DMA((n // 2,)),
        ]

    def __init__(self, n, block_of, sums, near_refs, out, far_refs):
        self.n, self.block_of, self.sums, self.out = n, block_of, sums, out
        if near_refs is not None:
            self.near, self.near_send, self.near_recv = near_refs
        if far_refs is not None:
            self.got, self.far_send, self.far_recv = far_refs

    def near_copy(self, k):
        d, t, sib, far, opp = places()
        parity = lax.rem(d, 2)
        src = self.block_of(2 * k + 1 - parity)
        return remote(src, self.near.at[k], self.near_send.at[k], self.near_recv.at[k], (d + 1 - 2 * parity, t))

    def far_copy(self, k, source):
        d, t, sib, far, opp = places()
        return remote(
            self.sums.at[k], self.got.at[source], self.far_send.at[k], self.far_recv.at[source], (2 * k + lax.rem(d, 2), t)
        )

    def spot(self, j):
        d = lax.axis_index("dp")
        return lax.rem(d // 2 + j, self.n // 2)

    def loop(self, first, last, action):
        def one(j, carry):
            action(self.spot(j))
            return carry

        lax.fori_loop(first, last, one, 0)

    def near_start(self, first, last):
        self.loop(first, last, lambda k: self.near_copy(k).start())

    def near_sum(self, k):
        d = lax.axis_index("dp")
        self.near_copy(k).wait_recv()
        mine = self.block_of(2 * k + lax.rem(d, 2))[...].astype(f32)
        self.sums[k] = (mine + self.near[k].astype(f32)).astype(bf16)

    def near_sums(self):
        self.loop(1, self.n // 2 + 1, self.near_sum)

    def near_wait_sends(self):
        self.loop(0, self.n // 2, lambda k: self.near_copy(k).wait_send())

    def far_start(self):
        d = lax.axis_index("dp")
        self.loop(1, self.n // 2, lambda k: self.far_copy(k, d // 2).start())

    def both(self, ahead):
        d = lax.axis_index("dp")
        total = self.n // 2

        def one(j, carry):
            k = self.spot(j)

            @pl.when(j + ahead <= total)
            def _():
                self.near_copy(self.spot(j + ahead)).start()

            self.near_sum(k)

            @pl.when(k != d // 2)
            def _():
                self.far_copy(k, d // 2).start()

            return carry

        lax.fori_loop(1, total + 1, one, 0)

    def finish(self):
        d = lax.axis_index("dp")
        total = self.sums[d // 2].astype(f32)

        def one(j, carry):
            k = self.spot(j)
            self.far_copy(k, k).wait_recv()
            return carry + self.got[k].astype(f32)

        self.out[...] = lax.fori_loop(1, self.n // 2, one, total)
        self.loop(1, self.n // 2, lambda k: self.far_copy(k, d // 2).wait_send())


def final_program(n, experts, heads):
    own = D // n

    def final_kernel(m):
        d, t, sib, far, opp = places()
        saves = Saves(m.save_sems)

        def rows_of(e):
            return pl.ds(pl.multiple_of(e * own, 16), own)

        late_qkv = Scatter(n, None, m.qkv_sums_next, None, m.qkv_grad.at[1], m.far_a)
        late_out = Scatter(n, None, m.out_sums_next, None, m.out_grad.at[1], m.far_b)
        early_qkv = Scatter(n, lambda e: m.qkvg.at[:, rows_of(e)], m.qkv_sums, m.near_c, m.qkv_grad.at[0], m.far_c)
        early_out = Scatter(n, lambda e: m.wog.at[rows_of(e)], m.out_sums, m.near_d, m.out_grad.at[0], m.far_d)
        half = n // 2
        output = Gather(m.output_buf, m.output_gather)
        dx_all = Gather(m.dx_buf, m.dx_gather)
        greet(n, True)
        late_out.far_start()
        late_qkv.far_start()

        def after_out():
            early_out.near_start(1, half + 1)

        def after_qkv():
            early_qkv.near_start(1, 3)
            early_out.both(half)

        def after_gather():
            for b in range(2):
                output.start(b, m.y_last[block_rows(b)].astype(bf16))

        dx, gain_one = attention_back(m, 0, heads, after_gather, after_out, after_qkv)
        for b in range(2):
            dx_all.start(b, dx[block_rows(b)].astype(bf16))
        place = lax.broadcasted_iota(jnp.int32, (8, HALF), 0)
        m.pack[0:8] = jnp.where(
            place == 0,
            gain_one,
            jnp.where(
                place == 1,
                m.gain_rows_0[0:1],
                jnp.where(place == 2, m.gain_rows_0[1:2], jnp.where(place == 3, m.gain_rows_1[0:1], 0.0)),
            ),
        )
        m.pack[8:16] = jnp.concatenate([m.table[...], m.table_next[...]], axis=1)
        m.pack[16 : 16 + experts] = m.router_g_0[...]
        m.pack[16 + experts : 16 + 2 * experts] = m.router_g_1[...]

        def pack_copy(j, source, target):
            return remote(m.pack, m.packs.at[source], m.pack_send.at[j], m.pack_recv.at[source], (target, t))

        def spread(j, carry):
            pack_copy(j, d, lax.rem(d + j, n)).start()
            return carry

        lax.fori_loop(1, n, spread, 0)
        early_qkv.both(2)
        for b in range(2):
            output.forward(b)
        for b in range(2):
            dx_all.forward(b)
        m.packs[d] = m.pack[...]

        def collect(j, carry):
            source = lax.rem(d + j, n)
            pack_copy(j, source, source).wait_recv()
            return carry

        lax.fori_loop(1, n, collect, 0)

        def add(i, carry):
            return carry + m.packs[i]

        m.small_out[t] = lax.fori_loop(1, n, add, m.packs[0])

        def all_copies():
            return [
                remote(m.small_out.at[t], m.small_out.at[t], m.all_send.at[i], m.all_recv.at[i], (d, peer))
                for i, peer in enumerate((sib, far, opp))
            ]

        for copy in all_copies():
            copy.start()
        for gather, out in ((output, m.output), (dx_all, m.dx_full)):
            for b in range(2):
                gather.finish(b)
            for q in range(SLICES):
                saves.start(gather.buf.at[q], out.at[:, pl.ds(q * HALF, HALF)])
        for one in (late_out, late_qkv, early_out, early_qkv):
            one.finish()
        early_out.near_wait_sends()
        early_qkv.near_wait_sends()

        def sent(j, carry):
            pack_copy(j, d, lax.rem(d + j, n)).wait_send()
            return carry

        lax.fori_loop(1, n, sent, 0)
        for copy in all_copies():
            copy.wait()
        output.wait_sends()
        dx_all.wait_sends()
        saves.wait()

    return final_kernel


def widen_kernel(*refs):
    ins, outs = refs[: 3 * LAYERS + 4], refs[3 * LAYERS + 4 :]
    for i in range(3):
        for layer in range(LAYERS):
            outs[i][layer, 0] = ins[3 * layer + i][...].astype(f32)
    for i in range(4):
        outs[3 + i][...] = ins[3 * LAYERS + i][...].astype(outs[3 + i].dtype)


def widen(grads, others):
    hidden = grads[0][0].shape[0]
    steps = 4
    tile = hidden // steps
    specs = []
    shapes = []
    for one in others:
        dim = one.ndim - 2
        count = min(steps, one.shape[dim] // 8)
        block = one.shape[:dim] + (one.shape[dim] // count,) + one.shape[dim + 1 :]
        specs.append(
            pl.BlockSpec(block, lambda i, dim=dim, count=count: (0,) * dim + (jnp.minimum(i, count - 1), 0))
        )
        shapes.append(one.shape)
    return pl.pallas_call(
        widen_kernel,
        grid=(steps,),
        out_shape=[shaped((LAYERS, 1, hidden, D), f32)] * 3
        + [shaped(shapes[0], bf16)]
        + [shaped(shape, f32) for shape in shapes[1:]],
        in_specs=[pl.BlockSpec((tile, D), lambda i: (i, 0))] * (3 * LAYERS) + specs,
        out_specs=[pl.BlockSpec((LAYERS, 1, tile, D), lambda i: (0, 0, i, 0))] * 3 + specs,
        compiler_params=pltpu.CompilerParams(vmem_limit_bytes=vmem_bytes),
    )(*[one for layer in grads for one in layer], *others)


def local(tokens, cotangent, w_qkv, w_out, router, gains, rel_table, w_gate, w_up, w_down, routes, slots, segments):
    n = lax.axis_size("dp")
    own = D // n
    experts = router.shape[2]
    heads = rel_table.shape[2]
    width = w_qkv.shape[3]
    hidden = w_down.shape[2]
    cap = 3 * SEQ // n
    rows = 2 * LAYERS + LAYERS * experts + LAYERS * heads
    table_rows = rel_table.astype(bf16).transpose(0, 2, 1).reshape(LAYERS * heads, BUCKETS // n)
    small = jnp.concatenate(
        [
            gains.astype(bf16).reshape(2 * LAYERS, own),
            router.astype(bf16).transpose(0, 2, 1).reshape(LAYERS * experts, own),
            jnp.pad(table_rows, ((0, 0), (0, own - BUCKETS // n))),
        ]
    )
    small = jnp.pad(small, ((0, -rows % 16), (0, 0)))
    rows = small.shape[0]
    gate_t = w_gate.transpose(0, 1, 3, 2)
    up_t = w_up.transpose(0, 1, 3, 2)
    routes_row = routes.transpose(0, 2, 1)
    slots_row = slots.transpose(0, 2, 1)
    seg_row = segments.reshape(1, SEQ)
    index_ins = [
        named.routes_row(routes_row, vmem_spec),
        named.slots_row(slots_row, vmem_spec),
        named.seg_row(seg_row, vmem_spec),
    ]
    weight_ins = [named.gate_f(gate_t, any_spec), named.up_f(up_t, any_spec), named.down_f(w_down, any_spec)]
    attention_weights = [
        named.wqkv(pltpu.VMEM((3, D, width), bf16)),
        named.wo(pltpu.VMEM((D, width), bf16)),
        named.hg(pltpu.VMEM((SLICES, SEQ, HALF), bf16)),
    ]
    pieces = 5 + 2 * (LAYERS - 1)
    first = call(
        first_program(n, cap, experts, heads),
        [named.tok(tokens, vmem_spec), named.qkv(w_qkv, vmem_spec), named.out(w_out, vmem_spec), named.small(small, vmem_spec)]
        + index_ins
        + weight_ins,
        [
            named.wide((SLICES, rows, HALF), bf16, vmem_spec),
            named.tab((8, LANES), f32, vmem_spec),
            named.wqkv_out((3, D, width), bf16, any_spec),
            named.wo_out((D, width), bf16, any_spec),
            named.wqkv_next((3, D, width), bf16, any_spec),
            named.wo_next((D, width), bf16, any_spec),
            named.hg_out((SLICES, SEQ, HALF), bf16, any_spec),
        ]
        + attention_outs(width)
        + forward_outs(n, cap, hidden),
        attention_weights
        + attention_scratch
        + [
            named.small_all(pltpu.VMEM((n, rows, own), bf16)),
            named.qkv_low(pltpu.VMEM((LAYERS, 3, own, width), bf16)),
            named.out_low(pltpu.VMEM((LAYERS, own, width), bf16)),
            named.piece_send(pltpu.SemaphoreType.DMA((pieces, 2, n // 2))),
            named.piece_recv(pltpu.SemaphoreType.DMA((pieces, 2, n // 2))),
        ]
        + forward_scratch(n, cap, hidden, experts),
        0,
    )
    wide_ins = [named.wide(first.wide, vmem_spec), named.tab(first.tab, vmem_spec)]
    chunks, route_rows = Route.shape(n, cap)
    chunk_rows = pltpu.VMEM((chunks, route_rows, hidden), bf16)
    top = call(
        top_program(n, cap, experts, heads, 1),
        [
            named.h(first.y, vmem_spec),
            named.cot(cotangent, late_spec),
            named.wqkv_in(first.wqkv_next, any_spec),
            named.wo_in(first.wo_next, any_spec),
        ]
        + wide_ins
        + index_ins
        + weight_ins,
        [named.hg_out((SLICES, SEQ, HALF), bf16, any_spec), named.y((SEQ, HALF), f32, saved_spec)]
        + attention_outs(width)
        + backward_outs(n, cap, hidden, experts),
        attention_weights
        + attention_scratch
        + [
            named.gather(Gather.scratch),
            named.tiny_zero(Tiny.scratch(8, SEQ)),
            named.tiny_one(Tiny.scratch(8, SEQ)),
            named.tiny_two(Tiny.scratch(experts, SEQ)),
            named.tiny_three(Tiny.scratch(8, SEQ)),
            named.tiny_four(Tiny.scratch(8, SEQ)),
            named.weight_sems(pltpu.SemaphoreType.DMA((2,))),
            named.load_sems(pltpu.SemaphoreType.DMA((3,))),
            named.save_sems(pltpu.SemaphoreType.DMA((32,))),
            named.stage(pltpu.VMEM((hidden, D), f32)),
            named.wg(pltpu.VMEM((hidden, D), bf16)),
            named.wu(pltpu.VMEM((hidden, D), bf16)),
            named.wd(pltpu.VMEM((hidden, D), bf16)),
            named.inner(chunk_rows),
            named.act(chunk_rows),
            named.slope(chunk_rows),
            named.gpg(chunk_rows),
            named.upg(chunk_rows),
            named.mid(pltpu.VMEM((SEQ, HALF), f32)),
            named.normed(pltpu.VMEM((SEQ, HALF), bf16)),
            named.r2(pltpu.VMEM((SEQ, LANES), f32)),
            named.gates(pltpu.VMEM((SEQ, LANES), f32)),
            named.picked(pltpu.VMEM((2, SEQ, HALF), bf16)),
            named.dy(pltpu.VMEM((SEQ, HALF), f32)),
            named.pgs(pltpu.VMEM((2 * SEQ, HALF), bf16)),
            named.hot(pltpu.VMEM((2, SEQ, n * cap), bf16)),
            named.logit_g(pltpu.VMEM((experts, SEQ), f32)),
            named.targ_row(pltpu.VMEM((2, SEQ), jnp.int32)),
            named.targ_col(pltpu.VMEM((SEQ, LANES), jnp.int32)),
            named.route(Route.scratch(n, cap, 2)),
        ],
        1,
    )

    def kept_of(state, wqkv, wo, h):
        return types.SimpleNamespace(
            ctx=state.ctx, proj=state.proj, lse=state.lse, r1=state.r1, hg=state.hg_out, wqkv=wqkv, wo=wo, h=h
        )

    gradient_scratch = [named.wog(pltpu.VMEM((D, width), bf16)), named.qkvg(pltpu.VMEM((3, D, width), bf16))]
    fourth = call(
        back_program(n, cap, experts, heads, 0),
        wide_ins
        + index_ins
        + attention_back_ins(kept_of(top, first.wqkv_next, first.wo_next, first.y), top.midg)
        + backward_ins(first),
        backward_outs(n, cap, hidden, experts)
        + [
            named.qkv_sums((n // 2, 3, own, width), bf16, saved_spec),
            named.out_sums((n // 2, own, width), bf16, saved_spec),
            named.table((8, LANES), f32, vmem_spec),
        ],
        gradient_scratch
        + [
            named.near_a(Scatter.near_scratch(n, (3, own, width))),
            named.near_b(Scatter.near_scratch(n, (own, width))),
        ]
        + attention_back_scratch(width, heads)
        + backward_scratch(n, cap, hidden, experts),
        3,
    )
    pack_rows = 16 + LAYERS * experts
    big, less = (3, own, width), (own, width)
    scatter_scratch = [
        named.far_a(Scatter.far_scratch(n, big)),
        named.far_b(Scatter.far_scratch(n, less)),
        named.near_c(Scatter.near_scratch(n, big)),
        named.near_d(Scatter.near_scratch(n, less)),
        named.far_c(Scatter.far_scratch(n, big)),
        named.far_d(Scatter.far_scratch(n, less)),
        named.qkv_sums(pltpu.VMEM((n // 2,) + big, bf16)),
        named.out_sums(pltpu.VMEM((n // 2,) + less, bf16)),
    ]
    final = call(
        final_program(n, experts, heads),
        wide_ins
        + index_ins[2:]
        + attention_back_ins(kept_of(first, first.wqkv_out, first.wo_out, tokens), fourth.midg)
        + [
            named.qkv_sums_next(fourth.qkv_sums, vmem_spec),
            named.out_sums_next(fourth.out_sums, vmem_spec),
            named.y_last(top.y, late_spec),
            named.gain_rows_0(fourth.gain_rows, vmem_spec),
            named.gain_rows_1(top.gain_rows, vmem_spec),
            named.router_g_0(fourth.router_g, vmem_spec),
            named.router_g_1(top.router_g, vmem_spec),
            named.table_next(fourth.table, vmem_spec),
        ],
        [
            named.output((SEQ, D), bf16, any_spec),
            named.dx_full((SEQ, D), bf16, any_spec),
            named.qkv_grad((LAYERS, 3, own, width), f32, vmem_spec),
            named.out_grad((LAYERS, own, width), f32, vmem_spec),
            named.small_out((SLICES, pack_rows, HALF), f32, vmem_spec),
        ],
        gradient_scratch
        + attention_back_scratch(width, heads)
        + scatter_scratch
        + [
            named.table(pltpu.VMEM((8, LANES), f32)),
            named.output_buf(pltpu.VMEM((SLICES, SEQ, HALF), bf16)),
            named.output_gather(Gather.scratch),
            named.dx_buf(pltpu.VMEM((SLICES, SEQ, HALF), bf16)),
            named.dx_gather(Gather.scratch),
            named.pack(pltpu.VMEM((pack_rows, HALF), f32)),
            named.packs(pltpu.VMEM((n, pack_rows, HALF), f32)),
            named.pack_send(pltpu.SemaphoreType.DMA((n,))),
            named.pack_recv(pltpu.SemaphoreType.DMA((n,))),
            named.all_send(pltpu.SemaphoreType.DMA((3,))),
            named.all_recv(pltpu.SemaphoreType.DMA((3,))),
            named.save_sems(pltpu.SemaphoreType.DMA((32,))),
        ],
        4,
    )
    grads = [[one.wg_grad, one.wu_grad, one.wd_grad] for one in (fourth, top)]
    gate_g, up_g, down_g, output, dx_wide, qkv_grad, out_grad = widen(
        grads, [final.output, final.dx_full, final.qkv_grad, final.out_grad]
    )
    d, t = lax.axis_index("dp"), lax.axis_index("tensor")
    small_sum = final.small_out

    def rows_wide(start, count):
        wide = small_sum[:, start : start + count].transpose(1, 0, 2).reshape(count, D)
        return lax.dynamic_slice_in_dim(wide, d * own, own, 1)

    gains_grad = rows_wide(0, 2 * LAYERS).reshape(LAYERS, 2, own)
    router_grad = rows_wide(16, LAYERS * experts).reshape(LAYERS, experts, own).transpose(0, 2, 1)
    table_all = lax.dynamic_slice_in_dim(small_sum, t, 1, 0)[0, 8 : 8 + heads].reshape(heads, LAYERS, LANES)
    table_grad = lax.dynamic_slice_in_dim(table_all, d * (BUCKETS // n), BUCKETS // n, 2).transpose(1, 2, 0)
    return (
        output,
        dx_wide,
        qkv_grad,
        out_grad,
        router_grad,
        gains_grad,
        table_grad,
        gate_g.transpose(0, 1, 3, 2),
        up_g.transpose(0, 1, 3, 2),
        down_g,
    )


def solution(mesh):
    placed = (
        P("dp", None),
        P("dp", None),
        P(None, None, "dp", "tensor"),
        P(None, "dp", "tensor"),
        P(None, "dp", None),
        P(None, None, "dp"),
        P(None, "dp", "tensor"),
        P(None, "dp", None, "tensor"),
        P(None, "dp", None, "tensor"),
        P(None, "dp", "tensor", None),
        P(None, "dp", None),
        P(None, "dp", None),
        P("dp"),
    )
    return jax.shard_map(
        local,
        mesh=mesh,
        in_specs=placed,
        out_specs=(P("dp", None), P("dp", None)) + placed[2:10],
        check_vma=False,
    )
```

```python
import types

import jax
import jax.numpy as jnp
from jax import lax
from jax.experimental import pallas as pl
from jax.experimental.pallas import tpu as pltpu
from jax.sharding import PartitionSpec as P

D = 1024
HDIM = 64
SEQ = 512
LAYERS = 2
BUCKETS = 32
HALF = 256
SLICES = 4
WINDOW_CHUNKS = 2
STAGE_LAGS = (1, 2, 3, 4)
LANES = 128
WINDOW = 768

eps_norm = 1e-06
rise_points = (12, 16, 23, 32, 46, 64, 91)
masked_score = -1e30
vmem_bytes = 63 * 1024 * 1024
f32 = jnp.float32
bf16 = jnp.bfloat16
MESH = pl.DeviceIdType.MESH
nn_dims = (((1,), (0,)), ((), ()))
nt_dims = (((1,), (1,)), ((), ()))
tn_dims = (((0,), (0,)), ((), ()))
vmem_spec = pl.BlockSpec(memory_space=pltpu.VMEM)
any_spec = pl.BlockSpec(memory_space=pl.ANY)
late_spec = pl.BlockSpec(memory_space=pl.ANY)
saved_spec = pl.BlockSpec(memory_space=pl.ANY)


def nn(a, b):
    return lax.dot_general(a, b, nn_dims, preferred_element_type=f32)


def nt(a, b):
    return lax.dot_general(a, b, nt_dims, preferred_element_type=f32)


def tn(a, b):
    return lax.dot_general(a, b, tn_dims, preferred_element_type=f32)


def shaped(shape, kind):
    return jax.ShapeDtypeStruct(shape, kind)


def bucket_index(offset):
    upward = jnp.where(offset > 0, BUCKETS // 2, 0)
    distance = jnp.abs(offset)
    far_part = 8 + sum(((distance >= rise_point).astype(jnp.int32) for rise_point in rise_points))
    return upward + jnp.where(distance < 8, distance, far_part)


def toeplitz_bias(row):
    tile = jnp.broadcast_to(row, (HALF, WINDOW))
    rolled = pltpu.roll(tile, WINDOW - HALF + 1, 1, stride=1, stride_axis=0)
    return rolled[:, : 2 * HALF]


def diagonal_sums(grad):
    rows = jnp.concatenate([grad, jnp.zeros((HALF, WINDOW - 2 * HALF), f32)], axis=1)
    count = HALF
    while count > 8:
        count //= 2
        rows = rows[:count] + pltpu.roll(rows[count:], WINDOW - count, 1)
    total = jnp.zeros((8, WINDOW), f32)
    place = lax.broadcasted_iota(jnp.int32, (8, WINDOW), 0)
    for i in range(8):
        moved = pltpu.roll(rows, (HALF - 1 - i) % WINDOW, 1)
        total = total + jnp.where(place == i, moved, 0.0)
    return total


def half_lanes(shape, which):
    lane = lax.broadcasted_iota(jnp.int32, shape, 1)
    return (lane < HDIM) if which == 0 else (lane >= HDIM)


def allowed_tile(seg_col, seg_row):
    i = lax.broadcasted_iota(jnp.int32, (HALF, HALF), 0)
    j = lax.broadcasted_iota(jnp.int32, (HALF, HALF), 1)
    return (j <= i) | ((seg_col == seg_row) & (seg_col > 0))


def masked_scores(query, keys, bias, allowed, block):
    raw = nt(query, keys)
    if block == 0:
        return jnp.where(allowed, raw + bias[:, HALF:], masked_score)
    left = raw[:, :HALF] + bias[:, :HALF]
    right = jnp.where(allowed, raw[:, HALF:] + bias[:, HALF:], masked_score)
    return jnp.concatenate([left, right], axis=1)


def bias_rows(table):
    place = lax.broadcasted_iota(jnp.int32, (BUCKETS, WINDOW), 1) - (SEQ - 1)
    hot = (bucket_index(place) == lax.broadcasted_iota(jnp.int32, (BUCKETS, WINDOW), 0)).astype(bf16)
    return nn(table, hot)


def block_rows(block):
    return slice(block * HALF, (block + 1) * HALF)


def attend_block(m, block, first_head):
    width = m.ctx.shape[1]
    rows = block_rows(block)
    count = (block + 1) * HALF
    lane = lax.broadcasted_iota(jnp.int32, (HALF, LANES), 1)
    allowed = allowed_tile(m.seg_col[rows, :1], m.seg_row[:, rows])
    lse = jnp.zeros((HALF, LANES), f32)
    for pair in range(width // LANES):
        cols = slice(pair * LANES, (pair + 1) * LANES)
        q2 = m.proj[rows, cols]
        k2 = m.proj[:count, width + pair * LANES : width + (pair + 1) * LANES]
        v2 = m.proj[:count, 2 * width + pair * LANES : 2 * width + (pair + 1) * LANES]
        outs = []
        for which in range(2):
            head = 2 * pair + which
            scaled = q2 * jnp.asarray(HDIM**-0.5, bf16)
            qm = jnp.where(half_lanes(q2.shape, which), scaled, jnp.zeros_like(q2))
            bias = toeplitz_bias(m.bias[first_head + head : first_head + head + 1])
            scores = masked_scores(qm, k2, bias, allowed, block)
            top = jnp.max(scores, axis=1, keepdims=True)
            powers = jnp.exp(scores - top)
            total = jnp.sum(powers, axis=1, keepdims=True)
            probs = (powers * (1.0 / total)).astype(bf16)
            outs.append(nn(probs, v2))
            lse = jnp.where(lane == head, top + jnp.log(total), lse)
        m.ctx[rows, cols] = jnp.where(half_lanes(outs[0].shape, 0), outs[0], outs[1]).astype(bf16)
    m.lse[rows, :] = lse


def wide_rows(ref, rows):
    return jnp.concatenate([ref[q, rows] for q in range(SLICES)], axis=1)


def project(m, block, c):
    width = m.ctx.shape[1]
    rows = block_rows(block)
    m.proj[rows, c * width : (c + 1) * width] = (
        nn(wide_rows(m.hg, rows), m.wqkv[c]) * m.r1[rows, :1]
    ).astype(bf16)


def project_out(m, block):
    rows = block_rows(block)
    for q in range(SLICES):
        m.part[q, rows] = nt(m.ctx[rows], m.wo[q * HALF : (q + 1) * HALF, :]).astype(bf16)


def attention_block(m, block, first_head, between):
    for c in range(3):
        project(m, block, c)
    between()
    attend_block(m, block, first_head)
    project_out(m, block)


def prob_cols(block):
    return slice(0, HALF) if block == 0 else slice(HALF, 3 * HALF)


def attention_probs(m, block, first_head):
    width = m.ctx.shape[1]
    rows = block_rows(block)
    count = (block + 1) * HALF
    allowed = allowed_tile(m.seg_col[rows, :1], m.seg_row[:, rows])
    scale = jnp.asarray(HDIM**-0.5, bf16)
    for head in range(width // HDIM):
        pair, which = head // 2, head % 2
        q2 = m.proj[rows, pair * LANES : (pair + 1) * LANES]
        k2 = m.proj[:count, width + pair * LANES : width + (pair + 1) * LANES]
        qm = jnp.where(half_lanes(q2.shape, which), q2 * scale, jnp.zeros_like(q2))
        bias = toeplitz_bias(m.bias[first_head + head : first_head + head + 1])
        scores = masked_scores(qm, k2, bias, allowed, block)
        m.probs[head, :, prob_cols(block)] = jnp.exp(scores - m.lse[rows, head : head + 1])


def attention_back_block(m, block, between):
    width = m.ctx.shape[1]
    rows = block_rows(block)
    count = (block + 1) * HALF
    dctx = nn(wide_rows(m.ag, rows), m.wo[...]).astype(bf16)
    scale = jnp.asarray(HDIM**-0.5, bf16)
    for pair in range(width // LANES):
        if pair == 1:
            between()
        cols = slice(pair * LANES, (pair + 1) * LANES)
        q2 = m.proj[rows, cols]
        k2 = m.proj[:count, width + pair * LANES : width + (pair + 1) * LANES]
        v2 = m.proj[:count, 2 * width + pair * LANES : 2 * width + (pair + 1) * LANES]
        g2 = dctx[:, cols]
        outs = []
        dk = None
        dv = None
        for which in range(2):
            head = 2 * pair + which
            mine = half_lanes(q2.shape, which)
            qm = jnp.where(mine, q2 * scale, jnp.zeros_like(q2))
            gm = jnp.where(mine, g2, jnp.zeros_like(g2))
            probs = m.probs[head, :, prob_cols(block)]
            prob_grad = nt(gm, v2).astype(bf16).astype(f32)
            inner = jnp.sum(probs * prob_grad, axis=1, keepdims=True)
            grad_low = (probs * (prob_grad - inner)).astype(bf16)
            dv_one = tn(probs.astype(bf16), gm)
            dk_one = tn(grad_low, qm)
            dv = dv_one if dv is None else dv + dv_one
            dk = dk_one if dk is None else dk + dk_one
            outs.append(nn(grad_low, k2))
            wide = grad_low.astype(f32)
            if block == 1:
                m.bias_grad[head] = wide
            else:
                m.bias_grad[head, :, HALF:] = m.bias_grad[head, :, HALF:] + wide
        dq = jnp.where(half_lanes(outs[0].shape, 0), outs[0], outs[1]) * HDIM**-0.5
        if block == 1:
            m.dk[:, cols] = dk
            m.dv[:, cols] = dv
        else:
            m.dk[:HALF, cols] = m.dk[:HALF, cols] + dk
            m.dv[:HALF, cols] = m.dv[:HALF, cols] + dv
        m.pg[rows, cols] = dq.astype(bf16)
        m.pg[rows, width + pair * LANES : width + (pair + 1) * LANES] = m.dk[rows, cols].astype(bf16)
        m.pg[rows, 2 * width + pair * LANES : 2 * width + (pair + 1) * LANES] = m.dv[rows, cols].astype(bf16)
    dots = None
    for q in range(SLICES):
        total = None
        for c in range(3):
            one = nt(m.pg[rows, c * width : (c + 1) * width], m.wqkv[c, q * HALF : (q + 1) * HALF, :])
            total = one if total is None else total + one
        m.part[q, rows] = total.astype(bf16)
        product = jnp.sum(total * m.hg[q, rows].astype(f32), axis=1, keepdims=True)
        dots = product if dots is None else dots + product
    return dots


def table_gradient(m):
    place = lax.broadcasted_iota(jnp.int32, (8, WINDOW), 0)
    diag_all = jnp.zeros((8, WINDOW), f32)
    for head in range(m.bias_grad.shape[0]):
        sums = jnp.sum(diagonal_sums(m.bias_grad[head]), axis=0, keepdims=True)
        diag_all = jnp.where(place == head, sums, diag_all)
    spot = lax.broadcasted_iota(jnp.int32, (WINDOW, LANES), 0) - (SEQ - 1)
    hot = (bucket_index(spot) == lax.broadcasted_iota(jnp.int32, (WINDOW, LANES), 1)).astype(f32)
    return lax.dot_general(
        diag_all, hot, nn_dims, precision=lax.Precision.HIGHEST, preferred_element_type=f32
    )


def out_gradient(m):
    for q in range(SLICES):
        m.wog[q * HALF : (q + 1) * HALF] = tn(m.ag[q], m.ctx[...]).astype(bf16)


def qkv_gradient(m):
    width = m.ctx.shape[1]
    for q in range(SLICES):
        normed = (m.hg[q].astype(f32) * m.r1[:, :1]).astype(bf16)
        for c in range(3):
            m.qkvg[c, q * HALF : (q + 1) * HALF] = tn(normed, m.pg[:, c * width : (c + 1) * width]).astype(bf16)


def places():
    d = lax.axis_index("dp")
    t = lax.axis_index("tensor")
    sib = t + 1 - 2 * lax.rem(t, 2)
    far = lax.rem(t + 2, SLICES)
    opp = SLICES - 1 - t
    return d, t, sib, far, opp


def remote(src, dst, send, recv, device):
    return pltpu.make_async_remote_copy(
        src_ref=src, dst_ref=dst, send_sem=send, recv_sem=recv, device_id=device, device_id_type=MESH
    )


def greet(n, with_dp):
    d, t, sib, far, opp = places()
    barrier = pltpu.get_barrier_semaphore()
    for peer in (sib, far, opp):
        pl.semaphore_signal(barrier, inc=1, device_id=(d, peer), device_id_type=MESH)
    if with_dp:

        def hello(j, carry):
            pl.semaphore_signal(barrier, inc=1, device_id=(lax.rem(d + j, n), t), device_id_type=MESH)
            return carry

        lax.fori_loop(1, n, hello, 0)
    pl.semaphore_wait(barrier, 3 + (n - 1 if with_dp else 0))


class Tiny:
    scratch = lambda rows, cols: [
        pltpu.VMEM((SLICES, rows, cols), f32),
        pltpu.SemaphoreType.DMA((3,)),
        pltpu.SemaphoreType.DMA((3,)),
    ]

    def __init__(self, refs):
        self.buf, self.send, self.recv = refs

    def copies(self):
        d, t, sib, far, opp = places()
        return [
            remote(self.buf.at[t], self.buf.at[t], self.send.at[i], self.recv.at[i], (d, peer))
            for i, peer in enumerate((sib, far, opp))
        ]

    def start(self, tile):
        d, t, sib, far, opp = places()
        self.buf[t] = tile
        for copy in self.copies():
            copy.start()

    def finish(self):
        for copy in self.copies():
            copy.wait()

    def total(self):
        self.finish()
        return (self.buf[0] + self.buf[1]) + (self.buf[2] + self.buf[3])


class Gather:
    scratch = [pltpu.SemaphoreType.DMA((2, 3)), pltpu.SemaphoreType.DMA((2, 3))]

    def __init__(self, buf, refs):
        self.buf = buf
        self.send, self.recv = refs

    def copies(self, b):
        d, t, sib, far, opp = places()
        rows = pl.ds(b * HALF, HALF)
        mine, others = self.buf.at[t, rows], self.buf.at[far, rows]
        return [
            lambda: remote(mine, mine, self.send.at[b, 0], self.recv.at[b, 0], (d, far)),
            lambda: remote(mine, mine, self.send.at[b, 1], self.recv.at[b, 1], (d, sib)),
            lambda: remote(others, others, self.send.at[b, 2], self.recv.at[b, 2], (d, sib)),
        ]

    def start(self, b, tile):
        d, t, sib, far, opp = places()
        self.buf[t, pl.ds(b * HALF, HALF)] = tile
        far_copy, near_copy, pass_copy = self.copies(b)
        far_copy().start()
        near_copy().start()

    def forward(self, b):
        far_copy, near_copy, pass_copy = self.copies(b)
        far_copy().wait_recv()
        pass_copy().start()

    def finish(self, b):
        far_copy, near_copy, pass_copy = self.copies(b)
        near_copy().wait_recv()
        pass_copy().wait_recv()

    def wait_sends(self):
        for b in range(2):
            for copy in self.copies(b):
                copy().wait_send()


class Reduce:
    scratch = [
        pltpu.VMEM((2, SEQ, HALF), bf16),
        pltpu.VMEM((2, SEQ, HALF), bf16),
        pltpu.SemaphoreType.DMA((2, 3)),
        pltpu.SemaphoreType.DMA((2, 3)),
    ]

    def __init__(self, part, refs):
        self.part = part
        self.near, self.across, self.send, self.recv = refs

    def copies(self, b):
        d, t, sib, far, opp = places()
        rows = pl.ds(b * HALF, HALF)

        def one(i, src, dst, peer):
            return lambda: remote(src, dst, self.send.at[b, i], self.recv.at[b, i], (d, peer))

        return [
            one(0, self.part.at[opp, rows], self.near.at[1, rows], sib),
            one(1, self.part.at[sib, rows], self.near.at[0, rows], sib),
            one(2, self.across.at[0, rows], self.across.at[1, rows], far),
        ]

    def start(self, b):
        first, second, third = self.copies(b)
        first().start()
        second().start()

    def middle(self, b):
        d, t, sib, far, opp = places()
        rows = pl.ds(b * HALF, HALF)
        first, second, third = self.copies(b)
        first().wait_recv()
        self.across[0, rows] = (self.part[far, rows].astype(f32) + self.near[1, rows].astype(f32)).astype(bf16)
        third().start()

    def finish(self, b):
        d, t, sib, far, opp = places()
        rows = pl.ds(b * HALF, HALF)
        first, second, third = self.copies(b)
        second().wait_recv()
        mine = self.part[t, rows].astype(f32) + self.near[0, rows].astype(f32)
        third().wait_recv()
        return mine + self.across[1, rows].astype(f32)

    def wait_sends(self):
        for b in range(2):
            for copy in self.copies(b):
                copy().wait_send()


class Saves:
    def __init__(self, sems):
        self.sems, self.copies = sems, []

    def start(self, src, dst, span=None):
        place = len(self.copies)

        def copy():
            if span is None:
                return pltpu.make_async_copy(src, dst, self.sems.at[place])
            return pltpu.make_async_copy(src.at[span], dst.at[span], self.sems.at[place])

        copy().start()
        self.copies.append(copy)

    def wait(self):
        for copy in self.copies:
            copy().wait()


def to_row(col):
    return jnp.transpose(jnp.broadcast_to(col, (col.shape[0], LANES)))[:8]


def to_cols(rows8):
    return jnp.transpose(jnp.concatenate([rows8] * (LANES // 8), axis=0))


def int_cols(rows):
    whole = jnp.concatenate([rows.astype(f32)] * (8 // rows.shape[0]), axis=0)
    return to_cols(whole).astype(jnp.int32)


def pick_slice(wide):
    t = lax.axis_index("tensor")
    out = wide[:, :HALF]
    for q in range(1, SLICES):
        out = jnp.where(t == q, wide[:, q * HALF : (q + 1) * HALF], out)
    return out


def hot_columns(targ, k, count):
    return (targ[:, k : k + 1] == lax.broadcasted_iota(jnp.int32, (SEQ, count), 1)).astype(f32).astype(bf16)


class Route:
    @staticmethod
    def piece(cap):
        return 32 if cap % 32 == 0 else 16

    @staticmethod
    def shape(n, cap):
        piece = Route.piece(cap)
        return cap // piece, n * piece

    @staticmethod
    def slots(chunks, rounds):
        return chunks if rounds == 1 else max(chunks, STAGE_LAGS[3] + 1)

    @staticmethod
    def scratch(n, cap, rounds):
        chunks, rows = Route.shape(n, cap)
        slots = Route.slots(chunks, rounds)
        total = chunks * rounds
        return [
            pltpu.VMEM((total, rows, HALF), bf16),
            pltpu.VMEM((total, SLICES, rows, HALF), bf16),
            pltpu.VMEM((slots, SLICES, rows, HALF), bf16),
            pltpu.VMEM((slots, 2, rows, HALF), bf16),
            pltpu.VMEM((slots, rows, HALF), bf16),
            pltpu.VMEM((slots, rows, HALF), bf16),
            pltpu.VMEM((slots, rows, HALF), bf16),
            pltpu.VMEM((total, rows, HALF), bf16),
            pltpu.SemaphoreType.DMA((total, n)),
            pltpu.SemaphoreType.DMA((total, n)),
            pltpu.SemaphoreType.DMA((3, total)),
            pltpu.SemaphoreType.DMA((3, total)),
            pltpu.SemaphoreType.DMA((3, total)),
            pltpu.SemaphoreType.DMA((3, total)),
            pltpu.SemaphoreType.DMA((total, n)),
            pltpu.SemaphoreType.DMA((total, n)),
        ]

    def __init__(self, n, cap, rounds, refs):
        self.n = n
        self.size = Route.piece(cap)
        self.chunks, self.rows = Route.shape(n, cap)
        self.slot_count = Route.slots(self.chunks, rounds)
        self.total = self.chunks * rounds
        (
            self.out,
            self.x,
            self.p,
            self.ra,
            self.sb,
            self.rb,
            self.ro,
            self.ret,
            self.as_,
            self.ar,
            self.fs,
            self.fr,
            self.ps,
            self.pr,
            self.rs,
            self.rr,
        ) = refs

    def span(self, place):
        return pl.ds(pl.multiple_of(place * self.size, 16), self.size)

    def peers(self, action):
        d = lax.axis_index("dp")

        def one(j, carry):
            action(lax.rem(d + j, self.n))
            return carry

        lax.fori_loop(1, self.n, one, 0)

    def out_copy(self, chunk, source, expert):
        d, t, sib, far, opp = places()
        return remote(
            self.out.at[chunk, self.span(expert)],
            self.x.at[chunk, t, self.span(source)],
            self.as_.at[chunk, expert],
            self.ar.at[chunk, source],
            (expert, t),
        )

    def back_copy(self, chunk, source, expert):
        d, t, sib, far, opp = places()
        return remote(
            self.ro.at[self.slot(chunk), self.span(source)],
            self.ret.at[chunk, self.span(expert)],
            self.rs.at[chunk, source],
            self.rr.at[chunk, expert],
            (source, t),
        )

    def spread_copies(self, chunk):
        d, t, sib, far, opp = places()
        mine, others = self.x.at[chunk, t], self.x.at[chunk, far]
        return [
            lambda: remote(mine, mine, self.fs.at[0, chunk], self.fr.at[0, chunk], (d, far)),
            lambda: remote(mine, mine, self.fs.at[1, chunk], self.fr.at[1, chunk], (d, sib)),
            lambda: remote(others, others, self.fs.at[2, chunk], self.fr.at[2, chunk], (d, sib)),
        ]

    def slot(self, chunk):
        return chunk if self.slot_count == self.total else lax.rem(chunk, self.slot_count)

    def reused(self, chunk, action):
        if self.slot_count < self.total:

            @pl.when(chunk >= self.slot_count)
            def _():
                action(chunk - self.slot_count)

    def sum_copies(self, chunk):
        d, t, sib, far, opp = places()
        p, ps, pr = self.p, self.ps, self.pr
        slot = self.slot(chunk)
        return [
            lambda: remote(p.at[slot, opp], self.ra.at[slot, 1], ps.at[0, chunk], pr.at[0, chunk], (d, sib)),
            lambda: remote(p.at[slot, sib], self.ra.at[slot, 0], ps.at[1, chunk], pr.at[1, chunk], (d, sib)),
            lambda: remote(self.sb.at[slot], self.rb.at[slot], ps.at[2, chunk], pr.at[2, chunk], (d, far)),
        ]

    def send(self, chunk, fill):
        d, t, sib, far, opp = places()
        fill(chunk)
        self.peers(lambda e: self.out_copy(chunk, d, e).start())
        self.x[chunk, t, self.span(d)] = self.out[chunk, self.span(d)]

    def begin(self, fill_first, fill):
        self.fill = fill
        for chunk in range(WINDOW_CHUNKS):
            self.send(chunk, fill_first)

    def put(self, chunk, products):
        for q in range(SLICES):
            self.p[self.slot(chunk), q] = products[:, q * HALF : (q + 1) * HALF].astype(bf16)

    def run(self, compute, hook):
        d, t, sib, far, opp = places()

        def more(chunk):
            self.send(chunk, self.fill)

        def arrive(chunk):
            self.peers(lambda s: self.out_copy(chunk, s, s).wait_recv())
            far_copy, near_copy, pass_copy = self.spread_copies(chunk)
            far_copy().start()
            near_copy().start()

        def forward(chunk):
            far_copy, near_copy, pass_copy = self.spread_copies(chunk)
            far_copy().wait_recv()
            pass_copy().start()

        def work(chunk):
            far_copy, near_copy, pass_copy = self.spread_copies(chunk)
            near_copy().wait_recv()
            pass_copy().wait_recv()
            rows = jnp.concatenate([self.x[chunk, q] for q in range(SLICES)], axis=1)

            def sent(old):
                first, second, third = self.sum_copies(old)
                first().wait_send()
                second().wait_send()

            self.reused(chunk, sent)
            compute(chunk, rows)
            first, second, third = self.sum_copies(chunk)
            first().start()
            second().start()

        def add_near(chunk):
            first, second, third = self.sum_copies(chunk)
            first().wait_recv()
            slot = self.slot(chunk)
            self.reused(chunk, lambda old: self.sum_copies(old)[2]().wait_send())
            self.sb[slot] = (self.p[slot, far].astype(f32) + self.ra[slot, 1].astype(f32)).astype(bf16)
            third().start()

        def add_far(chunk):
            first, second, third = self.sum_copies(chunk)
            second().wait_recv()
            third().wait_recv()
            slot = self.slot(chunk)
            self.reused(chunk, lambda old: self.peers(lambda s: self.back_copy(old, s, d).wait_send()))
            mine = self.p[slot, t].astype(f32) + self.ra[slot, 0].astype(f32)
            self.ro[slot] = (mine + self.rb[slot].astype(f32)).astype(bf16)
            self.peers(lambda s: self.back_copy(chunk, s, d).start())
            self.ret[chunk, self.span(d)] = self.ro[slot, self.span(d)]

        stages = (
            (more, -WINDOW_CHUNKS),
            (arrive, 0),
            (forward, STAGE_LAGS[0]),
            (work, STAGE_LAGS[1]),
            (add_near, STAGE_LAGS[2]),
            (add_far, STAGE_LAGS[3]),
        )

        def step(i, carry):
            for stage, lag in stages:

                @pl.when((i >= lag) & (i < self.total + lag))
                def _(stage=stage, lag=lag):
                    stage(i - lag)

            if hook is not None:
                hook(i)
            return carry

        lax.fori_loop(0, self.total + stages[-1][1], step, 0)

    def wait_back(self, first):
        d = lax.axis_index("dp")

        def one(chunk, carry):
            self.peers(lambda e: self.back_copy(chunk, d, e).wait_recv())
            return carry

        lax.fori_loop(first, first + self.chunks, one, 0)

    def returned(self, first):
        return self.ret[first : first + self.chunks].reshape(self.chunks * self.rows, HALF)

    def arrived(self, first, q):
        return self.x[first : first + self.chunks, q].reshape(self.chunks * self.rows, HALF)

    def wait_sends(self):
        d = lax.axis_index("dp")

        def one(chunk, carry):
            self.peers(lambda e: self.out_copy(chunk, d, e).wait_send())
            for copy in self.spread_copies(chunk):
                copy().wait_send()
            return carry

        lax.fori_loop(0, self.total, one, 0)

        def two(chunk, carry):
            self.peers(lambda e: self.back_copy(chunk, e, d).wait_send())
            for copy in self.sum_copies(chunk):
                copy().wait_send()
            return carry

        lax.fori_loop(self.total - self.slot_count, self.total, two, 0)


gelu_c = 0.7978845608028654
gelu_a = 0.044715


class Named:
    def __getattr__(self, name):
        return lambda *rest: (name, *rest)


named = Named()


def call(fn, ins, outs, scratch, collective_id):
    late = [one for one in ins if one[2] is late_spec]
    saved = [one for one in outs if one[3] is saved_spec]

    def kernel(*refs):
        refs = list(refs)
        m = types.SimpleNamespace(outs=types.SimpleNamespace())
        late_refs = []
        for one in ins:
            ref = refs.pop(0)
            if one[2] is late_spec:
                late_refs.append(ref)
            else:
                setattr(m, one[0], ref)
        for one in outs:
            setattr(m.outs if one[3] is saved_spec else m, one[0], refs.pop(0))
        copies = []
        if late:
            sems = refs.pop(0)
            for i, one in enumerate(late):
                buffer = refs.pop(0)
                setattr(m, one[0], buffer)
                copies.append(pltpu.make_async_copy(late_refs[i], buffer, sems.at[i]))
        for one in saved:
            setattr(m, one[0], refs.pop(0))
        for name, kinds in scratch:
            if isinstance(kinds, list):
                setattr(m, name, [refs.pop(0) for one in kinds])
            else:
                setattr(m, name, refs.pop(0))

        def late_wait():
            for copy in copies:
                copy.wait()

        m.late_wait = late_wait
        for copy in copies:
            copy.start()
        fn(m)

    flat = []
    if late:
        flat.append(pltpu.SemaphoreType.DMA((len(late),)))
        flat += [pltpu.VMEM(one[1].shape, one[1].dtype) for one in late]
    flat += [pltpu.VMEM(one[1], one[2]) for one in saved]
    for name, kinds in scratch:
        flat += kinds if isinstance(kinds, list) else [kinds]
    results = pl.pallas_call(
        kernel,
        name=fn.__name__,
        out_shape=[shaped(one[1], one[2]) for one in outs],
        in_specs=[one[2] for one in ins],
        out_specs=[one[3] for one in outs],
        scratch_shapes=flat,
        compiler_params=pltpu.CompilerParams(
            vmem_limit_bytes=vmem_bytes, collective_id=collective_id, has_side_effects=True
        ),
    )(*[one[1] for one in ins])
    return types.SimpleNamespace(**{one[0]: result for one, result in zip(outs, results)})


def gain_of(m, layer, which):
    t = lax.axis_index("tensor")
    return m.wide[t, 2 * layer + which : 2 * layer + which + 1].astype(f32)


def router_of(m, layer, experts):
    t = lax.axis_index("tensor")
    start = 2 * LAYERS + layer * experts
    return m.wide[t][start : start + experts]


def cap_count(cap):
    return 3 * SEQ // cap


def save_attention(m, saves):
    for buffer, out in ((m.proj, m.outs.proj), (m.lse, m.outs.lse), (m.ctx, m.outs.ctx), (m.r1, m.outs.r1)):
        saves.start(buffer, out)


def set_targets(m, layer, cap):
    piece = Route.piece(cap)
    chunks, rows = Route.shape(cap_count(cap), cap)
    slots = m.slots_row[layer]
    m.targ_row[...] = (slots // piece) * rows + m.routes_row[layer] * piece + lax.rem(slots, piece)
    m.targ_col[...] = int_cols(m.targ_row[...])


def set_attention_tables(m):
    m.seg_col[...] = int_cols(m.seg_row[...])
    m.bias[...] = bias_rows(m.tab[:, :BUCKETS].astype(bf16))


attention_scratch = [
    named.seg_col(pltpu.VMEM((SEQ, LANES), jnp.int32)),
    named.bias(pltpu.VMEM((8, WINDOW), f32)),
    named.part(pltpu.VMEM((SLICES, SEQ, HALF), bf16)),
    named.reduce(Reduce.scratch),
]


def attention_outs(width):
    return [
        named.proj((SEQ, 3 * width), bf16, saved_spec),
        named.lse((SEQ, LANES), f32, saved_spec),
        named.ctx((SEQ, width), bf16, saved_spec),
        named.r1((SEQ, LANES), f32, saved_spec),
    ]


def forward_outs(n, cap, hidden):
    chunks, rows = Route.shape(n, cap)
    return [
        named.mid((SEQ, HALF), f32, saved_spec),
        named.normed((SEQ, HALF), bf16, saved_spec),
        named.r2((SEQ, LANES), f32, saved_spec),
        named.gates((SEQ, LANES), f32, saved_spec),
        named.picked((2, SEQ, HALF), bf16, saved_spec),
        named.y((SEQ, HALF), f32, saved_spec),
        named.x_out((chunks, SLICES, rows, HALF), bf16, any_spec),
        named.inner_out((chunks, rows, hidden), bf16, any_spec),
        named.act_out((chunks, rows, hidden), bf16, any_spec),
        named.slope_out((chunks, rows, hidden), bf16, any_spec),
        named.wg_out((hidden, D), bf16, any_spec),
        named.wu_out((hidden, D), bf16, any_spec),
        named.wd_out((hidden, D), bf16, any_spec),
    ]


def forward_scratch(n, cap, hidden, experts):
    chunks, rows = Route.shape(n, cap)
    return [
        named.wg_stage(pltpu.VMEM((hidden, D), f32)),
        named.wu_stage(pltpu.VMEM((hidden, D), f32)),
        named.wd_stage(pltpu.VMEM((hidden, D), f32)),
        named.wg(pltpu.VMEM((hidden, D), bf16)),
        named.wu(pltpu.VMEM((hidden, D), bf16)),
        named.wd(pltpu.VMEM((hidden, D), bf16)),
        named.inner(pltpu.VMEM((chunks, rows, hidden), bf16)),
        named.act(pltpu.VMEM((chunks, rows, hidden), bf16)),
        named.slope(pltpu.VMEM((chunks, rows, hidden), bf16)),
        named.hot(pltpu.VMEM((2, SEQ, n * cap), bf16)),
        named.targ_row(pltpu.VMEM((2, SEQ), jnp.int32)),
        named.targ_col(pltpu.VMEM((SEQ, LANES), jnp.int32)),
        named.load_sems(pltpu.SemaphoreType.DMA((3,))),
        named.save_sems(pltpu.SemaphoreType.DMA((32,))),
        named.chunk_sems(pltpu.SemaphoreType.DMA((4, chunks))),
        named.tiny_one(Tiny.scratch(8, SEQ)),
        named.tiny_two(Tiny.scratch(experts, SEQ)),
        named.route(Route.scratch(n, cap, 1)),
    ]


def start_weight_loads(m, layer):
    loads = [
        pltpu.make_async_copy(src.at[layer, 0], dst, m.load_sems.at[i])
        for i, (src, dst) in enumerate(((m.gate_f, m.wg_stage), (m.up_f, m.wu_stage), (m.down_f, m.wd_stage)))
    ]
    for copy in loads:
        copy.start()
    return loads


def forward_rows(m, layer, experts, tiny_one, tiny_two, route):
    tiny_one.start(to_row(jnp.sum(m.mid[...] * m.mid[...], axis=1, keepdims=True)))
    scale = to_cols(lax.rsqrt(tiny_one.total() * (1.0 / D) + eps_norm))
    m.r2[...] = scale
    m.normed[...] = (m.mid[...] * scale[:, :1] * gain_of(m, layer, 1)).astype(bf16)

    def fill(chunk):
        number = chunk * route.rows + lax.broadcasted_iota(jnp.int32, (route.rows, SEQ), 0)
        hit = (m.targ_row[0:1] == number) | (m.targ_row[1:2] == number)
        route.out[chunk] = nn(hit.astype(f32).astype(bf16), m.normed[...]).astype(bf16)

    return fill


def narrow_weights(stage, low):
    def narrow(i, carry):
        rows = pl.ds(pl.multiple_of(i * 64, 64), 64)
        low[rows] = stage[rows].astype(bf16)
        return carry

    lax.fori_loop(0, low.shape[0] // 64, narrow, 0)


def router_gates(m, layer, tiny_two):
    logits = tiny_two.total()
    expert_no = lax.broadcasted_iota(jnp.int32, logits.shape, 0)
    chosen = [
        jnp.sum(jnp.where(expert_no == m.routes_row[layer, k : k + 1], logits, 0.0), axis=0, keepdims=True)
        for k in range(2)
    ]
    share = [1.0 / (1.0 + jnp.exp(chosen[1 - k] - chosen[k])) for k in range(2)]
    place = lax.broadcasted_iota(jnp.int32, (8, SEQ), 0)
    m.gates[...] = to_cols(jnp.where(place == 0, share[0], share[1]))


def forward_products(m, chunk, rows):
    gate_pre = nt(rows, m.wg[...])
    up_pre = nt(rows, m.wu[...])
    square = gate_pre * gate_pre
    bent = jnp.tanh(gelu_c * gate_pre * (1.0 + gelu_a * square))
    half = 0.5 * (1.0 + bent)
    active = gate_pre * half
    steep = half + 0.5 * gate_pre * (1.0 - bent * bent) * (gelu_c * (1.0 + 3.0 * gelu_a * square))
    inner_rows = (active * up_pre).astype(bf16)
    m.inner[chunk] = inner_rows
    m.act[chunk] = active.astype(bf16)
    m.slope[chunk] = (up_pre * steep).astype(bf16)
    return nn(inner_rows, m.wd[...])


def set_hot(m, count):
    for k in range(2):
        m.hot[k] = hot_columns(m.targ_col, k, count)


def forward_combine(m, route):
    route.wait_back(0)
    y = m.mid[...]
    for k in range(2):
        rows = nn(m.hot[k], route.returned(0))
        m.picked[k] = rows.astype(bf16)
        y = y + m.gates[:, k : k + 1] * rows
    m.y[...] = y


def forward_experts(m, n, cap, layer, experts, loads, saves, hook):
    tiny_one = Tiny(m.tiny_one)
    tiny_two = Tiny(m.tiny_two)
    route = Route(n, cap, 1, m.route)
    fill = forward_rows(m, layer, experts, tiny_one, tiny_two, route)
    route.begin(fill, fill)
    tiny_two.start(nt(router_of(m, layer, experts), m.normed[...]))
    for buffer, out in ((m.mid, m.outs.mid), (m.normed, m.outs.normed), (m.r2, m.outs.r2)):
        saves.start(buffer, out)
    stages = (m.wg_stage, m.wu_stage, m.wd_stage)
    lows = (m.wg, m.wu, m.wd)
    for copy, stage, low, out in zip(loads, stages, lows, (m.wg_out, m.wu_out, m.wd_out)):
        copy.wait()
        narrow_weights(stage, low)
        saves.start(low, out)
    router_gates(m, layer, tiny_two)
    saves.start(m.gates, m.outs.gates)

    def chunk_saves(chunk):
        pairs = ((route.x, m.x_out), (m.inner, m.inner_out), (m.act, m.act_out), (m.slope, m.slope_out))
        return [
            pltpu.make_async_copy(src.at[chunk], dst.at[chunk], m.chunk_sems.at[i, chunk])
            for i, (src, dst) in enumerate(pairs)
        ]

    def compute(chunk, rows):
        products = forward_products(m, chunk, rows)
        for copy in chunk_saves(chunk):
            copy.start()
        route.put(chunk, products)

    def hook_all(i):
        @pl.when(i == 2)
        def _():
            set_hot(m, n * cap)

        if hook is not None:
            hook(i)

    route.run(compute, hook_all)
    forward_combine(m, route)
    saves.start(m.picked, m.outs.picked)
    saves.start(m.y, m.outs.y)
    route.wait_sends()

    def drain(chunk, carry):
        for copy in chunk_saves(chunk):
            copy.wait()
        return carry

    lax.fori_loop(0, route.chunks, drain, 0)


class Pieces:
    def __init__(self, n, pieces, send, recv):
        self.n, self.pieces, self.send, self.recv = n, pieces, send, recv

    def copies(self, piece, k):
        d, t, sib, far, opp = places()
        n = self.n
        near = d + 1 - 2 * lax.rem(d, 2)
        view, src = self.pieces[piece]
        peer = lax.rem(d + 2 * k, n)
        source = lax.rem(d - 2 * k + n, n)
        send, recv = self.send, self.recv
        return (
            lambda: remote(src, view(d), send.at[piece, 0, k], recv.at[piece, 0, k], (peer, t)),
            lambda: remote(view(source), view(source), send.at[piece, 1, k], recv.at[piece, 1, k], (near, t)),
        )

    def own(self, piece):
        d, t, sib, far, opp = places()
        near = d + 1 - 2 * lax.rem(d, 2)
        view, src = self.pieces[piece]
        return remote(src, view(d), self.send.at[piece, 1, 0], self.recv.at[piece, 1, 0], (near, t))

    def loop(self, action):
        def one(k, carry):
            action(k)
            return carry

        lax.fori_loop(1, self.n // 2, one, 0)

    def start(self, piece):
        self.loop(lambda k: self.copies(piece, k)[0]().start())
        self.own(piece).start()

    def forward_one(self, piece, k):
        direct, passed = self.copies(piece, k)
        direct().wait_recv()
        passed().start()

    def forward(self, piece):
        self.loop(lambda k: self.forward_one(piece, k))

    def finish(self, piece):
        self.own(piece).wait_recv()
        self.loop(lambda k: self.copies(piece, k)[1]().wait_recv())

    def wait_sends(self, piece):
        self.own(piece).wait_send()

        def one(k):
            direct, passed = self.copies(piece, k)
            direct().wait_send()
            passed().wait_send()

        self.loop(one)


def set_small(m, heads):
    own = m.small.shape[1]
    shape = (LAYERS * heads, own)
    row = lax.broadcasted_iota(jnp.int32, shape, 0)
    lane = lax.broadcasted_iota(jnp.int32, shape, 1)
    table = jnp.zeros(shape, f32)
    for layer in range(LAYERS):
        for j in range(m.table.shape[1]):
            for head in range(heads):
                value = m.table[layer, j : j + 1, head : head + 1]
                table = jnp.where((row == layer * heads + head) & (lane == j), value, table)
    parts = [m.gains[layer] for layer in range(LAYERS)]
    parts += [m.router_t[layer] for layer in range(LAYERS)]
    parts.append(table)
    count = sum(one.shape[0] for one in parts)
    if count < m.small.shape[0]:
        parts.append(jnp.zeros((m.small.shape[0] - count, own), f32))
    m.small[...] = jnp.concatenate(parts, axis=0).astype(bf16)


def place_small(n, small_all, rows):
    own = small_all.shape[2]
    if own == LANES:
        return [
            jnp.concatenate([small_all[2 * q].astype(f32), small_all[2 * q + 1].astype(f32)], axis=1)
            for q in range(SLICES)
        ]
    out = []
    for q in range(SLICES):
        total = jnp.zeros((rows, HALF), f32)
        for i in range(HALF // own):
            lane = lax.broadcasted_iota(jnp.int32, (own, HALF), 1)
            spot = lax.broadcasted_iota(jnp.int32, (own, HALF), 0)
            hot = (lane == spot + i * own).astype(f32).astype(bf16)
            total = total + nn(small_all[q * (HALF // own) + i], hot)
        out.append(total)
    return out


def first_program(n, cap, experts, heads):
    buckets = BUCKETS // n

    def first_kernel(m):
        d, t, sib, far, opp = places()
        own = D // n
        saves = Saves(m.save_sems)
        loads = start_weight_loads(m, 0)
        reduce = Reduce(m.part, m.reduce)

        def span(i):
            return pl.ds(pl.multiple_of(i * own, 16), own)

        views = [
            (lambda i: m.small_all.at[i], m.small),
            (lambda i: m.wqkv.at[0, span(i)], m.qkv_low.at[0, 0]),
            (lambda i: m.wqkv.at[1, span(i)], m.qkv_low.at[0, 1]),
            (lambda i: m.wqkv.at[2, span(i)], m.qkv_low.at[0, 2]),
            (lambda i: m.wo.at[span(i)], m.out_low.at[0]),
            (lambda i: m.wqkv_next.at[:, span(i)], m.qkv_low.at[1]),
            (lambda i: m.wo_next.at[span(i)], m.out_low.at[1]),
        ]
        pieces = Pieces(n, views, m.piece_send, m.piece_recv)
        set_small(m, heads)
        m.qkv_low[0] = m.qkv[0].astype(bf16)
        greet(n, True)
        pieces.start(0)
        pieces.start(1)
        pieces.start(2)
        m.late_wait()
        m.out_low[0] = m.out[0].astype(bf16)
        m.small_all[d] = m.small[...]
        m.wqkv[:, span(d)] = m.qkv_low[0]
        m.wo[span(d)] = m.out_low[0]
        m.qkv_low[1] = m.qkv[1].astype(bf16)
        m.out_low[1] = m.out[1].astype(bf16)
        saves.start(m.qkv_low.at[1], m.wqkv_next.at[:, span(d)])
        saves.start(m.out_low.at[1], m.wo_next.at[span(d)])
        set_targets(m, 0, cap)
        pieces.forward(0)
        pieces.finish(0)
        rows = m.small.shape[0]
        slices = place_small(n, m.small_all, rows)
        for q in range(SLICES):
            m.wide[q] = slices[q].astype(bf16)
        first = 2 * LAYERS + LAYERS * experts
        table = jnp.zeros((LAYERS * heads, LANES), f32)
        width = m.small_all.shape[2]
        for i in range(n):
            lane = lax.broadcasted_iota(jnp.int32, (width, LANES), 1)
            spot = lax.broadcasted_iota(jnp.int32, (width, LANES), 0)
            hot = ((lane == spot + i * buckets) & (spot < buckets)).astype(f32).astype(bf16)
            table = table + nn(m.small_all[i][first : first + LAYERS * heads], hot)
        m.tab[...] = table
        set_attention_tables(m)
        total = None
        for q in range(SLICES):
            x = m.tok[:, q * HALF : (q + 1) * HALF].astype(f32)
            m.hg[q] = (x * m.wide[q, 0:1].astype(f32)).astype(bf16)
            squares = jnp.sum(x * x, axis=1, keepdims=True)
            total = squares if total is None else total + squares
        m.r1[...] = jnp.broadcast_to(lax.rsqrt(total * (1.0 / D) + eps_norm), (SEQ, LANES))
        saves.start(m.hg, m.hg_out)
        pieces.forward(1)
        pieces.start(3)
        pieces.forward(2)
        pieces.start(4)
        pieces.finish(1)
        for b in range(2):
            project(m, b, 0)
        pieces.forward(3)
        pieces.finish(2)
        for b in range(2):
            project(m, b, 1)
        pieces.forward(4)
        for piece in (5, 6):
            pieces.start(piece)
        pieces.finish(3)
        for b in range(2):
            project(m, b, 2)
        saves.start(m.wqkv, m.wqkv_out)
        for b in range(2):
            attend_block(m, b, 0)
            if b == 0:
                pieces.finish(4)
                saves.start(m.wo, m.wo_out)
            project_out(m, b)
            reduce.start(b)
            reduce.middle(b)
        save_attention(m, saves)
        for b in range(2):
            span_b = block_rows(b)
            m.mid[span_b] = pick_slice(m.tok[span_b].astype(f32)) + reduce.finish(b)

        half = n // 2
        share = max(1, half // 4)

        def pass_on(first):
            def one(k, carry):
                for piece in (5, 6):
                    pieces.forward_one(piece, k)
                return carry

            lax.fori_loop(first, min(first + share, half), one, 0)

        def hook(i):
            for event in range(3):

                @pl.when(i == 2 * event + 1)
                def _(event=event):
                    pass_on(1 + event * share)

        forward_experts(m, n, cap, 0, experts, loads, saves, hook)
        if 1 + 3 * share < half:
            pass_on(1 + 3 * share)
        for piece in (5, 6):
            pieces.finish(piece)
        for piece in range(7):
            pieces.wait_sends(piece)
        reduce.wait_sends()
        saves.wait()

    return first_kernel


def norm_backward(tiny, grad, rows, scale, gain, upstream):
    weighted = grad * gain
    tiny.start(to_row(jnp.sum(weighted * rows, axis=1, keepdims=True)))
    gain_grad = jnp.sum(grad * rows * scale, axis=0, keepdims=True)
    base = upstream + scale * weighted
    mean = to_cols(tiny.total())[:, :1] * (1.0 / D)
    return base - rows * (scale * scale * scale * mean), gain_grad


def backward_outs(n, cap, hidden, experts):
    return [
        named.midg((SEQ, HALF), f32, vmem_spec),
        named.gain_rows((8, HALF), f32, vmem_spec),
        named.router_g((experts, HALF), f32, vmem_spec),
        named.wg_grad((hidden, D), bf16, any_spec),
        named.wu_grad((hidden, D), bf16, any_spec),
        named.wd_grad((hidden, D), bf16, any_spec),
    ]


def backward_ins(state):
    return [
        named.picked(state.picked, late_spec),
        named.gates(state.gates, late_spec),
        named.mid(state.mid, late_spec),
        named.normed(state.normed, late_spec),
        named.r2(state.r2, late_spec),
        named.x_in(state.x_out, any_spec),
        named.inner_in(state.inner_out, any_spec),
        named.act_in(state.act_out, any_spec),
        named.slope_in(state.slope_out, any_spec),
        named.wg_in(state.wg_out, any_spec),
        named.wu_in(state.wu_out, any_spec),
        named.wd_in(state.wd_out, any_spec),
    ]


def backward_scratch(n, cap, hidden, experts):
    chunks, rows = Route.shape(n, cap)
    return [
        named.wg(pltpu.VMEM((hidden, D), bf16)),
        named.wu(pltpu.VMEM((hidden, D), bf16)),
        named.wd(pltpu.VMEM((hidden, D), bf16)),
        named.xs(pltpu.VMEM((chunks, SLICES, rows, HALF), bf16)),
        named.inner(pltpu.VMEM((chunks, rows, hidden), bf16)),
        named.act(pltpu.VMEM((chunks, rows, hidden), bf16)),
        named.slope(pltpu.VMEM((chunks, rows, hidden), bf16)),
        named.gpg(pltpu.VMEM((chunks, rows, hidden), bf16)),
        named.upg(pltpu.VMEM((chunks, rows, hidden), bf16)),
        named.dy(pltpu.VMEM((SEQ, HALF), f32)),
        named.pgs(pltpu.VMEM((2 * SEQ, HALF), bf16)),
        named.hot(pltpu.VMEM((2, SEQ, n * cap), bf16)),
        named.logit_g(pltpu.VMEM((experts, SEQ), f32)),
        named.targ_row(pltpu.VMEM((2, SEQ), jnp.int32)),
        named.targ_col(pltpu.VMEM((SEQ, LANES), jnp.int32)),
        named.load_sems(pltpu.SemaphoreType.DMA((7,))),
        named.save_sems(pltpu.SemaphoreType.DMA((32,))),
        named.tiny_one(Tiny.scratch(8, SEQ)),
        named.tiny_two(Tiny.scratch(8, SEQ)),
        named.route(Route.scratch(n, cap, 1)),
    ]


def start_backward_loads(m):
    pairs = (
        (m.wd_in, m.wd),
        (m.act_in, m.act),
        (m.slope_in, m.slope),
        (m.wg_in, m.wg),
        (m.wu_in, m.wu),
        (m.inner_in, m.inner),
        (m.x_in, m.xs),
    )
    loads = [pltpu.make_async_copy(src, dst, m.load_sems.at[i]) for i, (src, dst) in enumerate(pairs)]
    for copy in loads:
        copy.start()
    return loads


def backward_rows(m, route):
    for k in range(2):
        m.pgs[k * SEQ : (k + 1) * SEQ] = (m.gates[:, k : k + 1] * m.dy[...]).astype(bf16)

    def fill(chunk, place):
        number = chunk * route.rows + lax.broadcasted_iota(jnp.int32, (route.rows, SEQ), 0)
        hits = [(m.targ_row[k : k + 1] == number).astype(f32).astype(bf16) for k in range(2)]
        route.out[place] = nn(jnp.concatenate(hits, axis=1), m.pgs[...]).astype(bf16)

    return fill


def start_shares(m, tiny):
    place = lax.broadcasted_iota(jnp.int32, (8, SEQ), 0)
    shares = [to_row(jnp.sum(m.dy[...] * m.picked[k].astype(f32), axis=1, keepdims=True)) for k in range(2)]
    tiny.start(jnp.where(place == 0, shares[0], shares[1]))


def logit_gradient(m, layer, experts, tiny):
    share_grad = tiny.total()
    gate_rows = jnp.transpose(m.gates[...])[:8]
    product = gate_rows * share_grad
    both = product[0:1] + product[1:2]
    chosen = gate_rows * (share_grad - both)
    expert_no = lax.broadcasted_iota(jnp.int32, (experts, SEQ), 0)
    logit_g = jnp.zeros((experts, SEQ), f32)
    for k in range(2):
        logit_g = logit_g + jnp.where(expert_no == m.routes_row[layer, k : k + 1], chosen[k : k + 1], 0.0)
    m.logit_g[...] = logit_g
    m.router_g[...] = nn(logit_g.astype(bf16), m.normed[...])


def backward_products(m, chunk, rows):
    inner_grad = nt(rows, m.wd[...])
    up_low = (inner_grad * m.act[chunk].astype(f32)).astype(bf16)
    gate_low = (inner_grad * m.slope[chunk].astype(f32)).astype(bf16)
    m.upg[chunk] = up_low
    m.gpg[chunk] = gate_low
    return nn(gate_low, m.wg[...]) + nn(up_low, m.wu[...])


class Products:
    def __init__(self, m, route, first, inputs_of, saves):
        self.m, self.route, self.first, self.inputs_of, self.saves = m, route, first, inputs_of, saves

    def one(self, left_ref, right_of, stage, out):
        count = self.route.chunks * self.route.rows
        hidden = stage.shape[0]
        right = jnp.concatenate([right_of(q) for q in range(SLICES)], axis=1)
        for start in range(0, hidden, HALF):
            size = min(HALF, hidden - start)
            left = left_ref[:, :, start : start + size].reshape(count, size)
            stage[start : start + size] = tn(left, right).astype(bf16)
            self.saves.start(stage, out, slice(start, start + size))

    def step(self):
        return self.route.total + STAGE_LAGS[2] - 1

    def in_loop(self, i):
        @pl.when(i == self.step())
        def _():
            self.one(self.m.gpg, self.inputs_of, self.m.wg, self.m.wg_grad)

    def after(self):
        self.one(self.m.upg, self.inputs_of, self.m.wu, self.m.wu_grad)
        self.one(self.m.inner, lambda q: self.route.arrived(self.first, q), self.m.wd, self.m.wd_grad)


def backward_tail(m, layer, experts, tiny, route, first, gain_one):
    route.wait_back(first)
    grad = tn(m.logit_g[...].astype(bf16), router_of(m, layer, experts))
    for k in range(2):
        grad = grad + nn(m.hot[k], route.returned(first))
    value, gain_two = norm_backward(tiny, grad, m.mid[...], m.r2[:, :1], gain_of(m, layer, 1), m.dy[...])
    m.midg[...] = value
    gain_place = lax.broadcasted_iota(jnp.int32, (8, HALF), 0)
    m.gain_rows[...] = jnp.where(gain_place == 0, gain_two, jnp.where(gain_place == 1, gain_one, 0.0))
    route.wait_sends()


def backward_experts(m, n, cap, layer, experts, loads, saves, gain_one, hook, hook_end):
    tiny_one = Tiny(m.tiny_one)
    tiny_two = Tiny(m.tiny_two)
    route = Route(n, cap, 1, m.route)
    fill_one = backward_rows(m, route)

    def fill(chunk):
        fill_one(chunk, chunk)

    route.begin(fill, fill)
    start_shares(m, tiny_one)
    for copy in loads[:5]:
        copy.wait()
    logit_gradient(m, layer, experts, tiny_one)

    def compute(chunk, rows):
        route.put(chunk, backward_products(m, chunk, rows))

    def hook_all(i):
        @pl.when(i == 1)
        def _():
            set_hot(m, n * cap)

        hook(i)
        products.in_loop(i)

    count = route.chunks * route.rows
    products = Products(m, route, 0, lambda q: m.xs[:, q].reshape(count, HALF), saves)
    for copy in loads[5:]:
        copy.wait()
    route.run(compute, hook_all)
    products.after()
    hook_end()
    backward_tail(m, layer, experts, tiny_two, route, 0, gain_one)


def top_program(n, cap, experts, heads, layer):
    def top_kernel(m):
        saves = Saves(m.save_sems)
        weight_copies = [
            pltpu.make_async_copy(m.wqkv_in, m.wqkv, m.weight_sems.at[0]),
            pltpu.make_async_copy(m.wo_in, m.wo, m.weight_sems.at[1]),
        ]
        expert_weights = [
            pltpu.make_async_copy(src.at[layer, 0], m.stage, m.load_sems.at[i])
            for i, src in enumerate((m.gate_f, m.up_f, m.down_f))
        ]
        expert_weights[0].start()
        for copy in weight_copies:
            copy.start()
        reduce = Reduce(m.part, m.reduce)
        gather = Gather(m.hg, m.gather)
        tiny = Tiny(m.tiny_zero)
        greet(n, True)
        gain = gain_of(m, layer, 0)
        for b in range(2):
            gather.start(b, (m.h[block_rows(b)] * gain).astype(bf16))
        tiny.start(to_row(jnp.sum(m.h[...] * m.h[...], axis=1, keepdims=True)))
        set_attention_tables(m)
        set_targets(m, layer, cap)
        m.r1[...] = to_cols(lax.rsqrt(tiny.total() * (1.0 / D) + eps_norm))
        m.late_wait()
        m.dy[...] = pick_slice(m.cot[...].astype(f32))
        lows = (m.wg, m.wu, m.wd)
        expert_weights[0].wait()
        narrow_weights(m.stage, lows[0])
        expert_weights[1].start()
        for copy in weight_copies:
            copy.wait()
        gather.forward(0)
        gather.finish(0)
        gather.forward(1)
        attention_block(m, 0, layer * heads, lambda: None)
        reduce.start(0)
        gather.finish(1)
        attention_block(m, 1, layer * heads, lambda: reduce.middle(0))
        reduce.start(1)
        saves.start(m.hg, m.hg_out)
        save_attention(m, saves)
        reduce.middle(1)
        expert_weights[1].wait()
        narrow_weights(m.stage, lows[1])
        expert_weights[2].start()
        for b in range(2):
            span_b = block_rows(b)
            m.mid[span_b] = m.h[span_b] + reduce.finish(b)
        tiny_one = Tiny(m.tiny_one)
        tiny_two = Tiny(m.tiny_two)
        tiny_three = Tiny(m.tiny_three)
        tiny_four = Tiny(m.tiny_four)
        route = Route(n, cap, 2, m.route)
        chunks = route.chunks
        fill_forward = forward_rows(m, layer, experts, tiny_one, tiny_two, route)

        def fill(chunk):
            @pl.when(chunk < chunks)
            def _():
                fill_forward(chunk)

            @pl.when(chunk >= chunks)
            def _():
                fill_backward(chunk - chunks, chunk)

        route.begin(fill_forward, fill)
        tiny_two.start(nt(router_of(m, layer, experts), m.normed[...]))
        expert_weights[2].wait()
        narrow_weights(m.stage, lows[2])
        router_gates(m, layer, tiny_two)
        fill_backward = backward_rows(m, route)

        def compute(chunk, rows):
            @pl.when(chunk < chunks)
            def _():
                route.put(chunk, forward_products(m, chunk, rows))

            @pl.when(chunk >= chunks)
            def _():
                route.put(chunk, backward_products(m, chunk - chunks, rows))

        def hook(i):
            @pl.when(i == 2)
            def _():
                set_hot(m, n * cap)

            @pl.when(i == chunks + STAGE_LAGS[3] + 1)
            def _():
                forward_combine(m, route)
                saves.start(m.y, m.outs.y)
                start_shares(m, tiny_three)

            products.in_loop(i)

        products = Products(m, route, chunks, lambda q: route.arrived(0, q), saves)
        route.run(compute, hook)
        logit_gradient(m, layer, experts, tiny_three)
        products.after()
        backward_tail(m, layer, experts, tiny_four, route, chunks, jnp.zeros((1, HALF), f32))
        gather.wait_sends()
        reduce.wait_sends()
        saves.wait()

    return top_kernel


def attention_back_ins(kept, midg):
    return [
        named.midg_in(midg, vmem_spec),
        named.a_ctx(kept.ctx, late_spec),
        named.a_proj(kept.proj, late_spec),
        named.a_lse(kept.lse, late_spec),
        named.a_r1(kept.r1, late_spec),
        named.a_hg(kept.hg, late_spec),
        named.a_wqkv(kept.wqkv, late_spec),
        named.a_wo(kept.wo, late_spec),
        named.a_h(kept.h, late_spec),
    ]


def attention_back_scratch(width, heads):
    return attention_scratch + [
        named.pg(pltpu.VMEM((SEQ, 3 * width), bf16)),
        named.dk(pltpu.VMEM((SEQ, width), f32)),
        named.dv(pltpu.VMEM((SEQ, width), f32)),
        named.bias_grad(pltpu.VMEM((heads, HALF, 2 * HALF), f32)),
        named.probs(pltpu.VMEM((heads, HALF, 3 * HALF), f32)),
        named.ag(pltpu.VMEM((SLICES, SEQ, HALF), bf16)),
        named.gather(Gather.scratch),
        named.tiny_zero(Tiny.scratch(8, SEQ)),
    ]


def attention_view(m):
    return types.SimpleNamespace(
        seg_col=m.seg_col,
        seg_row=m.seg_row,
        bias=m.bias,
        part=m.part,
        ctx=m.a_ctx,
        proj=m.a_proj,
        lse=m.a_lse,
        r1=m.a_r1,
        hg=m.a_hg,
        wqkv=m.a_wqkv,
        wo=m.a_wo,
        pg=m.pg,
        dk=m.dk,
        dv=m.dv,
        bias_grad=m.bias_grad,
        probs=m.probs,
        ag=m.ag,
        wog=m.wog,
        qkvg=m.qkvg,
    )


def attention_back(m, layer, heads, after_gather, after_out, after_qkv):
    gather = Gather(m.ag, m.gather)
    reduce = Reduce(m.part, m.reduce)
    tiny = Tiny(m.tiny_zero)
    a = attention_view(m)
    for b in (1, 0):
        gather.start(b, m.midg_in[block_rows(b)].astype(bf16))
    set_attention_tables(m)
    m.late_wait()
    attention_probs(a, 1, layer * heads)
    gather.forward(1)
    attention_probs(a, 0, layer * heads)
    gather.forward(0)
    gather.finish(1)
    late_dots = attention_back_block(a, 1, lambda: None)
    reduce.start(1)
    gather.finish(0)
    after_gather()
    early_dots = attention_back_block(a, 0, lambda: reduce.middle(1))
    reduce.start(0)
    tiny.start(to_row(jnp.concatenate([early_dots, late_dots], axis=0)))
    out_gradient(a)
    after_out()
    reduce.middle(0)
    qkv_gradient(a)
    after_qkv()
    m.table[...] = table_gradient(a)
    grad = jnp.concatenate([reduce.finish(0), reduce.finish(1)], axis=0)
    h = m.a_h[...] if m.a_h.shape[1] == HALF else pick_slice(m.a_h[...].astype(f32))
    scale = m.a_r1[:, :1]
    gain_grad = jnp.sum(grad * h * scale, axis=0, keepdims=True)
    base = m.midg_in[...] + scale * (grad * gain_of(m, layer, 0))
    mean = to_cols(tiny.total())[:, :1] * (1.0 / D)
    gather.wait_sends()
    reduce.wait_sends()
    return base - h * (scale * scale * scale * mean), gain_grad


def back_program(n, cap, experts, heads, layer):
    def back_next_kernel(m):
        saves = Saves(m.save_sems)
        loads = start_backward_loads(m)
        greet(n, True)
        set_targets(m, layer, cap)
        own = D // n

        def rows_of(e):
            return pl.ds(pl.multiple_of(e * own, 16), own)

        late_qkv = Scatter(n, lambda e: m.qkvg.at[:, rows_of(e)], m.qkv_sums, m.near_a, None, None)
        late_out = Scatter(n, lambda e: m.wog.at[rows_of(e)], m.out_sums, m.near_b, m.out_late, m.far_b)
        half = n // 2
        share = max(1, half // 4)
        value, gain_one = attention_back(
            m,
            layer + 1,
            heads,
            lambda: None,
            lambda: late_out.near_start(1, half + 1),
            lambda: late_qkv.near_start(1, 1 + share),
        )
        m.dy[...] = value

        def hook(i):
            for event in range(1, half // share):

                @pl.when(i == 2 * event - 1)
                def _(event=event):
                    late_qkv.near_start(1 + event * share, 1 + (event + 1) * share)

                @pl.when(i == 2 * event)
                def _(event=event):
                    late_qkv.loop(1 + (event - 1) * share, 1 + event * share, late_qkv.near_sum)

            @pl.when(i == 3)
            def _():
                late_out.near_sums()
                late_out.far_start()

        def hook_end():
            late_qkv.loop(1 + half - share, 1 + half, late_qkv.near_sum)
            saves.start(m.qkv_sums, m.outs.qkv_sums)

        backward_experts(m, n, cap, layer, experts, loads, saves, gain_one, hook, hook_end)
        late_out.finish()
        late_out.near_wait_sends()
        late_qkv.near_wait_sends()
        saves.wait()

    return back_next_kernel


class Scatter:
    @staticmethod
    def near_scratch(n, block):
        return [
            pltpu.VMEM((n // 2,) + block, bf16),
            pltpu.SemaphoreType.DMA((n // 2,)),
            pltpu.SemaphoreType.DMA((n // 2,)),
        ]

    @staticmethod
    def far_scratch(n, block):
        return [
            pltpu.VMEM((n // 2,) + block, bf16),
            pltpu.SemaphoreType.DMA((n // 2,)),
            pltpu.SemaphoreType.DMA((n // 2,)),
        ]

    def __init__(self, n, block_of, sums, near_refs, out, far_refs):
        self.n, self.block_of, self.sums, self.out = n, block_of, sums, out
        if near_refs is not None:
            self.near, self.near_send, self.near_recv = near_refs
        if far_refs is not None:
            self.got, self.far_send, self.far_recv = far_refs

    def near_copy(self, k):
        d, t, sib, far, opp = places()
        parity = lax.rem(d, 2)
        src = self.block_of(2 * k + 1 - parity)
        return remote(src, self.near.at[k], self.near_send.at[k], self.near_recv.at[k], (d + 1 - 2 * parity, t))

    def far_copy(self, k, source):
        d, t, sib, far, opp = places()
        return remote(
            self.sums.at[k], self.got.at[source], self.far_send.at[k], self.far_recv.at[source], (2 * k + lax.rem(d, 2), t)
        )

    def spot(self, j):
        d = lax.axis_index("dp")
        return lax.rem(d // 2 + j, self.n // 2)

    def loop(self, first, last, action):
        def one(j, carry):
            action(self.spot(j))
            return carry

        lax.fori_loop(first, last, one, 0)

    def near_start(self, first, last):
        self.loop(first, last, lambda k: self.near_copy(k).start())

    def near_sum(self, k):
        d = lax.axis_index("dp")
        self.near_copy(k).wait_recv()
        mine = self.block_of(2 * k + lax.rem(d, 2))[...].astype(f32)
        self.sums[k] = (mine + self.near[k].astype(f32)).astype(bf16)

    def near_sums(self):
        self.loop(1, self.n // 2 + 1, self.near_sum)

    def near_wait_sends(self):
        self.loop(0, self.n // 2, lambda k: self.near_copy(k).wait_send())

    def far_start(self):
        d = lax.axis_index("dp")
        self.loop(1, self.n // 2, lambda k: self.far_copy(k, d // 2).start())

    def both(self, ahead):
        d = lax.axis_index("dp")
        total = self.n // 2

        def one(j, carry):
            k = self.spot(j)

            @pl.when(j + ahead <= total)
            def _():
                self.near_copy(self.spot(j + ahead)).start()

            self.near_sum(k)

            @pl.when(k != d // 2)
            def _():
                self.far_copy(k, d // 2).start()

            return carry

        lax.fori_loop(1, total + 1, one, 0)

    def finish(self):
        d = lax.axis_index("dp")
        total = self.sums[d // 2].astype(f32)

        def one(j, carry):
            k = self.spot(j)
            self.far_copy(k, k).wait_recv()
            return carry + self.got[k].astype(f32)

        self.out[...] = lax.fori_loop(1, self.n // 2, one, total)
        self.loop(1, self.n // 2, lambda k: self.far_copy(k, d // 2).wait_send())


def final_program(n, experts, heads):
    own = D // n

    def final_kernel(m):
        d, t, sib, far, opp = places()
        saves = Saves(m.save_sems)

        def rows_of(e):
            return pl.ds(pl.multiple_of(e * own, 16), own)

        late_qkv = Scatter(n, None, m.qkv_sums_next, None, m.qkv_grad.at[1], m.far_a)
        early_qkv = Scatter(n, lambda e: m.qkvg.at[:, rows_of(e)], m.qkv_sums, m.near_c, m.qkv_grad.at[0], m.far_c)
        early_out = Scatter(n, lambda e: m.wog.at[rows_of(e)], m.out_sums, m.near_d, m.out_grad.at[0], m.far_d)
        half = n // 2
        output = Gather(m.output_buf, m.output_gather)
        dx_all = Gather(m.dx_buf, m.dx_gather)
        greet(n, True)
        late_qkv.far_start()
        m.out_grad[1] = m.out_late[...]

        def after_out():
            early_out.near_start(1, half + 1)

        def after_qkv():
            early_qkv.near_start(1, half + 1)
            early_out.both(half)

        def after_gather():
            for b in range(2):
                output.start(b, m.y_last[block_rows(b)].astype(bf16))

        dx, gain_one = attention_back(m, 0, heads, after_gather, after_out, after_qkv)
        for b in range(2):
            dx_all.start(b, dx[block_rows(b)].astype(bf16))
        place = lax.broadcasted_iota(jnp.int32, (8, HALF), 0)
        m.pack[0:8] = jnp.where(
            place == 0,
            gain_one,
            jnp.where(
                place == 1,
                m.gain_rows_0[0:1],
                jnp.where(place == 2, m.gain_rows_0[1:2], jnp.where(place == 3, m.gain_rows_1[0:1], 0.0)),
            ),
        )
        m.pack[8:16] = jnp.concatenate([m.table[...], m.table_next[...]], axis=1)
        m.pack[16 : 16 + experts] = m.router_g_0[...]
        m.pack[16 + experts : 16 + 2 * experts] = m.router_g_1[...]

        def pack_copy(j, source, target):
            return remote(m.pack, m.packs.at[source], m.pack_send.at[j], m.pack_recv.at[source], (target, t))

        def spread(j, carry):
            pack_copy(j, d, lax.rem(d + j, n)).start()
            return carry

        lax.fori_loop(1, n, spread, 0)
        early_qkv.both(half)
        for b in range(2):
            output.forward(b)
        for b in range(2):
            dx_all.forward(b)
        m.packs[d] = m.pack[...]

        def collect(j, carry):
            source = lax.rem(d + j, n)
            pack_copy(j, source, source).wait_recv()
            return carry

        lax.fori_loop(1, n, collect, 0)

        def add(i, carry):
            return carry + m.packs[i]

        m.small_out[t] = lax.fori_loop(1, n, add, m.packs[0])

        def all_copies():
            return [
                remote(m.small_out.at[t], m.small_out.at[t], m.all_send.at[i], m.all_recv.at[i], (d, peer))
                for i, peer in enumerate((sib, far, opp))
            ]

        for copy in all_copies():
            copy.start()
        for gather, out in ((output, m.output), (dx_all, m.dx_full)):
            for b in range(2):
                gather.finish(b)
            for q in range(SLICES):
                saves.start(gather.buf.at[q], out.at[:, pl.ds(q * HALF, HALF)])
        for one in (late_qkv, early_out, early_qkv):
            one.finish()
        early_out.near_wait_sends()
        early_qkv.near_wait_sends()

        def sent(j, carry):
            pack_copy(j, d, lax.rem(d + j, n)).wait_send()
            return carry

        lax.fori_loop(1, n, sent, 0)
        for copy in all_copies():
            copy.wait()
        output.wait_sends()
        dx_all.wait_sends()
        saves.wait()

    return final_kernel


def widen_kernel(*refs):
    ins, outs = refs[: 3 * LAYERS + 4], refs[3 * LAYERS + 4 :]
    for i in range(3):
        for layer in range(LAYERS):
            outs[i][layer, 0] = ins[3 * layer + i][...].astype(f32)
    for i in range(4):
        outs[3 + i][...] = ins[3 * LAYERS + i][...].astype(outs[3 + i].dtype)


def widen(grads, others):
    hidden = grads[0][0].shape[0]
    steps = 4
    tile = hidden // steps
    specs = []
    shapes = []
    for one in others:
        dim = one.ndim - 2
        count = min(steps, one.shape[dim] // 8)
        block = one.shape[:dim] + (one.shape[dim] // count,) + one.shape[dim + 1 :]
        specs.append(
            pl.BlockSpec(block, lambda i, dim=dim, count=count: (0,) * dim + (jnp.minimum(i, count - 1), 0))
        )
        shapes.append(one.shape)
    return pl.pallas_call(
        widen_kernel,
        grid=(steps,),
        out_shape=[shaped((LAYERS, 1, hidden, D), f32)] * 3
        + [shaped(shapes[0], bf16)]
        + [shaped(shape, f32) for shape in shapes[1:]],
        in_specs=[pl.BlockSpec((tile, D), lambda i: (i, 0))] * (3 * LAYERS) + specs,
        out_specs=[pl.BlockSpec((LAYERS, 1, tile, D), lambda i: (0, 0, i, 0))] * 3 + specs,
        compiler_params=pltpu.CompilerParams(vmem_limit_bytes=vmem_bytes),
    )(*[one for layer in grads for one in layer], *others)


def local(tokens, cotangent, w_qkv, w_out, router, gains, rel_table, w_gate, w_up, w_down, routes, slots, segments):
    n = lax.axis_size("dp")
    own = D // n
    experts = router.shape[2]
    heads = rel_table.shape[2]
    width = w_qkv.shape[3]
    hidden = w_down.shape[2]
    cap = 3 * SEQ // n
    rows = 2 * LAYERS + LAYERS * experts + LAYERS * heads
    rows = rows + -rows % 16
    gate_t = w_gate.transpose(0, 1, 3, 2)
    up_t = w_up.transpose(0, 1, 3, 2)
    routes_row = routes.transpose(0, 2, 1)
    slots_row = slots.transpose(0, 2, 1)
    seg_row = segments.reshape(1, SEQ)
    index_ins = [
        named.routes_row(routes_row, vmem_spec),
        named.slots_row(slots_row, vmem_spec),
        named.seg_row(seg_row, vmem_spec),
    ]
    weight_ins = [named.gate_f(gate_t, any_spec), named.up_f(up_t, any_spec), named.down_f(w_down, any_spec)]
    attention_weights = [
        named.wqkv(pltpu.VMEM((3, D, width), bf16)),
        named.wo(pltpu.VMEM((D, width), bf16)),
        named.hg(pltpu.VMEM((SLICES, SEQ, HALF), bf16)),
    ]
    pieces = 5 + 2 * (LAYERS - 1)
    first = call(
        first_program(n, cap, experts, heads),
        [named.tok(tokens, late_spec), named.qkv(w_qkv, vmem_spec), named.out(w_out, late_spec), named.gains(gains, vmem_spec)]
        + [named.router_t(router.transpose(0, 2, 1), vmem_spec), named.table(rel_table, vmem_spec)]
        + index_ins
        + weight_ins,
        [
            named.wide((SLICES, rows, HALF), bf16, vmem_spec),
            named.tab((8, LANES), f32, vmem_spec),
            named.wqkv_out((3, D, width), bf16, any_spec),
            named.wo_out((D, width), bf16, any_spec),
            named.wqkv_next((3, D, width), bf16, any_spec),
            named.wo_next((D, width), bf16, any_spec),
            named.hg_out((SLICES, SEQ, HALF), bf16, any_spec),
        ]
        + attention_outs(width)
        + forward_outs(n, cap, hidden),
        attention_weights
        + attention_scratch
        + [
            named.small(pltpu.VMEM((rows, own), bf16)),
            named.small_all(pltpu.VMEM((n, rows, own), bf16)),
            named.qkv_low(pltpu.VMEM((LAYERS, 3, own, width), bf16)),
            named.out_low(pltpu.VMEM((LAYERS, own, width), bf16)),
            named.piece_send(pltpu.SemaphoreType.DMA((pieces, 2, n // 2))),
            named.piece_recv(pltpu.SemaphoreType.DMA((pieces, 2, n // 2))),
        ]
        + forward_scratch(n, cap, hidden, experts),
        0,
    )
    wide_ins = [named.wide(first.wide, vmem_spec), named.tab(first.tab, vmem_spec)]
    chunks, route_rows = Route.shape(n, cap)
    chunk_rows = pltpu.VMEM((chunks, route_rows, hidden), bf16)
    top = call(
        top_program(n, cap, experts, heads, 1),
        [
            named.h(first.y, vmem_spec),
            named.cot(cotangent, late_spec),
            named.wqkv_in(first.wqkv_next, any_spec),
            named.wo_in(first.wo_next, any_spec),
        ]
        + wide_ins
        + index_ins
        + weight_ins,
        [named.hg_out((SLICES, SEQ, HALF), bf16, any_spec), named.y((SEQ, HALF), f32, saved_spec)]
        + attention_outs(width)
        + backward_outs(n, cap, hidden, experts),
        attention_weights
        + attention_scratch
        + [
            named.gather(Gather.scratch),
            named.tiny_zero(Tiny.scratch(8, SEQ)),
            named.tiny_one(Tiny.scratch(8, SEQ)),
            named.tiny_two(Tiny.scratch(experts, SEQ)),
            named.tiny_three(Tiny.scratch(8, SEQ)),
            named.tiny_four(Tiny.scratch(8, SEQ)),
            named.weight_sems(pltpu.SemaphoreType.DMA((2,))),
            named.load_sems(pltpu.SemaphoreType.DMA((3,))),
            named.save_sems(pltpu.SemaphoreType.DMA((32,))),
            named.stage(pltpu.VMEM((hidden, D), f32)),
            named.wg(pltpu.VMEM((hidden, D), bf16)),
            named.wu(pltpu.VMEM((hidden, D), bf16)),
            named.wd(pltpu.VMEM((hidden, D), bf16)),
            named.inner(chunk_rows),
            named.act(chunk_rows),
            named.slope(chunk_rows),
            named.gpg(chunk_rows),
            named.upg(chunk_rows),
            named.mid(pltpu.VMEM((SEQ, HALF), f32)),
            named.normed(pltpu.VMEM((SEQ, HALF), bf16)),
            named.r2(pltpu.VMEM((SEQ, LANES), f32)),
            named.gates(pltpu.VMEM((SEQ, LANES), f32)),
            named.picked(pltpu.VMEM((2, SEQ, HALF), bf16)),
            named.dy(pltpu.VMEM((SEQ, HALF), f32)),
            named.pgs(pltpu.VMEM((2 * SEQ, HALF), bf16)),
            named.hot(pltpu.VMEM((2, SEQ, n * cap), bf16)),
            named.logit_g(pltpu.VMEM((experts, SEQ), f32)),
            named.targ_row(pltpu.VMEM((2, SEQ), jnp.int32)),
            named.targ_col(pltpu.VMEM((SEQ, LANES), jnp.int32)),
            named.route(Route.scratch(n, cap, 2)),
        ],
        1,
    )

    def kept_of(state, wqkv, wo, h):
        return types.SimpleNamespace(
            ctx=state.ctx, proj=state.proj, lse=state.lse, r1=state.r1, hg=state.hg_out, wqkv=wqkv, wo=wo, h=h
        )

    gradient_scratch = [named.wog(pltpu.VMEM((D, width), bf16)), named.qkvg(pltpu.VMEM((3, D, width), bf16))]
    fourth = call(
        back_program(n, cap, experts, heads, 0),
        wide_ins
        + index_ins
        + attention_back_ins(kept_of(top, first.wqkv_next, first.wo_next, first.y), top.midg)
        + backward_ins(first),
        backward_outs(n, cap, hidden, experts)
        + [
            named.qkv_sums((n // 2, 3, own, width), bf16, saved_spec),
            named.out_late((own, width), f32, vmem_spec),
            named.table((8, LANES), f32, vmem_spec),
        ],
        gradient_scratch
        + [
            named.near_a(Scatter.near_scratch(n, (3, own, width))),
            named.near_b(Scatter.near_scratch(n, (own, width))),
            named.far_b(Scatter.far_scratch(n, (own, width))),
            named.out_sums(pltpu.VMEM((n // 2, own, width), bf16)),
        ]
        + attention_back_scratch(width, heads)
        + backward_scratch(n, cap, hidden, experts),
        3,
    )
    pack_rows = 16 + LAYERS * experts
    big, less = (3, own, width), (own, width)
    scatter_scratch = [
        named.far_a(Scatter.far_scratch(n, big)),
        named.near_c(Scatter.near_scratch(n, big)),
        named.near_d(Scatter.near_scratch(n, less)),
        named.far_c(Scatter.far_scratch(n, big)),
        named.far_d(Scatter.far_scratch(n, less)),
        named.qkv_sums(pltpu.VMEM((n // 2,) + big, bf16)),
        named.out_sums(pltpu.VMEM((n // 2,) + less, bf16)),
    ]
    final = call(
        final_program(n, experts, heads),
        wide_ins
        + index_ins[2:]
        + attention_back_ins(kept_of(first, first.wqkv_out, first.wo_out, tokens), fourth.midg)
        + [
            named.qkv_sums_next(fourth.qkv_sums, vmem_spec),
            named.out_late(fourth.out_late, vmem_spec),
            named.y_last(top.y, late_spec),
            named.gain_rows_0(fourth.gain_rows, vmem_spec),
            named.gain_rows_1(top.gain_rows, vmem_spec),
            named.router_g_0(fourth.router_g, vmem_spec),
            named.router_g_1(top.router_g, vmem_spec),
            named.table_next(fourth.table, vmem_spec),
        ],
        [
            named.output((SEQ, D), bf16, any_spec),
            named.dx_full((SEQ, D), bf16, any_spec),
            named.qkv_grad((LAYERS, 3, own, width), f32, vmem_spec),
            named.out_grad((LAYERS, own, width), f32, vmem_spec),
            named.small_out((SLICES, pack_rows, HALF), f32, vmem_spec),
        ],
        gradient_scratch
        + attention_back_scratch(width, heads)
        + scatter_scratch
        + [
            named.table(pltpu.VMEM((8, LANES), f32)),
            named.output_buf(pltpu.VMEM((SLICES, SEQ, HALF), bf16)),
            named.output_gather(Gather.scratch),
            named.dx_buf(pltpu.VMEM((SLICES, SEQ, HALF), bf16)),
            named.dx_gather(Gather.scratch),
            named.pack(pltpu.VMEM((pack_rows, HALF), f32)),
            named.packs(pltpu.VMEM((n, pack_rows, HALF), f32)),
            named.pack_send(pltpu.SemaphoreType.DMA((n,))),
            named.pack_recv(pltpu.SemaphoreType.DMA((n,))),
            named.all_send(pltpu.SemaphoreType.DMA((3,))),
            named.all_recv(pltpu.SemaphoreType.DMA((3,))),
            named.save_sems(pltpu.SemaphoreType.DMA((32,))),
        ],
        4,
    )
    grads = [[one.wg_grad, one.wu_grad, one.wd_grad] for one in (fourth, top)]
    gate_g, up_g, down_g, output, dx_wide, qkv_grad, out_grad = widen(
        grads, [final.output, final.dx_full, final.qkv_grad, final.out_grad]
    )
    d, t = lax.axis_index("dp"), lax.axis_index("tensor")
    small_sum = final.small_out

    def rows_wide(start, count):
        wide = small_sum[:, start : start + count].transpose(1, 0, 2).reshape(count, D)
        return lax.dynamic_slice_in_dim(wide, d * own, own, 1)

    gains_grad = rows_wide(0, 2 * LAYERS).reshape(LAYERS, 2, own)
    router_grad = rows_wide(16, LAYERS * experts).reshape(LAYERS, experts, own).transpose(0, 2, 1)
    table_all = lax.dynamic_slice_in_dim(small_sum, t, 1, 0)[0, 8 : 8 + heads].reshape(heads, LAYERS, LANES)
    table_grad = lax.dynamic_slice_in_dim(table_all, d * (BUCKETS // n), BUCKETS // n, 2).transpose(1, 2, 0)
    return (
        output,
        dx_wide,
        qkv_grad,
        out_grad,
        router_grad,
        gains_grad,
        table_grad,
        gate_g.transpose(0, 1, 3, 2),
        up_g.transpose(0, 1, 3, 2),
        down_g,
    )


def solution(mesh):
    placed = (
        P("dp", None),
        P("dp", None),
        P(None, None, "dp", "tensor"),
        P(None, "dp", "tensor"),
        P(None, "dp", None),
        P(None, None, "dp"),
        P(None, "dp", "tensor"),
        P(None, "dp", None, "tensor"),
        P(None, "dp", None, "tensor"),
        P(None, "dp", "tensor", None),
        P(None, "dp", None),
        P(None, "dp", None),
        P("dp"),
    )
    return jax.shard_map(
        local,
        mesh=mesh,
        in_specs=placed,
        out_specs=(P("dp", None), P("dp", None)) + placed[2:10],
        check_vma=False,
    )
```

```python
import types

import jax
import jax.numpy as jnp
from jax import lax
from jax.experimental import pallas as pl
from jax.experimental.pallas import tpu as pltpu
from jax.sharding import PartitionSpec as P

D = 1024
HDIM = 64
SEQ = 512
LAYERS = 2
BUCKETS = 32
HALF = 256
SLICES = 4
WINDOW_CHUNKS = 2
STAGE_LAGS = (1, 2, 3, 4)
LANES = 128
WINDOW = 768

eps_norm = 1e-06
rise_points = (12, 16, 23, 32, 46, 64, 91)
masked_score = -1e30
vmem_bytes = 63 * 1024 * 1024
f32 = jnp.float32
bf16 = jnp.bfloat16
MESH = pl.DeviceIdType.MESH
nn_dims = (((1,), (0,)), ((), ()))
nt_dims = (((1,), (1,)), ((), ()))
tn_dims = (((0,), (0,)), ((), ()))
vmem_spec = pl.BlockSpec(memory_space=pltpu.VMEM)
any_spec = pl.BlockSpec(memory_space=pl.ANY)
late_spec = pl.BlockSpec(memory_space=pl.ANY)
saved_spec = pl.BlockSpec(memory_space=pl.ANY)


def nn(a, b):
    return lax.dot_general(a, b, nn_dims, preferred_element_type=f32)


def nt(a, b):
    return lax.dot_general(a, b, nt_dims, preferred_element_type=f32)


def tn(a, b):
    return lax.dot_general(a, b, tn_dims, preferred_element_type=f32)


def shaped(shape, kind):
    return jax.ShapeDtypeStruct(shape, kind)


def bucket_index(offset):
    upward = jnp.where(offset > 0, BUCKETS // 2, 0)
    distance = jnp.abs(offset)
    far_part = 8 + sum(((distance >= rise_point).astype(jnp.int32) for rise_point in rise_points))
    return upward + jnp.where(distance < 8, distance, far_part)


def toeplitz_bias(row):
    tile = jnp.broadcast_to(row, (HALF, WINDOW))
    rolled = pltpu.roll(tile, WINDOW - HALF + 1, 1, stride=1, stride_axis=0)
    return rolled[:, : 2 * HALF]


def diagonal_sums(grad):
    rows = jnp.concatenate([grad, jnp.zeros((HALF, WINDOW - 2 * HALF), f32)], axis=1)
    count = HALF
    while count > 8:
        count //= 2
        rows = rows[:count] + pltpu.roll(rows[count:], WINDOW - count, 1)
    total = jnp.zeros((8, WINDOW), f32)
    place = lax.broadcasted_iota(jnp.int32, (8, WINDOW), 0)
    for i in range(8):
        moved = pltpu.roll(rows, (HALF - 1 - i) % WINDOW, 1)
        total = total + jnp.where(place == i, moved, 0.0)
    return total


def half_lanes(shape, which):
    lane = lax.broadcasted_iota(jnp.int32, shape, 1)
    return (lane < HDIM) if which == 0 else (lane >= HDIM)


def allowed_tile(seg_col, seg_row):
    i = lax.broadcasted_iota(jnp.int32, (HALF, HALF), 0)
    j = lax.broadcasted_iota(jnp.int32, (HALF, HALF), 1)
    return (j <= i) | ((seg_col == seg_row) & (seg_col > 0))


def masked_scores(query, keys, bias, allowed, block):
    raw = nt(query, keys)
    if block == 0:
        return jnp.where(allowed, raw + bias[:, HALF:], masked_score)
    left = raw[:, :HALF] + bias[:, :HALF]
    right = jnp.where(allowed, raw[:, HALF:] + bias[:, HALF:], masked_score)
    return jnp.concatenate([left, right], axis=1)


def bias_rows(table):
    place = lax.broadcasted_iota(jnp.int32, (BUCKETS, WINDOW), 1) - (SEQ - 1)
    hot = (bucket_index(place) == lax.broadcasted_iota(jnp.int32, (BUCKETS, WINDOW), 0)).astype(bf16)
    return nn(table, hot)


def block_rows(block):
    return slice(block * HALF, (block + 1) * HALF)


def attend_block(m, block, first_head):
    width = m.ctx.shape[1]
    rows = block_rows(block)
    count = (block + 1) * HALF
    lane = lax.broadcasted_iota(jnp.int32, (HALF, LANES), 1)
    allowed = allowed_tile(m.seg_col[rows, :1], m.seg_row[:, rows])
    lse = jnp.zeros((HALF, LANES), f32)
    for pair in range(width // LANES):
        cols = slice(pair * LANES, (pair + 1) * LANES)
        q2 = m.proj[rows, cols]
        k2 = m.proj[:count, width + pair * LANES : width + (pair + 1) * LANES]
        v2 = m.proj[:count, 2 * width + pair * LANES : 2 * width + (pair + 1) * LANES]
        outs = []
        for which in range(2):
            head = 2 * pair + which
            scaled = q2 * jnp.asarray(HDIM**-0.5, bf16)
            qm = jnp.where(half_lanes(q2.shape, which), scaled, jnp.zeros_like(q2))
            bias = toeplitz_bias(m.bias[first_head + head : first_head + head + 1])
            scores = masked_scores(qm, k2, bias, allowed, block)
            top = jnp.max(scores, axis=1, keepdims=True)
            powers = jnp.exp(scores - top)
            total = jnp.sum(powers, axis=1, keepdims=True)
            probs = (powers * (1.0 / total)).astype(bf16)
            outs.append(nn(probs, v2))
            lse = jnp.where(lane == head, top + jnp.log(total), lse)
        m.ctx[rows, cols] = jnp.where(half_lanes(outs[0].shape, 0), outs[0], outs[1]).astype(bf16)
    m.lse[rows, :] = lse


def wide_rows(ref, rows):
    return jnp.concatenate([ref[q, rows] for q in range(SLICES)], axis=1)


def project(m, block, c):
    width = m.ctx.shape[1]
    rows = block_rows(block)
    m.proj[rows, c * width : (c + 1) * width] = (
        nn(wide_rows(m.hg, rows), m.wqkv[c]) * m.r1[rows, :1]
    ).astype(bf16)


def project_out(m, block):
    rows = block_rows(block)
    for q in range(SLICES):
        m.part[q, rows] = nt(m.ctx[rows], m.wo[q * HALF : (q + 1) * HALF, :]).astype(bf16)


def attention_block(m, block, first_head, between):
    for c in range(3):
        project(m, block, c)
    between()
    attend_block(m, block, first_head)
    project_out(m, block)


def prob_cols(block):
    return slice(0, HALF) if block == 0 else slice(HALF, 3 * HALF)


def attention_probs(m, block, first_head):
    width = m.ctx.shape[1]
    rows = block_rows(block)
    count = (block + 1) * HALF
    allowed = allowed_tile(m.seg_col[rows, :1], m.seg_row[:, rows])
    scale = jnp.asarray(HDIM**-0.5, bf16)
    for head in range(width // HDIM):
        pair, which = head // 2, head % 2
        q2 = m.proj[rows, pair * LANES : (pair + 1) * LANES]
        k2 = m.proj[:count, width + pair * LANES : width + (pair + 1) * LANES]
        qm = jnp.where(half_lanes(q2.shape, which), q2 * scale, jnp.zeros_like(q2))
        bias = toeplitz_bias(m.bias[first_head + head : first_head + head + 1])
        scores = masked_scores(qm, k2, bias, allowed, block)
        m.probs[head, :, prob_cols(block)] = jnp.exp(scores - m.lse[rows, head : head + 1])


def attention_back_block(m, block, between):
    width = m.ctx.shape[1]
    rows = block_rows(block)
    count = (block + 1) * HALF
    dctx = nn(wide_rows(m.ag, rows), m.wo[...]).astype(bf16)
    scale = jnp.asarray(HDIM**-0.5, bf16)
    for pair in range(width // LANES):
        if pair == 1:
            between()
        cols = slice(pair * LANES, (pair + 1) * LANES)
        q2 = m.proj[rows, cols]
        k2 = m.proj[:count, width + pair * LANES : width + (pair + 1) * LANES]
        v2 = m.proj[:count, 2 * width + pair * LANES : 2 * width + (pair + 1) * LANES]
        g2 = dctx[:, cols]
        outs = []
        dk = None
        dv = None
        for which in range(2):
            head = 2 * pair + which
            mine = half_lanes(q2.shape, which)
            qm = jnp.where(mine, q2 * scale, jnp.zeros_like(q2))
            gm = jnp.where(mine, g2, jnp.zeros_like(g2))
            probs = m.probs[head, :, prob_cols(block)]
            prob_grad = nt(gm, v2).astype(bf16).astype(f32)
            inner = jnp.sum(probs * prob_grad, axis=1, keepdims=True)
            grad_low = (probs * (prob_grad - inner)).astype(bf16)
            dv_one = tn(probs.astype(bf16), gm)
            dk_one = tn(grad_low, qm)
            dv = dv_one if dv is None else dv + dv_one
            dk = dk_one if dk is None else dk + dk_one
            outs.append(nn(grad_low, k2))
            wide = grad_low.astype(f32)
            if block == 1:
                m.bias_grad[head] = wide
            else:
                m.bias_grad[head, :, HALF:] = m.bias_grad[head, :, HALF:] + wide
        dq = jnp.where(half_lanes(outs[0].shape, 0), outs[0], outs[1]) * HDIM**-0.5
        if block == 1:
            m.dk[:, cols] = dk
            m.dv[:, cols] = dv
        else:
            m.dk[:HALF, cols] = m.dk[:HALF, cols] + dk
            m.dv[:HALF, cols] = m.dv[:HALF, cols] + dv
        m.pg[rows, cols] = dq.astype(bf16)
        m.pg[rows, width + pair * LANES : width + (pair + 1) * LANES] = m.dk[rows, cols].astype(bf16)
        m.pg[rows, 2 * width + pair * LANES : 2 * width + (pair + 1) * LANES] = m.dv[rows, cols].astype(bf16)
    dots = None
    for q in range(SLICES):
        total = None
        for c in range(3):
            one = nt(m.pg[rows, c * width : (c + 1) * width], m.wqkv[c, q * HALF : (q + 1) * HALF, :])
            total = one if total is None else total + one
        m.part[q, rows] = total.astype(bf16)
        product = jnp.sum(total * m.hg[q, rows].astype(f32), axis=1, keepdims=True)
        dots = product if dots is None else dots + product
    return dots


def table_gradient(m):
    place = lax.broadcasted_iota(jnp.int32, (8, WINDOW), 0)
    diag_all = jnp.zeros((8, WINDOW), f32)
    for head in range(m.bias_grad.shape[0]):
        sums = jnp.sum(diagonal_sums(m.bias_grad[head]), axis=0, keepdims=True)
        diag_all = jnp.where(place == head, sums, diag_all)
    spot = lax.broadcasted_iota(jnp.int32, (WINDOW, LANES), 0) - (SEQ - 1)
    hot = (bucket_index(spot) == lax.broadcasted_iota(jnp.int32, (WINDOW, LANES), 1)).astype(f32)
    return lax.dot_general(
        diag_all, hot, nn_dims, precision=lax.Precision.HIGHEST, preferred_element_type=f32
    )


def out_gradient(m):
    for q in range(SLICES):
        m.wog[q * HALF : (q + 1) * HALF] = tn(m.ag[q], m.ctx[...]).astype(bf16)


def qkv_gradient(m):
    width = m.ctx.shape[1]
    for q in range(SLICES):
        normed = (m.hg[q].astype(f32) * m.r1[:, :1]).astype(bf16)
        for c in range(3):
            m.qkvg[c, q * HALF : (q + 1) * HALF] = tn(normed, m.pg[:, c * width : (c + 1) * width]).astype(bf16)


def places():
    d = lax.axis_index("dp")
    t = lax.axis_index("tensor")
    sib = t + 1 - 2 * lax.rem(t, 2)
    far = lax.rem(t + 2, SLICES)
    opp = SLICES - 1 - t
    return d, t, sib, far, opp


def remote(src, dst, send, recv, device):
    return pltpu.make_async_remote_copy(
        src_ref=src, dst_ref=dst, send_sem=send, recv_sem=recv, device_id=device, device_id_type=MESH
    )


def greet(n, with_dp):
    d, t, sib, far, opp = places()
    barrier = pltpu.get_barrier_semaphore()
    for peer in (sib, far, opp):
        pl.semaphore_signal(barrier, inc=1, device_id=(d, peer), device_id_type=MESH)
    if with_dp:

        def hello(j, carry):
            pl.semaphore_signal(barrier, inc=1, device_id=(lax.rem(d + j, n), t), device_id_type=MESH)
            return carry

        lax.fori_loop(1, n, hello, 0)
    pl.semaphore_wait(barrier, 3 + (n - 1 if with_dp else 0))


class Tiny:
    scratch = lambda rows, cols: [
        pltpu.VMEM((SLICES, rows, cols), f32),
        pltpu.SemaphoreType.DMA((3,)),
        pltpu.SemaphoreType.DMA((3,)),
    ]

    def __init__(self, refs):
        self.buf, self.send, self.recv = refs

    def copies(self):
        d, t, sib, far, opp = places()
        return [
            remote(self.buf.at[t], self.buf.at[t], self.send.at[i], self.recv.at[i], (d, peer))
            for i, peer in enumerate((sib, far, opp))
        ]

    def start(self, tile):
        d, t, sib, far, opp = places()
        self.buf[t] = tile
        for copy in self.copies():
            copy.start()

    def finish(self):
        for copy in self.copies():
            copy.wait()

    def total(self):
        self.finish()
        return (self.buf[0] + self.buf[1]) + (self.buf[2] + self.buf[3])


class Gather:
    scratch = [pltpu.SemaphoreType.DMA((2, 3)), pltpu.SemaphoreType.DMA((2, 3))]

    def __init__(self, buf, refs):
        self.buf = buf
        self.send, self.recv = refs

    def copies(self, b):
        d, t, sib, far, opp = places()
        rows = pl.ds(b * HALF, HALF)
        mine, others = self.buf.at[t, rows], self.buf.at[far, rows]
        return [
            lambda: remote(mine, mine, self.send.at[b, 0], self.recv.at[b, 0], (d, far)),
            lambda: remote(mine, mine, self.send.at[b, 1], self.recv.at[b, 1], (d, sib)),
            lambda: remote(others, others, self.send.at[b, 2], self.recv.at[b, 2], (d, sib)),
        ]

    def start(self, b, tile):
        d, t, sib, far, opp = places()
        self.buf[t, pl.ds(b * HALF, HALF)] = tile
        far_copy, near_copy, pass_copy = self.copies(b)
        far_copy().start()
        near_copy().start()

    def forward(self, b):
        far_copy, near_copy, pass_copy = self.copies(b)
        far_copy().wait_recv()
        pass_copy().start()

    def finish(self, b):
        far_copy, near_copy, pass_copy = self.copies(b)
        near_copy().wait_recv()
        pass_copy().wait_recv()

    def wait_sends(self):
        for b in range(2):
            for copy in self.copies(b):
                copy().wait_send()


class Reduce:
    scratch = [
        pltpu.VMEM((2, SEQ, HALF), bf16),
        pltpu.VMEM((2, SEQ, HALF), bf16),
        pltpu.SemaphoreType.DMA((2, 3)),
        pltpu.SemaphoreType.DMA((2, 3)),
    ]

    def __init__(self, part, refs):
        self.part = part
        self.near, self.across, self.send, self.recv = refs

    def copies(self, b):
        d, t, sib, far, opp = places()
        rows = pl.ds(b * HALF, HALF)

        def one(i, src, dst, peer):
            return lambda: remote(src, dst, self.send.at[b, i], self.recv.at[b, i], (d, peer))

        return [
            one(0, self.part.at[opp, rows], self.near.at[1, rows], sib),
            one(1, self.part.at[sib, rows], self.near.at[0, rows], sib),
            one(2, self.across.at[0, rows], self.across.at[1, rows], far),
        ]

    def start(self, b):
        first, second, third = self.copies(b)
        first().start()
        second().start()

    def middle(self, b):
        d, t, sib, far, opp = places()
        rows = pl.ds(b * HALF, HALF)
        first, second, third = self.copies(b)
        first().wait_recv()
        self.across[0, rows] = (self.part[far, rows].astype(f32) + self.near[1, rows].astype(f32)).astype(bf16)
        third().start()

    def finish(self, b):
        d, t, sib, far, opp = places()
        rows = pl.ds(b * HALF, HALF)
        first, second, third = self.copies(b)
        second().wait_recv()
        mine = self.part[t, rows].astype(f32) + self.near[0, rows].astype(f32)
        third().wait_recv()
        return mine + self.across[1, rows].astype(f32)

    def wait_sends(self):
        for b in range(2):
            for copy in self.copies(b):
                copy().wait_send()


class Saves:
    def __init__(self, sems):
        self.sems, self.copies = sems, []

    def start(self, src, dst, span=None):
        place = len(self.copies)

        def copy():
            if span is None:
                return pltpu.make_async_copy(src, dst, self.sems.at[place])
            return pltpu.make_async_copy(src.at[span], dst.at[span], self.sems.at[place])

        copy().start()
        self.copies.append(copy)

    def wait(self):
        for copy in self.copies:
            copy().wait()


def to_row(col):
    return jnp.transpose(jnp.broadcast_to(col, (col.shape[0], LANES)))[:8]


def to_cols(rows8):
    return jnp.transpose(jnp.concatenate([rows8] * (LANES // 8), axis=0))


def int_cols(rows):
    whole = jnp.concatenate([rows.astype(f32)] * (8 // rows.shape[0]), axis=0)
    return to_cols(whole).astype(jnp.int32)


def pick_slice(wide):
    t = lax.axis_index("tensor")
    out = wide[:, :HALF]
    for q in range(1, SLICES):
        out = jnp.where(t == q, wide[:, q * HALF : (q + 1) * HALF], out)
    return out


def hot_columns(targ, k, count):
    return (targ[:, k : k + 1] == lax.broadcasted_iota(jnp.int32, (SEQ, count), 1)).astype(f32).astype(bf16)


class Route:
    @staticmethod
    def piece(cap):
        return 32 if cap % 32 == 0 else 16

    @staticmethod
    def shape(n, cap):
        piece = Route.piece(cap)
        return cap // piece, n * piece

    @staticmethod
    def slots(chunks, rounds):
        return chunks if rounds == 1 else max(chunks, STAGE_LAGS[3] + 1)

    @staticmethod
    def scratch(n, cap, rounds):
        chunks, rows = Route.shape(n, cap)
        slots = Route.slots(chunks, rounds)
        total = chunks * rounds
        return [
            pltpu.VMEM((total, rows, HALF), bf16),
            pltpu.VMEM((total, SLICES, rows, HALF), bf16),
            pltpu.VMEM((slots, SLICES, rows, HALF), bf16),
            pltpu.VMEM((slots, 2, rows, HALF), bf16),
            pltpu.VMEM((slots, rows, HALF), bf16),
            pltpu.VMEM((slots, rows, HALF), bf16),
            pltpu.VMEM((slots, rows, HALF), bf16),
            pltpu.VMEM((total, rows, HALF), bf16),
            pltpu.SemaphoreType.DMA((total, n)),
            pltpu.SemaphoreType.DMA((total, n)),
            pltpu.SemaphoreType.DMA((3, total)),
            pltpu.SemaphoreType.DMA((3, total)),
            pltpu.SemaphoreType.DMA((3, total)),
            pltpu.SemaphoreType.DMA((3, total)),
            pltpu.SemaphoreType.DMA((total, n)),
            pltpu.SemaphoreType.DMA((total, n)),
        ]

    def __init__(self, n, cap, rounds, refs):
        self.n = n
        self.window = WINDOW_CHUNKS if rounds == 1 else 1
        self.size = Route.piece(cap)
        self.chunks, self.rows = Route.shape(n, cap)
        self.slot_count = Route.slots(self.chunks, rounds)
        self.total = self.chunks * rounds
        (
            self.out,
            self.x,
            self.p,
            self.ra,
            self.sb,
            self.rb,
            self.ro,
            self.ret,
            self.as_,
            self.ar,
            self.fs,
            self.fr,
            self.ps,
            self.pr,
            self.rs,
            self.rr,
        ) = refs

    def span(self, place):
        return pl.ds(pl.multiple_of(place * self.size, 16), self.size)

    def peers(self, action):
        d = lax.axis_index("dp")

        def one(j, carry):
            action(lax.rem(d + j, self.n))
            return carry

        lax.fori_loop(1, self.n, one, 0)

    def out_copy(self, chunk, source, expert):
        d, t, sib, far, opp = places()
        return remote(
            self.out.at[chunk, self.span(expert)],
            self.x.at[chunk, t, self.span(source)],
            self.as_.at[chunk, expert],
            self.ar.at[chunk, source],
            (expert, t),
        )

    def back_copy(self, chunk, source, expert):
        d, t, sib, far, opp = places()
        return remote(
            self.ro.at[self.slot(chunk), self.span(source)],
            self.ret.at[chunk, self.span(expert)],
            self.rs.at[chunk, source],
            self.rr.at[chunk, expert],
            (source, t),
        )

    def spread_copies(self, chunk):
        d, t, sib, far, opp = places()
        mine, others = self.x.at[chunk, t], self.x.at[chunk, far]
        return [
            lambda: remote(mine, mine, self.fs.at[0, chunk], self.fr.at[0, chunk], (d, far)),
            lambda: remote(mine, mine, self.fs.at[1, chunk], self.fr.at[1, chunk], (d, sib)),
            lambda: remote(others, others, self.fs.at[2, chunk], self.fr.at[2, chunk], (d, sib)),
        ]

    def slot(self, chunk):
        return chunk if self.slot_count == self.total else lax.rem(chunk, self.slot_count)

    def reused(self, chunk, action):
        if self.slot_count < self.total:

            @pl.when(chunk >= self.slot_count)
            def _():
                action(chunk - self.slot_count)

    def sum_copies(self, chunk):
        d, t, sib, far, opp = places()
        p, ps, pr = self.p, self.ps, self.pr
        slot = self.slot(chunk)
        return [
            lambda: remote(p.at[slot, opp], self.ra.at[slot, 1], ps.at[0, chunk], pr.at[0, chunk], (d, sib)),
            lambda: remote(p.at[slot, sib], self.ra.at[slot, 0], ps.at[1, chunk], pr.at[1, chunk], (d, sib)),
            lambda: remote(self.sb.at[slot], self.rb.at[slot], ps.at[2, chunk], pr.at[2, chunk], (d, far)),
        ]

    def send(self, chunk, fill):
        d, t, sib, far, opp = places()
        fill(chunk)
        self.peers(lambda e: self.out_copy(chunk, d, e).start())
        self.x[chunk, t, self.span(d)] = self.out[chunk, self.span(d)]

    def begin(self, fill_first, fill):
        self.fill = fill
        for chunk in range(self.window):
            self.send(chunk, fill_first)

    def put(self, chunk, products):
        for q in range(SLICES):
            self.p[self.slot(chunk), q] = products[:, q * HALF : (q + 1) * HALF].astype(bf16)

    def run(self, compute, hook):
        d, t, sib, far, opp = places()

        def more(chunk):
            self.send(chunk, self.fill)

        def arrive(chunk):
            self.peers(lambda s: self.out_copy(chunk, s, s).wait_recv())
            far_copy, near_copy, pass_copy = self.spread_copies(chunk)
            far_copy().start()
            near_copy().start()

        def forward(chunk):
            far_copy, near_copy, pass_copy = self.spread_copies(chunk)
            far_copy().wait_recv()
            pass_copy().start()

        def work(chunk):
            far_copy, near_copy, pass_copy = self.spread_copies(chunk)
            near_copy().wait_recv()
            pass_copy().wait_recv()
            rows = jnp.concatenate([self.x[chunk, q] for q in range(SLICES)], axis=1)

            def sent(old):
                first, second, third = self.sum_copies(old)
                first().wait_send()
                second().wait_send()

            self.reused(chunk, sent)
            compute(chunk, rows)
            first, second, third = self.sum_copies(chunk)
            first().start()
            second().start()

        def add_near(chunk):
            first, second, third = self.sum_copies(chunk)
            first().wait_recv()
            slot = self.slot(chunk)
            self.reused(chunk, lambda old: self.sum_copies(old)[2]().wait_send())
            self.sb[slot] = (self.p[slot, far].astype(f32) + self.ra[slot, 1].astype(f32)).astype(bf16)
            third().start()

        def add_far(chunk):
            first, second, third = self.sum_copies(chunk)
            second().wait_recv()
            third().wait_recv()
            slot = self.slot(chunk)
            self.reused(chunk, lambda old: self.peers(lambda s: self.back_copy(old, s, d).wait_send()))
            mine = self.p[slot, t].astype(f32) + self.ra[slot, 0].astype(f32)
            self.ro[slot] = (mine + self.rb[slot].astype(f32)).astype(bf16)
            self.peers(lambda s: self.back_copy(chunk, s, d).start())
            self.ret[chunk, self.span(d)] = self.ro[slot, self.span(d)]

        stages = (
            (more, -self.window),
            (arrive, 0),
            (forward, STAGE_LAGS[0]),
            (work, STAGE_LAGS[1]),
            (add_near, STAGE_LAGS[2]),
            (add_far, STAGE_LAGS[3]),
        )

        def step(i, carry):
            for stage, lag in stages:

                @pl.when((i >= lag) & (i < self.total + lag))
                def _(stage=stage, lag=lag):
                    stage(i - lag)

            if hook is not None:
                hook(i)
            return carry

        lax.fori_loop(0, self.total + stages[-1][1], step, 0)

    def wait_back(self, first):
        d = lax.axis_index("dp")

        def one(chunk, carry):
            self.peers(lambda e: self.back_copy(chunk, d, e).wait_recv())
            return carry

        lax.fori_loop(first, first + self.chunks, one, 0)

    def returned(self, first):
        return self.ret[first : first + self.chunks].reshape(self.chunks * self.rows, HALF)

    def arrived(self, first, q):
        return self.x[first : first + self.chunks, q].reshape(self.chunks * self.rows, HALF)

    def wait_sends(self):
        d = lax.axis_index("dp")

        def one(chunk, carry):
            self.peers(lambda e: self.out_copy(chunk, d, e).wait_send())
            for copy in self.spread_copies(chunk):
                copy().wait_send()
            return carry

        lax.fori_loop(0, self.total, one, 0)

        def two(chunk, carry):
            self.peers(lambda e: self.back_copy(chunk, e, d).wait_send())
            for copy in self.sum_copies(chunk):
                copy().wait_send()
            return carry

        lax.fori_loop(self.total - self.slot_count, self.total, two, 0)


gelu_c = 0.7978845608028654
gelu_a = 0.044715


class Named:
    def __getattr__(self, name):
        return lambda *rest: (name, *rest)


named = Named()


def call(fn, ins, outs, scratch, collective_id):
    late = [one for one in ins if one[2] is late_spec]
    saved = [one for one in outs if one[3] is saved_spec]

    def kernel(*refs):
        refs = list(refs)
        m = types.SimpleNamespace(outs=types.SimpleNamespace())
        late_refs = []
        for one in ins:
            ref = refs.pop(0)
            if one[2] is late_spec:
                late_refs.append(ref)
            else:
                setattr(m, one[0], ref)
        for one in outs:
            setattr(m.outs if one[3] is saved_spec else m, one[0], refs.pop(0))
        copies = []
        if late:
            sems = refs.pop(0)
            for i, one in enumerate(late):
                buffer = refs.pop(0)
                setattr(m, one[0], buffer)
                copies.append(pltpu.make_async_copy(late_refs[i], buffer, sems.at[i]))
        for one in saved:
            setattr(m, one[0], refs.pop(0))
        for name, kinds in scratch:
            if isinstance(kinds, list):
                setattr(m, name, [refs.pop(0) for one in kinds])
            else:
                setattr(m, name, refs.pop(0))

        def late_wait():
            for copy in copies:
                copy.wait()

        m.late_wait = late_wait
        for copy in copies:
            copy.start()
        fn(m)

    flat = []
    if late:
        flat.append(pltpu.SemaphoreType.DMA((len(late),)))
        flat += [pltpu.VMEM(one[1].shape, one[1].dtype) for one in late]
    flat += [pltpu.VMEM(one[1], one[2]) for one in saved]
    for name, kinds in scratch:
        flat += kinds if isinstance(kinds, list) else [kinds]
    results = pl.pallas_call(
        kernel,
        name=fn.__name__,
        out_shape=[shaped(one[1], one[2]) for one in outs],
        in_specs=[one[2] for one in ins],
        out_specs=[one[3] for one in outs],
        scratch_shapes=flat,
        compiler_params=pltpu.CompilerParams(
            vmem_limit_bytes=vmem_bytes, collective_id=collective_id, has_side_effects=True
        ),
    )(*[one[1] for one in ins])
    return types.SimpleNamespace(**{one[0]: result for one, result in zip(outs, results)})


def gain_of(m, layer, which):
    t = lax.axis_index("tensor")
    return m.wide[t, 2 * layer + which : 2 * layer + which + 1].astype(f32)


def router_of(m, layer, experts):
    t = lax.axis_index("tensor")
    start = 2 * LAYERS + layer * experts
    return m.wide[t][start : start + experts]


def cap_count(cap):
    return 3 * SEQ // cap


def save_attention(m, saves):
    for buffer, out in ((m.proj, m.outs.proj), (m.lse, m.outs.lse), (m.ctx, m.outs.ctx), (m.r1, m.outs.r1)):
        saves.start(buffer, out)


def set_targets(m, layer, cap):
    piece = Route.piece(cap)
    chunks, rows = Route.shape(cap_count(cap), cap)
    slots = m.slots_row[layer]
    m.targ_row[...] = (slots // piece) * rows + m.routes_row[layer] * piece + lax.rem(slots, piece)
    m.targ_col[...] = int_cols(m.targ_row[...])


def set_attention_tables(m):
    m.seg_col[...] = int_cols(m.seg_row[...])
    m.bias[...] = bias_rows(m.tab[:, :BUCKETS].astype(bf16))


attention_scratch = [
    named.seg_col(pltpu.VMEM((SEQ, LANES), jnp.int32)),
    named.bias(pltpu.VMEM((8, WINDOW), f32)),
    named.part(pltpu.VMEM((SLICES, SEQ, HALF), bf16)),
    named.reduce(Reduce.scratch),
]


def attention_outs(width):
    return [
        named.proj((SEQ, 3 * width), bf16, saved_spec),
        named.lse((SEQ, LANES), f32, saved_spec),
        named.ctx((SEQ, width), bf16, saved_spec),
        named.r1((SEQ, LANES), f32, saved_spec),
    ]


def forward_outs(n, cap, hidden):
    chunks, rows = Route.shape(n, cap)
    return [
        named.mid((SEQ, HALF), f32, saved_spec),
        named.normed((SEQ, HALF), bf16, saved_spec),
        named.r2((SEQ, LANES), f32, saved_spec),
        named.gates((SEQ, LANES), f32, saved_spec),
        named.picked((2, SEQ, HALF), bf16, saved_spec),
        named.y((SEQ, HALF), f32, saved_spec),
        named.x_out((chunks, SLICES, rows, HALF), bf16, any_spec),
        named.inner_out((chunks, rows, hidden), bf16, any_spec),
        named.act_out((chunks, rows, hidden), bf16, any_spec),
        named.slope_out((chunks, rows, hidden), bf16, any_spec),
        named.wg_out((hidden, D), bf16, any_spec),
        named.wu_out((hidden, D), bf16, any_spec),
        named.wd_out((hidden, D), bf16, any_spec),
    ]


def forward_scratch(n, cap, hidden, experts):
    chunks, rows = Route.shape(n, cap)
    return [
        named.wg_stage(pltpu.VMEM((hidden, D), f32)),
        named.wu_stage(pltpu.VMEM((hidden, D), f32)),
        named.wd_stage(pltpu.VMEM((hidden, D), f32)),
        named.wg(pltpu.VMEM((hidden, D), bf16)),
        named.wu(pltpu.VMEM((hidden, D), bf16)),
        named.wd(pltpu.VMEM((hidden, D), bf16)),
        named.inner(pltpu.VMEM((chunks, rows, hidden), bf16)),
        named.act(pltpu.VMEM((chunks, rows, hidden), bf16)),
        named.slope(pltpu.VMEM((chunks, rows, hidden), bf16)),
        named.hot(pltpu.VMEM((2, SEQ, n * cap), bf16)),
        named.targ_row(pltpu.VMEM((2, SEQ), jnp.int32)),
        named.targ_col(pltpu.VMEM((SEQ, LANES), jnp.int32)),
        named.load_sems(pltpu.SemaphoreType.DMA((3,))),
        named.save_sems(pltpu.SemaphoreType.DMA((32,))),
        named.chunk_sems(pltpu.SemaphoreType.DMA((4, chunks))),
        named.tiny_one(Tiny.scratch(8, SEQ)),
        named.tiny_two(Tiny.scratch(experts, SEQ)),
        named.route(Route.scratch(n, cap, 1)),
    ]


def start_weight_loads(m, layer):
    loads = [
        pltpu.make_async_copy(src.at[layer, 0], dst, m.load_sems.at[i])
        for i, (src, dst) in enumerate(((m.gate_f, m.wg_stage), (m.up_f, m.wu_stage), (m.down_f, m.wd_stage)))
    ]
    for copy in loads:
        copy.start()
    return loads


def forward_rows(m, layer, experts, tiny_one, tiny_two, route):
    tiny_one.start(to_row(jnp.sum(m.mid[...] * m.mid[...], axis=1, keepdims=True)))
    scale = to_cols(lax.rsqrt(tiny_one.total() * (1.0 / D) + eps_norm))
    m.r2[...] = scale
    m.normed[...] = (m.mid[...] * scale[:, :1] * gain_of(m, layer, 1)).astype(bf16)

    def fill(chunk):
        number = chunk * route.rows + lax.broadcasted_iota(jnp.int32, (route.rows, SEQ), 0)
        hit = (m.targ_row[0:1] == number) | (m.targ_row[1:2] == number)
        route.out[chunk] = nn(hit.astype(f32).astype(bf16), m.normed[...]).astype(bf16)

    return fill


def narrow_weights(stage, low):
    def narrow(i, carry):
        rows = pl.ds(pl.multiple_of(i * 64, 64), 64)
        low[rows] = stage[rows].astype(bf16)
        return carry

    lax.fori_loop(0, low.shape[0] // 64, narrow, 0)


def router_gates(m, layer, tiny_two):
    logits = tiny_two.total()
    expert_no = lax.broadcasted_iota(jnp.int32, logits.shape, 0)
    chosen = [
        jnp.sum(jnp.where(expert_no == m.routes_row[layer, k : k + 1], logits, 0.0), axis=0, keepdims=True)
        for k in range(2)
    ]
    share = [1.0 / (1.0 + jnp.exp(chosen[1 - k] - chosen[k])) for k in range(2)]
    place = lax.broadcasted_iota(jnp.int32, (8, SEQ), 0)
    m.gates[...] = to_cols(jnp.where(place == 0, share[0], share[1]))


def forward_products(m, chunk, rows):
    gate_pre = nt(rows, m.wg[...])
    up_pre = nt(rows, m.wu[...])
    square = gate_pre * gate_pre
    bent = jnp.tanh(gelu_c * gate_pre * (1.0 + gelu_a * square))
    half = 0.5 * (1.0 + bent)
    active = gate_pre * half
    steep = half + 0.5 * gate_pre * (1.0 - bent * bent) * (gelu_c * (1.0 + 3.0 * gelu_a * square))
    inner_rows = (active * up_pre).astype(bf16)
    m.inner[chunk] = inner_rows
    m.act[chunk] = active.astype(bf16)
    m.slope[chunk] = (up_pre * steep).astype(bf16)
    return nn(inner_rows, m.wd[...])


def set_hot(m, count):
    for k in range(2):
        m.hot[k] = hot_columns(m.targ_col, k, count)


def forward_combine(m, route):
    route.wait_back(0)
    y = m.mid[...]
    for k in range(2):
        rows = nn(m.hot[k], route.returned(0))
        m.picked[k] = rows.astype(bf16)
        y = y + m.gates[:, k : k + 1] * rows
    m.y[...] = y


def forward_experts(m, n, cap, layer, experts, loads, saves, hook):
    tiny_one = Tiny(m.tiny_one)
    tiny_two = Tiny(m.tiny_two)
    route = Route(n, cap, 1, m.route)
    fill = forward_rows(m, layer, experts, tiny_one, tiny_two, route)
    route.begin(fill, fill)
    tiny_two.start(nt(router_of(m, layer, experts), m.normed[...]))
    for buffer, out in ((m.mid, m.outs.mid), (m.normed, m.outs.normed), (m.r2, m.outs.r2)):
        saves.start(buffer, out)
    stages = (m.wg_stage, m.wu_stage, m.wd_stage)
    lows = (m.wg, m.wu, m.wd)
    for copy, stage, low, out in zip(loads, stages, lows, (m.wg_out, m.wu_out, m.wd_out)):
        copy.wait()
        narrow_weights(stage, low)
        saves.start(low, out)
    router_gates(m, layer, tiny_two)
    saves.start(m.gates, m.outs.gates)

    def chunk_saves(chunk):
        pairs = ((route.x, m.x_out), (m.inner, m.inner_out), (m.act, m.act_out), (m.slope, m.slope_out))
        return [
            pltpu.make_async_copy(src.at[chunk], dst.at[chunk], m.chunk_sems.at[i, chunk])
            for i, (src, dst) in enumerate(pairs)
        ]

    def compute(chunk, rows):
        products = forward_products(m, chunk, rows)
        for copy in chunk_saves(chunk):
            copy.start()
        route.put(chunk, products)

    def hook_all(i):
        @pl.when(i == 2)
        def _():
            set_hot(m, n * cap)

        if hook is not None:
            hook(i)

    route.run(compute, hook_all)
    forward_combine(m, route)
    saves.start(m.picked, m.outs.picked)
    saves.start(m.y, m.outs.y)
    route.wait_sends()

    def drain(chunk, carry):
        for copy in chunk_saves(chunk):
            copy.wait()
        return carry

    lax.fori_loop(0, route.chunks, drain, 0)


class Pieces:
    def __init__(self, n, pieces, send, recv):
        self.n, self.pieces, self.send, self.recv = n, pieces, send, recv

    def copies(self, piece, k):
        d, t, sib, far, opp = places()
        n = self.n
        near = d + 1 - 2 * lax.rem(d, 2)
        view, src = self.pieces[piece]
        peer = lax.rem(d + 2 * k, n)
        source = lax.rem(d - 2 * k + n, n)
        send, recv = self.send, self.recv
        return (
            lambda: remote(src, view(d), send.at[piece, 0, k], recv.at[piece, 0, k], (peer, t)),
            lambda: remote(view(source), view(source), send.at[piece, 1, k], recv.at[piece, 1, k], (near, t)),
        )

    def own(self, piece):
        d, t, sib, far, opp = places()
        near = d + 1 - 2 * lax.rem(d, 2)
        view, src = self.pieces[piece]
        return remote(src, view(d), self.send.at[piece, 1, 0], self.recv.at[piece, 1, 0], (near, t))

    def loop(self, action):
        def one(k, carry):
            action(k)
            return carry

        lax.fori_loop(1, self.n // 2, one, 0)

    def start(self, piece):
        self.loop(lambda k: self.copies(piece, k)[0]().start())
        self.own(piece).start()

    def forward_one(self, piece, k):
        direct, passed = self.copies(piece, k)
        direct().wait_recv()
        passed().start()

    def forward(self, piece):
        self.loop(lambda k: self.forward_one(piece, k))

    def finish(self, piece):
        self.own(piece).wait_recv()
        self.loop(lambda k: self.copies(piece, k)[1]().wait_recv())

    def wait_sends(self, piece):
        self.own(piece).wait_send()

        def one(k):
            direct, passed = self.copies(piece, k)
            direct().wait_send()
            passed().wait_send()

        self.loop(one)


def set_small(m, heads):
    own = m.small.shape[1]
    shape = (LAYERS * heads, own)
    row = lax.broadcasted_iota(jnp.int32, shape, 0)
    lane = lax.broadcasted_iota(jnp.int32, shape, 1)
    table = jnp.zeros(shape, f32)
    for layer in range(LAYERS):
        for j in range(m.table.shape[1]):
            for head in range(heads):
                value = m.table[layer, j : j + 1, head : head + 1]
                table = jnp.where((row == layer * heads + head) & (lane == j), value, table)
    parts = [m.gains[layer] for layer in range(LAYERS)]
    parts += [m.router_t[layer] for layer in range(LAYERS)]
    parts.append(table)
    count = sum(one.shape[0] for one in parts)
    if count < m.small.shape[0]:
        parts.append(jnp.zeros((m.small.shape[0] - count, own), f32))
    m.small[...] = jnp.concatenate(parts, axis=0).astype(bf16)


def place_small(n, small_all, rows):
    own = small_all.shape[2]
    if own == LANES:
        return [
            jnp.concatenate([small_all[2 * q].astype(f32), small_all[2 * q + 1].astype(f32)], axis=1)
            for q in range(SLICES)
        ]
    out = []
    for q in range(SLICES):
        total = jnp.zeros((rows, HALF), f32)
        for i in range(HALF // own):
            lane = lax.broadcasted_iota(jnp.int32, (own, HALF), 1)
            spot = lax.broadcasted_iota(jnp.int32, (own, HALF), 0)
            hot = (lane == spot + i * own).astype(f32).astype(bf16)
            total = total + nn(small_all[q * (HALF // own) + i], hot)
        out.append(total)
    return out


def first_program(n, cap, experts, heads):
    buckets = BUCKETS // n

    def first_kernel(m):
        d, t, sib, far, opp = places()
        own = D // n
        saves = Saves(m.save_sems)
        loads = start_weight_loads(m, 0)
        reduce = Reduce(m.part, m.reduce)

        def span(i):
            return pl.ds(pl.multiple_of(i * own, 16), own)

        views = [
            (lambda i: m.small_all.at[i], m.small),
            (lambda i: m.wqkv.at[0, span(i)], m.qkv_low.at[0, 0]),
            (lambda i: m.wqkv.at[1, span(i)], m.qkv_low.at[0, 1]),
            (lambda i: m.wqkv.at[2, span(i)], m.qkv_low.at[0, 2]),
            (lambda i: m.wo.at[span(i)], m.out_low.at[0]),
            (lambda i: m.wqkv_next.at[:, span(i)], m.qkv_low.at[1]),
            (lambda i: m.wo_next.at[span(i)], m.out_low.at[1]),
        ]
        pieces = Pieces(n, views, m.piece_send, m.piece_recv)
        set_small(m, heads)
        m.qkv_low[0] = m.qkv[0].astype(bf16)
        greet(n, True)
        pieces.start(0)
        pieces.start(1)
        pieces.start(2)
        m.late_wait()
        m.out_low[0] = m.out[0].astype(bf16)
        m.small_all[d] = m.small[...]
        m.wqkv[:, span(d)] = m.qkv_low[0]
        m.wo[span(d)] = m.out_low[0]
        m.qkv_low[1] = m.qkv[1].astype(bf16)
        m.out_low[1] = m.out[1].astype(bf16)
        saves.start(m.qkv_low.at[1], m.wqkv_next.at[:, span(d)])
        saves.start(m.out_low.at[1], m.wo_next.at[span(d)])
        set_targets(m, 0, cap)
        pieces.forward(0)
        pieces.finish(0)
        rows = m.small.shape[0]
        slices = place_small(n, m.small_all, rows)
        for q in range(SLICES):
            m.wide[q] = slices[q].astype(bf16)
        first = 2 * LAYERS + LAYERS * experts
        table = jnp.zeros((LAYERS * heads, LANES), f32)
        width = m.small_all.shape[2]
        for i in range(n):
            lane = lax.broadcasted_iota(jnp.int32, (width, LANES), 1)
            spot = lax.broadcasted_iota(jnp.int32, (width, LANES), 0)
            hot = ((lane == spot + i * buckets) & (spot < buckets)).astype(f32).astype(bf16)
            table = table + nn(m.small_all[i][first : first + LAYERS * heads], hot)
        m.tab[...] = table
        set_attention_tables(m)
        total = None
        for q in range(SLICES):
            x = m.tok[:, q * HALF : (q + 1) * HALF].astype(f32)
            m.hg[q] = (x * m.wide[q, 0:1].astype(f32)).astype(bf16)
            squares = jnp.sum(x * x, axis=1, keepdims=True)
            total = squares if total is None else total + squares
        m.r1[...] = jnp.broadcast_to(lax.rsqrt(total * (1.0 / D) + eps_norm), (SEQ, LANES))
        saves.start(m.hg, m.hg_out)
        pieces.forward(1)
        pieces.start(3)
        pieces.forward(2)
        pieces.start(4)
        pieces.finish(1)
        for b in range(2):
            project(m, b, 0)
        pieces.forward(3)
        pieces.finish(2)
        for b in range(2):
            project(m, b, 1)
        pieces.forward(4)
        for piece in (5, 6):
            pieces.start(piece)
        pieces.finish(3)
        for b in range(2):
            project(m, b, 2)
        saves.start(m.wqkv, m.wqkv_out)
        for b in range(2):
            attend_block(m, b, 0)
            if b == 0:
                pieces.finish(4)
                saves.start(m.wo, m.wo_out)
            project_out(m, b)
            reduce.start(b)
            reduce.middle(b)
        save_attention(m, saves)
        for b in range(2):
            span_b = block_rows(b)
            m.mid[span_b] = pick_slice(m.tok[span_b].astype(f32)) + reduce.finish(b)

        half = n // 2
        share = max(1, half // 4)

        def pass_on(first):
            def one(k, carry):
                for piece in (5, 6):
                    pieces.forward_one(piece, k)
                return carry

            lax.fori_loop(first, min(first + share, half), one, 0)

        def hook(i):
            for event in range(3):

                @pl.when(i == 2 * event + 1)
                def _(event=event):
                    pass_on(1 + event * share)

        forward_experts(m, n, cap, 0, experts, loads, saves, hook)
        if 1 + 3 * share < half:
            pass_on(1 + 3 * share)
        for piece in (5, 6):
            pieces.finish(piece)
        for piece in range(7):
            pieces.wait_sends(piece)
        reduce.wait_sends()
        saves.wait()

    return first_kernel


def norm_backward(tiny, grad, rows, scale, gain, upstream):
    weighted = grad * gain
    tiny.start(to_row(jnp.sum(weighted * rows, axis=1, keepdims=True)))
    gain_grad = jnp.sum(grad * rows * scale, axis=0, keepdims=True)
    base = upstream + scale * weighted
    mean = to_cols(tiny.total())[:, :1] * (1.0 / D)
    return base - rows * (scale * scale * scale * mean), gain_grad


def backward_outs(n, cap, hidden, experts):
    return [
        named.midg((SEQ, HALF), f32, vmem_spec),
        named.gain_rows((8, HALF), f32, vmem_spec),
        named.router_g((experts, HALF), f32, vmem_spec),
        named.wg_grad((hidden, D), bf16, any_spec),
        named.wu_grad((hidden, D), bf16, any_spec),
        named.wd_grad((hidden, D), bf16, any_spec),
    ]


def backward_ins(state):
    return [
        named.picked(state.picked, late_spec),
        named.gates(state.gates, late_spec),
        named.mid(state.mid, late_spec),
        named.normed(state.normed, late_spec),
        named.r2(state.r2, late_spec),
        named.x_in(state.x_out, any_spec),
        named.inner_in(state.inner_out, any_spec),
        named.act_in(state.act_out, any_spec),
        named.slope_in(state.slope_out, any_spec),
        named.wg_in(state.wg_out, any_spec),
        named.wu_in(state.wu_out, any_spec),
        named.wd_in(state.wd_out, any_spec),
    ]


def backward_scratch(n, cap, hidden, experts):
    chunks, rows = Route.shape(n, cap)
    return [
        named.wg(pltpu.VMEM((hidden, D), bf16)),
        named.wu(pltpu.VMEM((hidden, D), bf16)),
        named.wd(pltpu.VMEM((hidden, D), bf16)),
        named.xs(pltpu.VMEM((chunks, SLICES, rows, HALF), bf16)),
        named.inner(pltpu.VMEM((chunks, rows, hidden), bf16)),
        named.act(pltpu.VMEM((chunks, rows, hidden), bf16)),
        named.slope(pltpu.VMEM((chunks, rows, hidden), bf16)),
        named.gpg(pltpu.VMEM((chunks, rows, hidden), bf16)),
        named.upg(pltpu.VMEM((chunks, rows, hidden), bf16)),
        named.dy(pltpu.VMEM((SEQ, HALF), f32)),
        named.pgs(pltpu.VMEM((2 * SEQ, HALF), bf16)),
        named.hot(pltpu.VMEM((2, SEQ, n * cap), bf16)),
        named.logit_g(pltpu.VMEM((experts, SEQ), f32)),
        named.targ_row(pltpu.VMEM((2, SEQ), jnp.int32)),
        named.targ_col(pltpu.VMEM((SEQ, LANES), jnp.int32)),
        named.load_sems(pltpu.SemaphoreType.DMA((7,))),
        named.save_sems(pltpu.SemaphoreType.DMA((32,))),
        named.tiny_one(Tiny.scratch(8, SEQ)),
        named.tiny_two(Tiny.scratch(8, SEQ)),
        named.route(Route.scratch(n, cap, 1)),
    ]


def start_backward_loads(m):
    pairs = (
        (m.wd_in, m.wd),
        (m.act_in, m.act),
        (m.slope_in, m.slope),
        (m.wg_in, m.wg),
        (m.wu_in, m.wu),
        (m.inner_in, m.inner),
        (m.x_in, m.xs),
    )
    loads = [pltpu.make_async_copy(src, dst, m.load_sems.at[i]) for i, (src, dst) in enumerate(pairs)]
    for copy in loads:
        copy.start()
    return loads


def backward_rows(m, route):
    for k in range(2):
        m.pgs[k * SEQ : (k + 1) * SEQ] = (m.gates[:, k : k + 1] * m.dy[...]).astype(bf16)

    def fill(chunk, place):
        number = chunk * route.rows + lax.broadcasted_iota(jnp.int32, (route.rows, SEQ), 0)
        hits = [(m.targ_row[k : k + 1] == number).astype(f32).astype(bf16) for k in range(2)]
        route.out[place] = nn(jnp.concatenate(hits, axis=1), m.pgs[...]).astype(bf16)

    return fill


def start_shares(m, tiny):
    place = lax.broadcasted_iota(jnp.int32, (8, SEQ), 0)
    shares = [to_row(jnp.sum(m.dy[...] * m.picked[k].astype(f32), axis=1, keepdims=True)) for k in range(2)]
    tiny.start(jnp.where(place == 0, shares[0], shares[1]))


def logit_gradient(m, layer, experts, tiny):
    share_grad = tiny.total()
    gate_rows = jnp.transpose(m.gates[...])[:8]
    product = gate_rows * share_grad
    both = product[0:1] + product[1:2]
    chosen = gate_rows * (share_grad - both)
    expert_no = lax.broadcasted_iota(jnp.int32, (experts, SEQ), 0)
    logit_g = jnp.zeros((experts, SEQ), f32)
    for k in range(2):
        logit_g = logit_g + jnp.where(expert_no == m.routes_row[layer, k : k + 1], chosen[k : k + 1], 0.0)
    m.logit_g[...] = logit_g
    m.router_g[...] = nn(logit_g.astype(bf16), m.normed[...])


def backward_products(m, chunk, rows):
    inner_grad = nt(rows, m.wd[...])
    up_low = (inner_grad * m.act[chunk].astype(f32)).astype(bf16)
    gate_low = (inner_grad * m.slope[chunk].astype(f32)).astype(bf16)
    m.upg[chunk] = up_low
    m.gpg[chunk] = gate_low
    return nn(gate_low, m.wg[...]) + nn(up_low, m.wu[...])


class Products:
    def __init__(self, m, route, first, inputs_of, saves):
        self.m, self.route, self.first, self.inputs_of, self.saves = m, route, first, inputs_of, saves

    def one(self, left_ref, right_of, stage, out):
        count = self.route.chunks * self.route.rows
        hidden = stage.shape[0]
        right = jnp.concatenate([right_of(q) for q in range(SLICES)], axis=1)
        for start in range(0, hidden, HALF):
            size = min(HALF, hidden - start)
            left = left_ref[:, :, start : start + size].reshape(count, size)
            stage[start : start + size] = tn(left, right).astype(bf16)
            self.saves.start(stage, out, slice(start, start + size))

    def step(self):
        return self.route.total + STAGE_LAGS[2] - 1

    def in_loop(self, i):
        @pl.when(i == self.step())
        def _():
            self.one(self.m.gpg, self.inputs_of, self.m.wg, self.m.wg_grad)

    def after(self):
        self.one(self.m.upg, self.inputs_of, self.m.wu, self.m.wu_grad)
        self.one(self.m.inner, lambda q: self.route.arrived(self.first, q), self.m.wd, self.m.wd_grad)


def backward_tail(m, layer, experts, tiny, route, first, gain_one):
    route.wait_back(first)
    grad = tn(m.logit_g[...].astype(bf16), router_of(m, layer, experts))
    for k in range(2):
        grad = grad + nn(m.hot[k], route.returned(first))
    value, gain_two = norm_backward(tiny, grad, m.mid[...], m.r2[:, :1], gain_of(m, layer, 1), m.dy[...])
    m.midg[...] = value
    gain_place = lax.broadcasted_iota(jnp.int32, (8, HALF), 0)
    m.gain_rows[...] = jnp.where(gain_place == 0, gain_two, jnp.where(gain_place == 1, gain_one, 0.0))
    route.wait_sends()


def backward_experts(m, n, cap, layer, experts, loads, saves, gain_one, hook, hook_end):
    tiny_one = Tiny(m.tiny_one)
    tiny_two = Tiny(m.tiny_two)
    route = Route(n, cap, 1, m.route)
    fill_one = backward_rows(m, route)

    def fill(chunk):
        fill_one(chunk, chunk)

    route.begin(fill, fill)
    start_shares(m, tiny_one)
    for copy in loads[:5]:
        copy.wait()
    logit_gradient(m, layer, experts, tiny_one)

    def compute(chunk, rows):
        route.put(chunk, backward_products(m, chunk, rows))

    def hook_all(i):
        @pl.when(i == 1)
        def _():
            set_hot(m, n * cap)

        hook(i)
        products.in_loop(i)

    count = route.chunks * route.rows
    products = Products(m, route, 0, lambda q: m.xs[:, q].reshape(count, HALF), saves)
    for copy in loads[5:]:
        copy.wait()
    route.run(compute, hook_all)
    products.after()
    hook_end()
    backward_tail(m, layer, experts, tiny_two, route, 0, gain_one)


def top_program(n, cap, experts, heads, layer):
    def top_kernel(m):
        saves = Saves(m.save_sems)
        weight_copies = [
            pltpu.make_async_copy(m.wqkv_in, m.wqkv, m.weight_sems.at[0]),
            pltpu.make_async_copy(m.wo_in, m.wo, m.weight_sems.at[1]),
        ]
        expert_weights = [
            pltpu.make_async_copy(src.at[layer, 0], m.stage, m.load_sems.at[i])
            for i, src in enumerate((m.gate_f, m.up_f, m.down_f))
        ]
        expert_weights[0].start()
        for copy in weight_copies:
            copy.start()
        reduce = Reduce(m.part, m.reduce)
        gather = Gather(m.hg, m.gather)
        tiny = Tiny(m.tiny_zero)
        greet(n, True)
        gain = gain_of(m, layer, 0)
        for b in range(2):
            gather.start(b, (m.h[block_rows(b)] * gain).astype(bf16))
        tiny.start(to_row(jnp.sum(m.h[...] * m.h[...], axis=1, keepdims=True)))
        set_attention_tables(m)
        set_targets(m, layer, cap)
        m.r1[...] = to_cols(lax.rsqrt(tiny.total() * (1.0 / D) + eps_norm))
        m.late_wait()
        m.dy[...] = pick_slice(m.cot[...].astype(f32))
        lows = (m.wg, m.wu, m.wd)
        expert_weights[0].wait()
        narrow_weights(m.stage, lows[0])
        expert_weights[1].start()
        for copy in weight_copies:
            copy.wait()
        gather.forward(0)
        gather.finish(0)
        gather.forward(1)
        attention_block(m, 0, layer * heads, lambda: None)
        reduce.start(0)
        gather.finish(1)
        attention_block(m, 1, layer * heads, lambda: reduce.middle(0))
        reduce.start(1)
        saves.start(m.hg, m.hg_out)
        save_attention(m, saves)
        reduce.middle(1)
        expert_weights[1].wait()
        narrow_weights(m.stage, lows[1])
        expert_weights[2].start()
        for b in range(2):
            span_b = block_rows(b)
            m.mid[span_b] = m.h[span_b] + reduce.finish(b)
        tiny_one = Tiny(m.tiny_one)
        tiny_two = Tiny(m.tiny_two)
        tiny_three = Tiny(m.tiny_three)
        tiny_four = Tiny(m.tiny_four)
        route = Route(n, cap, 2, m.route)
        chunks = route.chunks
        fill_forward = forward_rows(m, layer, experts, tiny_one, tiny_two, route)

        def fill(chunk):
            @pl.when(chunk < chunks)
            def _():
                fill_forward(chunk)

            @pl.when(chunk >= chunks)
            def _():
                fill_backward(chunk - chunks, chunk)

        route.begin(fill_forward, fill)
        tiny_two.start(nt(router_of(m, layer, experts), m.normed[...]))
        expert_weights[2].wait()
        narrow_weights(m.stage, lows[2])
        router_gates(m, layer, tiny_two)
        fill_backward = backward_rows(m, route)

        def compute(chunk, rows):
            @pl.when(chunk < chunks)
            def _():
                route.put(chunk, forward_products(m, chunk, rows))

            @pl.when(chunk >= chunks)
            def _():
                route.put(chunk, backward_products(m, chunk - chunks, rows))

        def hook(i):
            @pl.when(i == 2)
            def _():
                set_hot(m, n * cap)

            @pl.when(i == chunks + STAGE_LAGS[3] + 1)
            def _():
                forward_combine(m, route)
                saves.start(m.y, m.outs.y)
                start_shares(m, tiny_three)

            products.in_loop(i)

        products = Products(m, route, chunks, lambda q: route.arrived(0, q), saves)
        route.run(compute, hook)
        logit_gradient(m, layer, experts, tiny_three)
        products.after()
        backward_tail(m, layer, experts, tiny_four, route, chunks, jnp.zeros((1, HALF), f32))
        gather.wait_sends()
        reduce.wait_sends()
        saves.wait()

    return top_kernel


def attention_back_ins(kept, midg):
    return [
        named.midg_in(midg, vmem_spec),
        named.a_ctx(kept.ctx, late_spec),
        named.a_proj(kept.proj, late_spec),
        named.a_lse(kept.lse, late_spec),
        named.a_r1(kept.r1, late_spec),
        named.a_hg(kept.hg, late_spec),
        named.a_wqkv(kept.wqkv, late_spec),
        named.a_wo(kept.wo, late_spec),
        named.a_h(kept.h, late_spec),
    ]


def attention_back_scratch(width, heads):
    return attention_scratch + [
        named.pg(pltpu.VMEM((SEQ, 3 * width), bf16)),
        named.dk(pltpu.VMEM((SEQ, width), f32)),
        named.dv(pltpu.VMEM((SEQ, width), f32)),
        named.bias_grad(pltpu.VMEM((heads, HALF, 2 * HALF), f32)),
        named.probs(pltpu.VMEM((heads, HALF, 3 * HALF), f32)),
        named.ag(pltpu.VMEM((SLICES, SEQ, HALF), bf16)),
        named.gather(Gather.scratch),
        named.tiny_zero(Tiny.scratch(8, SEQ)),
    ]


def attention_view(m):
    return types.SimpleNamespace(
        seg_col=m.seg_col,
        seg_row=m.seg_row,
        bias=m.bias,
        part=m.part,
        ctx=m.a_ctx,
        proj=m.a_proj,
        lse=m.a_lse,
        r1=m.a_r1,
        hg=m.a_hg,
        wqkv=m.a_wqkv,
        wo=m.a_wo,
        pg=m.pg,
        dk=m.dk,
        dv=m.dv,
        bias_grad=m.bias_grad,
        probs=m.probs,
        ag=m.ag,
        wog=m.wog,
        qkvg=m.qkvg,
    )


def attention_back(m, layer, heads, after_gather, after_out, after_qkv, out_first=False):
    gather = Gather(m.ag, m.gather)
    reduce = Reduce(m.part, m.reduce)
    tiny = Tiny(m.tiny_zero)
    a = attention_view(m)
    for b in (1, 0):
        gather.start(b, m.midg_in[block_rows(b)].astype(bf16))
    set_attention_tables(m)
    m.late_wait()
    attention_probs(a, 1, layer * heads)
    gather.forward(1)
    attention_probs(a, 0, layer * heads)
    gather.forward(0)
    gather.finish(1)
    late_dots = attention_back_block(a, 1, lambda: None)
    reduce.start(1)
    gather.finish(0)
    after_gather()
    if out_first:
        out_gradient(a)
        after_out()
    early_dots = attention_back_block(a, 0, lambda: reduce.middle(1))
    reduce.start(0)
    tiny.start(to_row(jnp.concatenate([early_dots, late_dots], axis=0)))
    if not out_first:
        out_gradient(a)
        after_out()
    reduce.middle(0)
    qkv_gradient(a)
    after_qkv()
    m.table[...] = table_gradient(a)
    grad = jnp.concatenate([reduce.finish(0), reduce.finish(1)], axis=0)
    h = m.a_h[...] if m.a_h.shape[1] == HALF else pick_slice(m.a_h[...].astype(f32))
    scale = m.a_r1[:, :1]
    gain_grad = jnp.sum(grad * h * scale, axis=0, keepdims=True)
    base = m.midg_in[...] + scale * (grad * gain_of(m, layer, 0))
    mean = to_cols(tiny.total())[:, :1] * (1.0 / D)
    gather.wait_sends()
    reduce.wait_sends()
    return base - h * (scale * scale * scale * mean), gain_grad


def back_program(n, cap, experts, heads, layer):
    def back_next_kernel(m):
        saves = Saves(m.save_sems)
        loads = start_backward_loads(m)
        greet(n, True)
        set_targets(m, layer, cap)
        own = D // n

        def rows_of(e):
            return pl.ds(pl.multiple_of(e * own, 16), own)

        late_qkv = Scatter(n, lambda e: m.qkvg.at[:, rows_of(e)], m.qkv_sums, m.near_a, None, None)
        late_out = Scatter(n, lambda e: m.wog.at[rows_of(e)], m.out_sums, m.near_b, m.out_late, m.far_b)
        half = n // 2
        share = max(1, half // 4)
        value, gain_one = attention_back(
            m,
            layer + 1,
            heads,
            lambda: None,
            lambda: late_out.near_start(1, half + 1),
            lambda: late_qkv.near_start(1, 1 + share),
        )
        m.dy[...] = value

        def hook(i):
            for event in range(1, half // share):

                @pl.when(i == 2 * event - 1)
                def _(event=event):
                    late_qkv.near_start(1 + event * share, 1 + (event + 1) * share)

                @pl.when(i == 2 * event)
                def _(event=event):
                    late_qkv.loop(1 + (event - 1) * share, 1 + event * share, late_qkv.near_sum)

            @pl.when(i == 3)
            def _():
                late_out.near_sums()
                late_out.far_start()

        def hook_end():
            late_qkv.loop(1 + half - share, 1 + half, late_qkv.near_sum)
            saves.start(m.qkv_sums, m.outs.qkv_sums)

        backward_experts(m, n, cap, layer, experts, loads, saves, gain_one, hook, hook_end)
        late_out.finish()
        late_out.near_wait_sends()
        late_qkv.near_wait_sends()
        saves.wait()

    return back_next_kernel


class Scatter:
    @staticmethod
    def near_scratch(n, block):
        return [
            pltpu.VMEM((n // 2,) + block, bf16),
            pltpu.SemaphoreType.DMA((n // 2,)),
            pltpu.SemaphoreType.DMA((n // 2,)),
        ]

    @staticmethod
    def far_scratch(n, block):
        return [
            pltpu.VMEM((n // 2,) + block, bf16),
            pltpu.SemaphoreType.DMA((n // 2,)),
            pltpu.SemaphoreType.DMA((n // 2,)),
        ]

    def __init__(self, n, block_of, sums, near_refs, out, far_refs):
        self.n, self.block_of, self.sums, self.out = n, block_of, sums, out
        if near_refs is not None:
            self.near, self.near_send, self.near_recv = near_refs
        if far_refs is not None:
            self.got, self.far_send, self.far_recv = far_refs

    def near_copy(self, k):
        d, t, sib, far, opp = places()
        parity = lax.rem(d, 2)
        src = self.block_of(2 * k + 1 - parity)
        return remote(src, self.near.at[k], self.near_send.at[k], self.near_recv.at[k], (d + 1 - 2 * parity, t))

    def far_copy(self, k, source):
        d, t, sib, far, opp = places()
        return remote(
            self.sums.at[k], self.got.at[source], self.far_send.at[k], self.far_recv.at[source], (2 * k + lax.rem(d, 2), t)
        )

    def spot(self, j):
        d = lax.axis_index("dp")
        return lax.rem(d // 2 + j, self.n // 2)

    def loop(self, first, last, action):
        def one(j, carry):
            action(self.spot(j))
            return carry

        lax.fori_loop(first, last, one, 0)

    def near_start(self, first, last):
        self.loop(first, last, lambda k: self.near_copy(k).start())

    def near_sum(self, k):
        d = lax.axis_index("dp")
        self.near_copy(k).wait_recv()
        mine = self.block_of(2 * k + lax.rem(d, 2))[...].astype(f32)
        self.sums[k] = (mine + self.near[k].astype(f32)).astype(bf16)

    def near_sums(self):
        self.loop(1, self.n // 2 + 1, self.near_sum)

    def near_wait_sends(self):
        self.loop(0, self.n // 2, lambda k: self.near_copy(k).wait_send())

    def far_start(self):
        d = lax.axis_index("dp")
        self.loop(1, self.n // 2, lambda k: self.far_copy(k, d // 2).start())

    def both(self, ahead):
        d = lax.axis_index("dp")
        total = self.n // 2

        def one(j, carry):
            k = self.spot(j)

            @pl.when(j + ahead <= total)
            def _():
                self.near_copy(self.spot(j + ahead)).start()

            self.near_sum(k)

            @pl.when(k != d // 2)
            def _():
                self.far_copy(k, d // 2).start()

            return carry

        lax.fori_loop(1, total + 1, one, 0)

    def finish(self):
        d = lax.axis_index("dp")
        total = self.sums[d // 2].astype(f32)

        def one(j, carry):
            k = self.spot(j)
            self.far_copy(k, k).wait_recv()
            return carry + self.got[k].astype(f32)

        self.out[...] = lax.fori_loop(1, self.n // 2, one, total)
        self.loop(1, self.n // 2, lambda k: self.far_copy(k, d // 2).wait_send())


def final_program(n, experts, heads):
    own = D // n

    def final_kernel(m):
        d, t, sib, far, opp = places()
        saves = Saves(m.save_sems)

        def rows_of(e):
            return pl.ds(pl.multiple_of(e * own, 16), own)

        late_qkv = Scatter(n, None, m.qkv_sums_next, None, m.qkv_grad.at[1], m.far_a)
        early_qkv = Scatter(n, lambda e: m.qkvg.at[:, rows_of(e)], m.qkv_sums, m.near_c, m.qkv_grad.at[0], m.far_c)
        early_out = Scatter(n, lambda e: m.wog.at[rows_of(e)], m.out_sums, m.near_d, m.out_grad.at[0], m.far_d)
        half = n // 2
        output = Gather(m.output_buf, m.output_gather)
        dx_all = Gather(m.dx_buf, m.dx_gather)
        greet(n, True)
        late_qkv.far_start()
        m.out_grad[1] = m.out_late[...]

        def after_out():
            early_out.near_start(1, half + 1)

        def after_qkv():
            early_qkv.near_start(1, half + 1)
            early_out.both(half)

        def after_gather():
            for b in range(2):
                output.start(b, m.y_last[block_rows(b)].astype(bf16))

        dx, gain_one = attention_back(m, 0, heads, after_gather, after_out, after_qkv, True)
        for b in range(2):
            dx_all.start(b, dx[block_rows(b)].astype(bf16))
        place = lax.broadcasted_iota(jnp.int32, (8, HALF), 0)
        m.pack[0:8] = jnp.where(
            place == 0,
            gain_one,
            jnp.where(
                place == 1,
                m.gain_rows_0[0:1],
                jnp.where(place == 2, m.gain_rows_0[1:2], jnp.where(place == 3, m.gain_rows_1[0:1], 0.0)),
            ),
        )
        m.pack[8:16] = jnp.concatenate([m.table[...], m.table_next[...]], axis=1)
        m.pack[16 : 16 + experts] = m.router_g_0[...]
        m.pack[16 + experts : 16 + 2 * experts] = m.router_g_1[...]

        def pack_copy(j, source, target):
            return remote(m.pack, m.packs.at[source], m.pack_send.at[j], m.pack_recv.at[source], (target, t))

        def spread(j, carry):
            pack_copy(j, d, lax.rem(d + j, n)).start()
            return carry

        lax.fori_loop(1, n, spread, 0)
        early_qkv.both(half)
        for b in range(2):
            output.forward(b)
        for b in range(2):
            dx_all.forward(b)
        m.packs[d] = m.pack[...]

        def collect(j, carry):
            source = lax.rem(d + j, n)
            pack_copy(j, source, source).wait_recv()
            return carry

        lax.fori_loop(1, n, collect, 0)

        def add(i, carry):
            return carry + m.packs[i]

        m.small_out[t] = lax.fori_loop(1, n, add, m.packs[0])

        def all_copies():
            return [
                remote(m.small_out.at[t], m.small_out.at[t], m.all_send.at[i], m.all_recv.at[i], (d, peer))
                for i, peer in enumerate((sib, far, opp))
            ]

        for copy in all_copies():
            copy.start()
        for gather, out in ((output, m.output), (dx_all, m.dx_full)):
            for b in range(2):
                gather.finish(b)
            for q in range(SLICES):
                saves.start(gather.buf.at[q], out.at[:, pl.ds(q * HALF, HALF)])
        for one in (late_qkv, early_out, early_qkv):
            one.finish()
        early_out.near_wait_sends()
        early_qkv.near_wait_sends()

        def sent(j, carry):
            pack_copy(j, d, lax.rem(d + j, n)).wait_send()
            return carry

        lax.fori_loop(1, n, sent, 0)
        for copy in all_copies():
            copy.wait()
        output.wait_sends()
        dx_all.wait_sends()
        saves.wait()

    return final_kernel


def widen_kernel(*refs):
    ins, outs = refs[: 3 * LAYERS + 4], refs[3 * LAYERS + 4 :]
    for i in range(3):
        for layer in range(LAYERS):
            outs[i][layer, 0] = ins[3 * layer + i][...].astype(f32)
    for i in range(4):
        outs[3 + i][...] = ins[3 * LAYERS + i][...].astype(outs[3 + i].dtype)


def widen(grads, others):
    hidden = grads[0][0].shape[0]
    steps = 4
    tile = hidden // steps
    specs = []
    shapes = []
    for one in others:
        dim = one.ndim - 2
        count = min(steps, one.shape[dim] // 8)
        block = one.shape[:dim] + (one.shape[dim] // count,) + one.shape[dim + 1 :]
        specs.append(
            pl.BlockSpec(block, lambda i, dim=dim, count=count: (0,) * dim + (jnp.minimum(i, count - 1), 0))
        )
        shapes.append(one.shape)
    return pl.pallas_call(
        widen_kernel,
        grid=(steps,),
        out_shape=[shaped((LAYERS, 1, hidden, D), f32)] * 3
        + [shaped(shapes[0], bf16)]
        + [shaped(shape, f32) for shape in shapes[1:]],
        in_specs=[pl.BlockSpec((tile, D), lambda i: (i, 0))] * (3 * LAYERS) + specs,
        out_specs=[pl.BlockSpec((LAYERS, 1, tile, D), lambda i: (0, 0, i, 0))] * 3 + specs,
        compiler_params=pltpu.CompilerParams(vmem_limit_bytes=vmem_bytes),
    )(*[one for layer in grads for one in layer], *others)


def local(tokens, cotangent, w_qkv, w_out, router, gains, rel_table, w_gate, w_up, w_down, routes, slots, segments):
    n = lax.axis_size("dp")
    own = D // n
    experts = router.shape[2]
    heads = rel_table.shape[2]
    width = w_qkv.shape[3]
    hidden = w_down.shape[2]
    cap = 3 * SEQ // n
    rows = 2 * LAYERS + LAYERS * experts + LAYERS * heads
    rows = rows + -rows % 16
    gate_t = w_gate.transpose(0, 1, 3, 2)
    up_t = w_up.transpose(0, 1, 3, 2)
    routes_row = routes.transpose(0, 2, 1)
    slots_row = slots.transpose(0, 2, 1)
    seg_row = segments.reshape(1, SEQ)
    index_ins = [
        named.routes_row(routes_row, vmem_spec),
        named.slots_row(slots_row, vmem_spec),
        named.seg_row(seg_row, vmem_spec),
    ]
    weight_ins = [named.gate_f(gate_t, any_spec), named.up_f(up_t, any_spec), named.down_f(w_down, any_spec)]
    attention_weights = [
        named.wqkv(pltpu.VMEM((3, D, width), bf16)),
        named.wo(pltpu.VMEM((D, width), bf16)),
        named.hg(pltpu.VMEM((SLICES, SEQ, HALF), bf16)),
    ]
    pieces = 5 + 2 * (LAYERS - 1)
    first = call(
        first_program(n, cap, experts, heads),
        [named.tok(tokens, late_spec), named.qkv(w_qkv, vmem_spec), named.out(w_out, late_spec), named.gains(gains, vmem_spec)]
        + [named.router_t(router.transpose(0, 2, 1), vmem_spec), named.table(rel_table, vmem_spec)]
        + index_ins
        + weight_ins,
        [
            named.wide((SLICES, rows, HALF), bf16, vmem_spec),
            named.tab((8, LANES), f32, vmem_spec),
            named.wqkv_out((3, D, width), bf16, any_spec),
            named.wo_out((D, width), bf16, any_spec),
            named.wqkv_next((3, D, width), bf16, any_spec),
            named.wo_next((D, width), bf16, any_spec),
            named.hg_out((SLICES, SEQ, HALF), bf16, any_spec),
        ]
        + attention_outs(width)
        + forward_outs(n, cap, hidden),
        attention_weights
        + attention_scratch
        + [
            named.small(pltpu.VMEM((rows, own), bf16)),
            named.small_all(pltpu.VMEM((n, rows, own), bf16)),
            named.qkv_low(pltpu.VMEM((LAYERS, 3, own, width), bf16)),
            named.out_low(pltpu.VMEM((LAYERS, own, width), bf16)),
            named.piece_send(pltpu.SemaphoreType.DMA((pieces, 2, n // 2))),
            named.piece_recv(pltpu.SemaphoreType.DMA((pieces, 2, n // 2))),
        ]
        + forward_scratch(n, cap, hidden, experts),
        0,
    )
    wide_ins = [named.wide(first.wide, vmem_spec), named.tab(first.tab, vmem_spec)]
    chunks, route_rows = Route.shape(n, cap)
    chunk_rows = pltpu.VMEM((chunks, route_rows, hidden), bf16)
    top = call(
        top_program(n, cap, experts, heads, 1),
        [
            named.h(first.y, vmem_spec),
            named.cot(cotangent, late_spec),
            named.wqkv_in(first.wqkv_next, any_spec),
            named.wo_in(first.wo_next, any_spec),
        ]
        + wide_ins
        + index_ins
        + weight_ins,
        [named.hg_out((SLICES, SEQ, HALF), bf16, any_spec), named.y((SEQ, HALF), f32, saved_spec)]
        + attention_outs(width)
        + backward_outs(n, cap, hidden, experts),
        attention_weights
        + attention_scratch
        + [
            named.gather(Gather.scratch),
            named.tiny_zero(Tiny.scratch(8, SEQ)),
            named.tiny_one(Tiny.scratch(8, SEQ)),
            named.tiny_two(Tiny.scratch(experts, SEQ)),
            named.tiny_three(Tiny.scratch(8, SEQ)),
            named.tiny_four(Tiny.scratch(8, SEQ)),
            named.weight_sems(pltpu.SemaphoreType.DMA((2,))),
            named.load_sems(pltpu.SemaphoreType.DMA((3,))),
            named.save_sems(pltpu.SemaphoreType.DMA((32,))),
            named.stage(pltpu.VMEM((hidden, D), f32)),
            named.wg(pltpu.VMEM((hidden, D), bf16)),
            named.wu(pltpu.VMEM((hidden, D), bf16)),
            named.wd(pltpu.VMEM((hidden, D), bf16)),
            named.inner(chunk_rows),
            named.act(chunk_rows),
            named.slope(chunk_rows),
            named.gpg(chunk_rows),
            named.upg(chunk_rows),
            named.mid(pltpu.VMEM((SEQ, HALF), f32)),
            named.normed(pltpu.VMEM((SEQ, HALF), bf16)),
            named.r2(pltpu.VMEM((SEQ, LANES), f32)),
            named.gates(pltpu.VMEM((SEQ, LANES), f32)),
            named.picked(pltpu.VMEM((2, SEQ, HALF), bf16)),
            named.dy(pltpu.VMEM((SEQ, HALF), f32)),
            named.pgs(pltpu.VMEM((2 * SEQ, HALF), bf16)),
            named.hot(pltpu.VMEM((2, SEQ, n * cap), bf16)),
            named.logit_g(pltpu.VMEM((experts, SEQ), f32)),
            named.targ_row(pltpu.VMEM((2, SEQ), jnp.int32)),
            named.targ_col(pltpu.VMEM((SEQ, LANES), jnp.int32)),
            named.route(Route.scratch(n, cap, 2)),
        ],
        1,
    )

    def kept_of(state, wqkv, wo, h):
        return types.SimpleNamespace(
            ctx=state.ctx, proj=state.proj, lse=state.lse, r1=state.r1, hg=state.hg_out, wqkv=wqkv, wo=wo, h=h
        )

    gradient_scratch = [named.wog(pltpu.VMEM((D, width), bf16)), named.qkvg(pltpu.VMEM((3, D, width), bf16))]
    fourth = call(
        back_program(n, cap, experts, heads, 0),
        wide_ins
        + index_ins
        + attention_back_ins(kept_of(top, first.wqkv_next, first.wo_next, first.y), top.midg)
        + backward_ins(first),
        backward_outs(n, cap, hidden, experts)
        + [
            named.qkv_sums((n // 2, 3, own, width), bf16, saved_spec),
            named.out_late((own, width), f32, vmem_spec),
            named.table((8, LANES), f32, vmem_spec),
        ],
        gradient_scratch
        + [
            named.near_a(Scatter.near_scratch(n, (3, own, width))),
            named.near_b(Scatter.near_scratch(n, (own, width))),
            named.far_b(Scatter.far_scratch(n, (own, width))),
            named.out_sums(pltpu.VMEM((n // 2, own, width), bf16)),
        ]
        + attention_back_scratch(width, heads)
        + backward_scratch(n, cap, hidden, experts),
        3,
    )
    pack_rows = 16 + LAYERS * experts
    big, less = (3, own, width), (own, width)
    scatter_scratch = [
        named.far_a(Scatter.far_scratch(n, big)),
        named.near_c(Scatter.near_scratch(n, big)),
        named.near_d(Scatter.near_scratch(n, less)),
        named.far_c(Scatter.far_scratch(n, big)),
        named.far_d(Scatter.far_scratch(n, less)),
        named.qkv_sums(pltpu.VMEM((n // 2,) + big, bf16)),
        named.out_sums(pltpu.VMEM((n // 2,) + less, bf16)),
    ]
    final = call(
        final_program(n, experts, heads),
        wide_ins
        + index_ins[2:]
        + attention_back_ins(kept_of(first, first.wqkv_out, first.wo_out, tokens), fourth.midg)
        + [
            named.qkv_sums_next(fourth.qkv_sums, vmem_spec),
            named.out_late(fourth.out_late, vmem_spec),
            named.y_last(top.y, late_spec),
            named.gain_rows_0(fourth.gain_rows, vmem_spec),
            named.gain_rows_1(top.gain_rows, vmem_spec),
            named.router_g_0(fourth.router_g, vmem_spec),
            named.router_g_1(top.router_g, vmem_spec),
            named.table_next(fourth.table, vmem_spec),
        ],
        [
            named.output((SEQ, D), bf16, any_spec),
            named.dx_full((SEQ, D), bf16, any_spec),
            named.qkv_grad((LAYERS, 3, own, width), f32, vmem_spec),
            named.out_grad((LAYERS, own, width), f32, vmem_spec),
            named.small_out((SLICES, pack_rows, HALF), f32, vmem_spec),
        ],
        gradient_scratch
        + attention_back_scratch(width, heads)
        + scatter_scratch
        + [
            named.table(pltpu.VMEM((8, LANES), f32)),
            named.output_buf(pltpu.VMEM((SLICES, SEQ, HALF), bf16)),
            named.output_gather(Gather.scratch),
            named.dx_buf(pltpu.VMEM((SLICES, SEQ, HALF), bf16)),
            named.dx_gather(Gather.scratch),
            named.pack(pltpu.VMEM((pack_rows, HALF), f32)),
            named.packs(pltpu.VMEM((n, pack_rows, HALF), f32)),
            named.pack_send(pltpu.SemaphoreType.DMA((n,))),
            named.pack_recv(pltpu.SemaphoreType.DMA((n,))),
            named.all_send(pltpu.SemaphoreType.DMA((3,))),
            named.all_recv(pltpu.SemaphoreType.DMA((3,))),
            named.save_sems(pltpu.SemaphoreType.DMA((32,))),
        ],
        4,
    )
    grads = [[one.wg_grad, one.wu_grad, one.wd_grad] for one in (fourth, top)]
    gate_g, up_g, down_g, output, dx_wide, qkv_grad, out_grad = widen(
        grads, [final.output, final.dx_full, final.qkv_grad, final.out_grad]
    )
    d, t = lax.axis_index("dp"), lax.axis_index("tensor")
    small_sum = final.small_out

    def rows_wide(start, count):
        wide = small_sum[:, start : start + count].transpose(1, 0, 2).reshape(count, D)
        return lax.dynamic_slice_in_dim(wide, d * own, own, 1)

    gains_grad = rows_wide(0, 2 * LAYERS).reshape(LAYERS, 2, own)
    router_grad = rows_wide(16, LAYERS * experts).reshape(LAYERS, experts, own).transpose(0, 2, 1)
    table_all = lax.dynamic_slice_in_dim(small_sum, t, 1, 0)[0, 8 : 8 + heads].reshape(heads, LAYERS, LANES)
    table_grad = lax.dynamic_slice_in_dim(table_all, d * (BUCKETS // n), BUCKETS // n, 2).transpose(1, 2, 0)
    return (
        output,
        dx_wide,
        qkv_grad,
        out_grad,
        router_grad,
        gains_grad,
        table_grad,
        gate_g.transpose(0, 1, 3, 2),
        up_g.transpose(0, 1, 3, 2),
        down_g,
    )


def solution(mesh):
    placed = (
        P("dp", None),
        P("dp", None),
        P(None, None, "dp", "tensor"),
        P(None, "dp", "tensor"),
        P(None, "dp", None),
        P(None, None, "dp"),
        P(None, "dp", "tensor"),
        P(None, "dp", None, "tensor"),
        P(None, "dp", None, "tensor"),
        P(None, "dp", "tensor", None),
        P(None, "dp", None),
        P(None, "dp", None),
        P("dp"),
    )
    return jax.shard_map(
        local,
        mesh=mesh,
        in_specs=placed,
        out_specs=(P("dp", None), P("dp", None)) + placed[2:10],
        check_vma=False,
    )
```
